32 devices in a mesh: dp: 8 (over z, y), tensor: 4 (over x, core).
Axes of the slice: x: 2, y: 2, z: 4, core: 2. Of those that a mesh axis runs over, the one named last changes fastest.
Arguments:
- inputs: bfloat16 [4096, 1280], P(('dp', 'tensor')), may hold values from -6 to 6
- weight_query: bfloat16 [1280, 1280], P('dp', 'tensor'), may hold values from -0.15625 to 0.15625
- weight_key: bfloat16 [1280, 1280], P('dp', 'tensor'), may hold values from -0.15625 to 0.15625
- weight_value: bfloat16 [1280, 1280], P('dp', 'tensor'), may hold values from -0.15625 to 0.15625
- weight_output: bfloat16 [1280, 1280], P('tensor', 'dp'), may hold values from -2 to 2
- weight_hidden: bfloat16 [1280, 1280], P('dp', 'tensor'), may hold values from -0.15625 to 0.15625
- weight_down: bfloat16 [1280, 1280], P('tensor', 'dp'), may hold values from -0.15625 to 0.15625
- bias_query: float32 [1280], replicated, may hold values from -6 to 6
- bias_value: float32 [1280], replicated, may hold values from -0.75 to 0.75
- bias_hidden: float32 [1280], replicated, may hold values from -6 to 6
- bias_output: float32 [1280], replicated, may hold values from -4 to 4
- bias_final: float32 [1280], replicated, may hold values from -4 to 4
- gain_attention: float32 [1280], replicated, may hold values from 0.25 to 1.75
- gain_mixer: float32 [1280], replicated, may hold values from 0.25 to 1.75
- query_scale: float32 [80], replicated, may hold values from 0 to 1.5
- lengths: int32 [8], P('dp'), may hold values from 128 to 512, as said below
- cotangent: bfloat16 [4096, 1280], P(('dp', 'tensor')), may hold values from -6 to 6
Outputs:
- output: bfloat16 [4096, 1280], P(('dp', 'tensor'))
- grad_inputs: bfloat16 [4096, 1280], P(('dp', 'tensor'))
- grad_weight_query: float32 [1280, 1280], P('dp', 'tensor')
- grad_weight_key: float32 [1280, 1280], P('dp', 'tensor')
- grad_weight_value: float32 [1280, 1280], P('dp', 'tensor')
- grad_weight_output: float32 [1280, 1280], P('tensor', 'dp')
- grad_weight_hidden: float32 [1280, 1280], P('dp', 'tensor')
- grad_weight_down: float32 [1280, 1280], P('tensor', 'dp')
- grad_bias_query: float32 [1280], replicated
- grad_bias_value: float32 [1280], replicated
- grad_bias_hidden: float32 [1280], replicated
- grad_bias_output: float32 [1280], replicated
- grad_bias_final: float32 [1280], replicated
- grad_gain_attention: float32 [1280], replicated
- grad_gain_mixer: float32 [1280], replicated
- grad_query_scale: float32 [80], replicated
The draws below stay inside these ranges and needn't reach their ends.
Inputs may be any that keep to these rules, and one draw needn't show every extreme that they name: `lengths`: each series slot holds at least 128 live positions, then padding; in every draw some slot is live throughout.
All inputs are finite; a program needn't handle non-finite values.
Results may differ from the reference program's by a relative error of at most 0.017.
Values may be sent and summed in bfloat16 or wider, within the bound.
No kernel may reach another device: no remote copies, remote signals or barrier semaphores. Data moves between devices by JAX's collectives and lax.ppermute only.
A program may use at most 128 MiB of HBM per device.

```python
import jax
import jax.numpy as jnp
from jax import lax

D = 1280
HEADS = 16
HD = 80
FF = 1280
SLOT = 512
SERIES = 8
TOKENS = 4096


def draw_lengths(key, part):
    first, second = jax.random.split(key)
    drawn = jax.random.randint(first, (SERIES,), SLOT // 4, SLOT + 1)
    chosen = jax.random.randint(second, (), 0, SERIES)
    return drawn.at[chosen].set(SLOT).astype(jnp.int32)


def steps_of(own_key, dims, cuts, smallest, high):
    def one(position, parts):
        heights = jax.random.uniform(jax.random.fold_in(jax.random.fold_in(own_key, 6), position), (parts,), jnp.float32, smallest / len(cuts), high / len(cuts))
        return jnp.repeat(jnp.exp(heights), dims[position] // parts).reshape((-1,) + (1,) * (len(dims) - position - 1))

    level = one(*cuts[0])
    for cut in cuts[1:]:
        level = level * one(*cut)
    return level


def scatter_about(key, shape, width, limit, pieces=(), kind=jnp.bfloat16):
    values = width * jax.random.normal(key, shape, jnp.float32)
    if pieces:
        values = values * steps_of(key, shape, pieces, -0.22, 0.18)
    return jnp.clip(values, -limit, limit).astype(kind)


def setup_inputs(seed: int = 0) -> dict:
    key_list = jax.random.split(jax.random.key(seed), 18)
    inputs = scatter_about(key_list[0], (TOKENS, D), 1.0, 6.0, ((0, 32),))
    weight_query = scatter_about(key_list[1], (D, D), D ** -0.5, 0.15625, ((0, 8), (1, 4)))
    weight_key = scatter_about(key_list[2], (D, D), D ** -0.5, 0.15625, ((0, 8), (1, 4)))
    weight_value = scatter_about(key_list[3], (D, D), D ** -0.5, 0.15625, ((0, 8), (1, 4)))
    weight_output = scatter_about(key_list[4], (D, D), (max(D // 128, 2)) ** -0.5, 2.0, ((0, 4), (1, 8)))
    weight_hidden = scatter_about(key_list[5], (D, FF), D ** -0.5, 0.15625, ((0, 8), (1, 4)))
    weight_down = scatter_about(key_list[6], (FF, D), FF ** -0.5, 0.15625, ((0, 4), (1, 8)))
    bias_query = scatter_about(key_list[7], (D,), 0.5, 6.0, (), jnp.float32)
    bias_value = scatter_about(key_list[8], (D,), 0.05, 0.75, (), jnp.float32)
    bias_hidden = scatter_about(key_list[9], (FF,), 0.5, 6.0, (), jnp.float32)
    bias_output = scatter_about(key_list[10], (D,), 0.3, 4.0, (), jnp.float32)
    bias_final = scatter_about(key_list[11], (D,), 0.3, 4.0, (), jnp.float32)
    gain_attention = jnp.clip(1.0 + 0.15 * jax.random.normal(key_list[12], (D,), jnp.float32), 0.25, 1.75)
    gain_mixer = jnp.clip(1.0 + 0.15 * jax.random.normal(key_list[13], (D,), jnp.float32), 0.25, 1.75)
    query_scale = jnp.clip(jax.random.uniform(key_list[14], (HD,), jnp.float32, 0.0, 1.5), 0.0, 1.5)
    lengths = draw_lengths(jax.random.fold_in(key_list[17], 71), 0)
    cotangent = scatter_about(key_list[16], (TOKENS, D), 1.0, 6.0, ((0, 32),))
    return dict(inputs=inputs, weight_query=weight_query, weight_key=weight_key, weight_value=weight_value, weight_output=weight_output, weight_hidden=weight_hidden, weight_down=weight_down, bias_query=bias_query, bias_value=bias_value, bias_hidden=bias_hidden, bias_output=bias_output, bias_final=bias_final, gain_attention=gain_attention, gain_mixer=gain_mixer, query_scale=query_scale, lengths=lengths, cotangent=cotangent)


EPSILON = 1e-06
SOFTPLUS_UNIT = 1.442695041
HIGH = lax.Precision.HIGHEST

@jax.custom_vjp
def low(v):
    return lax.optimization_barrier(v.astype(jnp.bfloat16)).astype(jnp.float32)

@jax.custom_vjp
def low_back(v):
    return v

def low_keep(v):
    return (low(v), None)

def low_pass(kept, grad):
    return (grad,)

def back_keep(v):
    return (v, None)

def back_low(kept, grad):
    return (low(grad),)
low.defvjp(low_keep, low_pass)
low_back.defvjp(back_keep, back_low)

def mat_product(left, right):
    return jnp.dot(left, right, precision=HIGH)

def normalize(values, gain):
    mean_square = lax.optimization_barrier(jnp.mean(values * values, axis=-1, keepdims=True))
    return values * lax.rsqrt(mean_square + EPSILON) * gain

def attention(queries, keys_all, values, length):
    block_rows = min(512, SLOT)
    blocks_count = SLOT // block_rows

    def one_block(number):
        offset = (number * block_rows).astype(jnp.int32)
        query_block = lax.dynamic_slice_in_dim(queries, offset, block_rows, 0)
        scores = jnp.einsum('qhd,khd->hqk', query_block, keys_all, precision=HIGH)
        scores = low_back(scores)
        row_place = offset + jnp.arange(block_rows, dtype=jnp.int32)
        col_place = jnp.arange(SLOT, dtype=jnp.int32)
        allowed = (col_place[None, :] <= row_place[:, None]) & (col_place[None, :] < length)
        scores = jnp.where(allowed[None], scores, -1e+30)
        maximum = lax.optimization_barrier(jnp.max(scores, axis=-1, keepdims=True))
        raised = jnp.exp(scores - maximum)
        chances = low(raised / lax.optimization_barrier(jnp.sum(raised, axis=-1, keepdims=True)))
        context = jnp.einsum('hqk,khd->qhd', chances, values, precision=HIGH)
        return low(low_back(context))
    blocks = lax.map(jax.checkpoint(one_block), jnp.arange(blocks_count, dtype=jnp.int32))
    return blocks.reshape(SLOT, HEADS, HD)

def layer(params, inputs_f, length):
    w_query, w_key, w_value, w_output, w_hidden, w_down, b_query, b_value, b_hidden, b_output, b_final, g_attention, g_mixer, q_scale = params
    h_one = low(normalize(inputs_f, g_attention))
    query_raw = low_back(mat_product(h_one, w_query) + b_query)
    key_raw = mat_product(h_one, w_key)
    value_raw = mat_product(h_one, w_value) + b_value
    scale = jax.nn.softplus(q_scale) * SOFTPLUS_UNIT / jnp.sqrt(jnp.float32(HD))
    queries = low(low_back(query_raw.reshape(SLOT, HEADS, HD) * scale))
    keys_all = low(low_back(key_raw.reshape(SLOT, HEADS, HD)))
    values = low(low_back(value_raw.reshape(SLOT, HEADS, HD)))
    context = attention(queries, keys_all, values, length).reshape(SLOT, D)
    mid = inputs_f + low_back(mat_product(context, w_output)) + b_output
    h_two = low(normalize(mid, g_mixer))
    pre = low_back(mat_product(h_two, w_hidden) + b_hidden)
    act = low(jax.nn.silu(pre))
    return mid + low_back(mat_product(act, w_down)) + b_final

def reference(inputs, weight_query, weight_key, weight_value, weight_output, weight_hidden, weight_down, bias_query, bias_value, bias_hidden, bias_output, bias_final, gain_attention, gain_mixer, query_scale, lengths, cotangent):
    params = tuple((a.astype(jnp.float32) for a in (weight_query, weight_key, weight_value, weight_output, weight_hidden, weight_down, bias_query, bias_value, bias_hidden, bias_output, bias_final, gain_attention, gain_mixer, query_scale)))
    series_in = inputs.astype(jnp.float32).reshape(SERIES, SLOT, D)
    series_cot = cotangent.astype(jnp.float32).reshape(SERIES, SLOT, D)

    def step(totals, item):
        inputs_f, cot_f, length = item
        live = (jnp.arange(SLOT, dtype=jnp.int32) < length).astype(jnp.float32)[:, None]
        final, pull = jax.vjp(lambda p, xx: layer(p, xx, length), params, inputs_f)
        grad_params, grad_in = pull(cot_f * live)
        totals = jax.tree.map(lambda a, b: a + b, totals, grad_params)
        return (totals, (final, grad_in))
    zeros = jax.tree.map(jnp.zeros_like, params)
    totals, (finals, grads_in) = lax.scan(step, zeros, (series_in, series_cot, lengths))
    output = finals.reshape(TOKENS, D).astype(jnp.bfloat16)
    grad_inputs = grads_in.reshape(TOKENS, D).astype(jnp.bfloat16)
    return (output, grad_inputs, totals[0], totals[1], totals[2], totals[3], totals[4], totals[5], totals[6], totals[7], totals[8], totals[9], totals[10], totals[11], totals[12], totals[13])
```

```python
import jax
import jax.numpy as jnp
from jax import lax
from jax.sharding import PartitionSpec as P

EPSILON = 1e-06
SOFTPLUS_UNIT = 1.442695041
AXES = ("dp", "tensor")
F32 = jnp.float32
BF16 = jnp.bfloat16


def dot(left, right, dims):
    return lax.dot_general(left, right, (dims, ((), ())), preferred_element_type=F32)


def normalize(values):
    mean_square = jnp.mean(values * values, axis=-1, keepdims=True)
    inverse = lax.rsqrt(mean_square + EPSILON)
    return (values * inverse, inverse)


def norm_back(grad_normed, normed, inverse, gain):
    scaled = grad_normed * gain
    return inverse * (scaled - normed * jnp.mean(scaled * normed, axis=-1, keepdims=True))


def silu_slope(pre):
    sigma = jax.nn.sigmoid(pre)
    return sigma * (1.0 + pre * (1.0 - sigma))


class Links:
    def __init__(self, n_dp, n_tensor):
        self.n_dp, self.n_tensor = n_dp, n_tensor
        self.ring = n_dp // 2

    def move(self, value, target):
        pairs = []
        for d in range(self.n_dp):
            for t in range(self.n_tensor):
                to_d, to_t = target(d, t)
                pairs.append((d * self.n_tensor + t, to_d * self.n_tensor + to_t))
        return lax.ppermute(value, AXES, pairs)

    def chip(self, value):
        return self.move(value, lambda d, t: (d, t ^ 2))

    def core(self, value):
        return self.move(value, lambda d, t: (d, t ^ 1))

    def pair(self, value):
        return self.move(value, lambda d, t: (d ^ 1, t))

    def shift(self, value, step):
        n = self.ring
        return self.move(value, lambda d, t: (((d // 2 + step) % n) * 2 + d % 2, t))

    def gather_tensor(self, rows):
        both = jnp.concatenate([rows, self.chip(rows)], axis=0)
        return jnp.concatenate([both, self.core(both)], axis=0)

    def scatter_tensor(self, rows):
        half = rows.shape[0] // 2
        got = self.core(rows[half:].astype(BF16))
        rows = rows[:half] + got.astype(F32)
        got = self.chip(rows[half // 2 :].astype(BF16))
        return rows[: half // 2] + got.astype(F32)

    def gather_dp(self, shard):
        blocks = []
        for j in range(self.ring):
            if j:
                shard = self.shift(shard, -1)
            blocks += [shard, self.pair(shard)]
        return jnp.concatenate(blocks, axis=0)

    def scatter_dp(self, total):
        depth = total.shape[0] // self.n_dp
        running = None
        for j in reversed(range(self.ring)):
            own = total[2 * j * depth : (2 * j + 1) * depth]
            other = total[(2 * j + 1) * depth : (2 * j + 2) * depth]
            summed = own.astype(F32) + self.pair(other).astype(F32)
            if running is not None:
                summed = summed + self.shift(running, 1).astype(F32)
            running = summed.astype(BF16) if j else summed
        return running

    def reduce_all(self, value):
        bit = 1
        while bit < self.n_tensor:
            value = value + self.move(value, lambda d, t: (d, t ^ bit))
            bit *= 2
        bit = 1
        while bit < self.n_dp:
            value = value + self.move(value, lambda d, t: (d ^ bit, t))
            bit *= 2
        return value


def body(
    inputs,
    weight_query,
    weight_key,
    weight_value,
    weight_output,
    weight_hidden,
    weight_down,
    bias_query,
    bias_value,
    bias_hidden,
    bias_output,
    bias_final,
    gain_attention,
    gain_mixer,
    query_scale,
    lengths,
    cotangent,
    n_dp,
    n_tensor,
):
    links = Links(n_dp, n_tensor)
    local_rows, width = inputs.shape
    depth = width // n_dp
    local_width = weight_query.shape[1]
    head_size = query_scale.shape[0]
    local_heads = local_width // head_size
    dp_index = lax.axis_index("dp")
    tensor_index = lax.axis_index("tensor")
    length = lengths[0]
    ring_place, pair_place = dp_index // 2, dp_index % 2

    def mine(vector):
        cut = vector.reshape(n_dp // 2, 2, depth)
        cut = jnp.roll(cut, -ring_place, axis=0)
        return jnp.where(pair_place == 1, cut[:, ::-1], cut).reshape(width)

    def whole(vector):
        cut = vector.reshape(n_dp // 2, 2, depth)
        cut = jnp.where(pair_place == 1, cut[:, ::-1], cut)
        return jnp.roll(cut, ring_place, axis=0).reshape(width)

    feature = lax.iota(jnp.int32, width)
    block = feature // depth
    source = (((ring_place + block // 2) % (n_dp // 2)) * 2 + (pair_place ^ (block % 2))) * depth
    source = source + feature % depth
    select = (feature[:, None] == source[None, :]).astype(BF16)

    x_own = dot(inputs, select, ((1,), (0,)))
    cotangent_own = dot(cotangent, select, ((1,), (0,)))
    gain_one, gain_two = mine(gain_attention), mine(gain_mixer)
    b_output, b_final = mine(bias_output), mine(bias_final)

    row = lax.iota(jnp.int32, local_rows)
    place = jnp.concatenate([(tensor_index ^ k) * local_rows + row for k in (0, 2, 1, 3)])
    all_rows = place.shape[0]
    live = (tensor_index * local_rows + row < length).astype(F32)[:, None]

    query_key = links.gather_dp(jnp.concatenate([weight_query, weight_key], axis=1))
    value_output = links.gather_dp(jnp.concatenate([weight_value, weight_output.T], axis=1))
    hidden_down = links.gather_dp(jnp.concatenate([weight_hidden, weight_down.T], axis=1))
    w_query, w_key = query_key[:, :local_width], query_key[:, local_width:]
    w_value, w_output = value_output[:, :local_width], value_output[:, local_width:]
    w_hidden, w_down = hidden_down[:, :local_width], hidden_down[:, local_width:]

    def share(vector):
        return lax.dynamic_slice_in_dim(vector, tensor_index * local_width, local_width, 0)

    normed_one, inverse_one = normalize(x_own)
    h_one = links.gather_tensor((normed_one * gain_one).astype(BF16))
    grad_final = cotangent_own * live
    grad_low = links.gather_tensor(grad_final.astype(BF16))

    scale = jax.nn.softplus(query_scale) * SOFTPLUS_UNIT / jnp.sqrt(F32(head_size))
    query_raw = dot(h_one, w_query, ((1,), (0,))) + share(bias_query)
    query_raw = query_raw.reshape(all_rows, local_heads, head_size)
    queries = (query_raw * scale).astype(BF16)
    keys = dot(h_one, w_key, ((1,), (0,))).astype(BF16).reshape(all_rows, local_heads, head_size)
    values = (dot(h_one, w_value, ((1,), (0,))) + share(bias_value)).astype(BF16)
    values = values.reshape(all_rows, local_heads, head_size)

    allowed = ((place[None, :] <= place[:, None]) & (place[None, :] < length))[None]
    scores = jnp.einsum("qhd,khd->hqk", queries, keys, preferred_element_type=F32)
    masked = jnp.where(allowed, scores, -1e30)
    maximum = jnp.max(masked, axis=-1, keepdims=True)
    raised = jnp.exp(masked - maximum)
    chances = raised / jnp.sum(raised, axis=-1, keepdims=True)
    chances_low = chances.astype(BF16)
    context = jnp.einsum("hqk,khd->qhd", chances_low, values, preferred_element_type=F32)
    context = context.astype(BF16).reshape(all_rows, local_width)
    attention_out = links.scatter_tensor(dot(context, w_output, ((1,), (1,))))
    middle = x_own + attention_out + b_output

    normed_two, inverse_two = normalize(middle)
    h_two = links.gather_tensor((normed_two * gain_two).astype(BF16))
    pre = dot(h_two, w_hidden, ((1,), (0,))) + share(bias_hidden)
    act = jax.nn.silu(pre).astype(BF16)
    grad_act = dot(grad_low, w_down, ((1,), (0,)))
    grad_pre = (grad_act * silu_slope(pre)).astype(BF16)
    grad_b_hidden = jnp.sum(grad_pre.astype(F32), axis=0)
    grad_h_two = links.scatter_tensor(dot(grad_pre, w_hidden, ((1,), (1,))))
    mixer_out = links.scatter_tensor(dot(act, w_down, ((1,), (1,))))
    final = middle + mixer_out + b_final
    term_hidden = dot(h_two, grad_pre, ((0,), (0,))).astype(BF16)
    term_down = dot(grad_low, act, ((0,), (0,))).astype(BF16)
    owned_hd = links.scatter_dp(jnp.concatenate([term_hidden, term_down], axis=1))

    grad_b_final = jnp.sum(grad_final, axis=0)
    grad_g_mixer = jnp.sum(grad_h_two * normed_two, axis=0)
    grad_middle = grad_final + norm_back(grad_h_two, normed_two, inverse_two, gain_two)
    grad_b_output = jnp.sum(grad_middle, axis=0)
    grad_middle_all = links.gather_tensor(grad_middle.astype(BF16))
    term_output = dot(grad_middle_all, context, ((0,), (0,))).astype(BF16)
    grad_context = dot(grad_middle_all, w_output, ((1,), (0,))).astype(BF16)
    grad_context = grad_context.reshape(all_rows, local_heads, head_size)

    grad_values = jnp.einsum("hqk,qhd->khd", chances_low, grad_context, preferred_element_type=F32)
    grad_v = grad_values.astype(BF16).reshape(all_rows, local_width)
    term_value = dot(h_one, grad_v, ((0,), (0,))).astype(BF16)
    owned_vo = links.scatter_dp(jnp.concatenate([term_value, term_output], axis=1))
    grad_chances = jnp.einsum("qhd,khd->hqk", grad_context, values, preferred_element_type=F32)
    center = jnp.sum(chances * grad_chances, axis=-1, keepdims=True)
    grad_scores = (chances * (grad_chances - center)).astype(BF16)
    grad_queries = jnp.einsum("hqk,khd->qhd", grad_scores, keys, preferred_element_type=F32)
    grad_keys = jnp.einsum("hqk,qhd->khd", grad_scores, queries, preferred_element_type=F32)
    grad_scaled = grad_queries.astype(BF16).astype(F32)
    scale_sum = jnp.sum(grad_scaled * query_raw, axis=(0, 1))
    grad_q_scale = scale_sum * jax.nn.sigmoid(query_scale) * SOFTPLUS_UNIT / jnp.sqrt(F32(head_size))
    grad_q = (grad_scaled * scale).astype(BF16).reshape(all_rows, local_width)
    grad_k = grad_keys.astype(BF16).reshape(all_rows, local_width)
    grad_h_one = links.scatter_tensor(
        dot(grad_q, w_query, ((1,), (1,)))
        + dot(grad_k, w_key, ((1,), (1,)))
        + dot(grad_v, w_value, ((1,), (1,)))
    )
    term_query = dot(h_one, grad_q, ((0,), (0,))).astype(BF16)
    term_key = dot(h_one, grad_k, ((0,), (0,))).astype(BF16)
    owned_qk = links.scatter_dp(jnp.concatenate([term_query, term_key], axis=1))

    grad_g_attention = jnp.sum(grad_h_one * normed_one, axis=0)
    grad_in = grad_middle + norm_back(grad_h_one, normed_one, inverse_one, gain_one)

    def spread(vector):
        zeros = jnp.zeros((n_tensor * local_width,), F32)
        return lax.dynamic_update_slice_in_dim(zeros, vector, tensor_index * local_width, 0)

    pieces = (
        spread(jnp.sum(grad_q.astype(F32), axis=0)),
        spread(jnp.sum(grad_v.astype(F32), axis=0)),
        spread(grad_b_hidden),
        whole(grad_b_output),
        whole(grad_b_final),
        whole(grad_g_attention),
        whole(grad_g_mixer),
        jnp.pad(grad_q_scale, (0, width - head_size)),
    )
    sums = links.reduce_all(jnp.stack(pieces))

    output = dot(final.astype(BF16), select, ((1,), (1,))).astype(BF16)
    grad_in = dot(grad_in.astype(BF16), select, ((1,), (1,))).astype(BF16)
    return (
        output,
        grad_in,
        owned_qk[:, :local_width],
        owned_qk[:, local_width:],
        owned_vo[:, :local_width],
        owned_vo[:, local_width:].T,
        owned_hd[:, :local_width],
        owned_hd[:, local_width:].T,
        *(sums[k] for k in range(7)),
        sums[7, :head_size],
    )


def solution(mesh):
    n_dp, n_tensor = mesh.shape["dp"], mesh.shape["tensor"]

    def local(*arguments):
        return body(*arguments, n_dp, n_tensor)

    rows = P(("dp", "tensor"), None)
    into, out_of = P("dp", "tensor"), P("tensor", "dp")
    return jax.shard_map(
        local,
        mesh=mesh,
        in_specs=(rows, into, into, into, out_of, into, out_of, *[P()] * 8, P("dp"), rows),
        out_specs=(rows, rows, into, into, into, out_of, into, out_of, *[P()] * 8),
        check_vma=False,
    )
```

```python
import jax
import jax.numpy as jnp
from jax import lax
from jax.experimental import pallas as pl
from jax.experimental.pallas import tpu as pltpu
from jax.sharding import PartitionSpec as P

EPSILON = 1e-06
SOFTPLUS_UNIT = 1.442695041
AXES = ("dp", "tensor")
F32 = jnp.float32
BF16 = jnp.bfloat16
LANES = 128
TENSOR_ORDER = (0, 2, 1, 3)
NN, NT, TN = ((1,), (0,)), ((1,), (1,)), ((0,), (0,))


def dot(left, right, dims=NN):
    return lax.dot_general(left, right, (dims, ((), ())), preferred_element_type=F32)


def shaped(shape, kind):
    return jax.ShapeDtypeStruct(shape, kind)


def call(name, kernel, outs, scalars, *arguments, flops=1e6, scratch=(), limit=12, remote=0):
    space = pl.BlockSpec(memory_space=pltpu.VMEM)
    apart = pl.BlockSpec(memory_space=pltpu.HBM)
    moved = sum(a.size * a.dtype.itemsize for a in (*arguments, *outs))
    return pl.pallas_call(
        kernel,
        name=name,
        out_shape=outs,
        in_specs=[pl.BlockSpec(memory_space=pltpu.SMEM)]
        + [space] * (len(arguments) - remote)
        + [apart] * remote,
        out_specs=[space] * len(outs),
        scratch_shapes=scratch,
        compiler_params=pltpu.CompilerParams(vmem_limit_bytes=limit << 20),
        cost_estimate=pl.CostEstimate(flops=int(flops), bytes_accessed=moved, transcendentals=0),
    )(scalars, *arguments)


def pack(first, second):
    main = first.shape[1] // LANES * LANES
    return jnp.concatenate([first[:, :main], second[:, :main], first[:, main:], second[:, main:]], axis=1)


def unpack(both):
    width = both.shape[1] // 2
    main = width // LANES * LANES
    edge = main * 2 + width - main
    first = jnp.concatenate([both[:, :main], both[:, 2 * main : edge]], axis=1)
    rest = both[:, 2 * main :].astype(F32)[:, width - main :].astype(both.dtype)
    second = jnp.concatenate([both[:, main : 2 * main], rest], axis=1)
    return first, second


def to_own(value, ring, pair, n_dp):
    width = value.shape[1]
    depth = width // n_dp
    value = swap_pairs(value, pair, depth)
    bit = 1
    while bit < n_dp // 2:
        moved = pltpu.roll(value, width - bit * 2 * depth, 1)
        value = jnp.where((ring & bit) != 0, moved, value)
        bit *= 2
    return value


def from_own(value, ring, pair, n_dp):
    width = value.shape[1]
    depth = width // n_dp
    bit = 1
    while bit < n_dp // 2:
        moved = pltpu.roll(value, bit * 2 * depth, 1)
        value = jnp.where((ring & bit) != 0, moved, value)
        bit *= 2
    return swap_pairs(value, pair, depth)


def swap_pairs(value, pair, depth):
    width = value.shape[1]
    lane = lax.broadcasted_iota(jnp.int32, value.shape, 1)
    low = lax.rem(lane, 2 * depth) < depth
    other = jnp.where(low, pltpu.roll(value, width - depth, 1), pltpu.roll(value, depth, 1))
    return jnp.where(pair != 0, other, value)


def row_mean(value):
    return jnp.sum(value, axis=1, keepdims=True) * (1.0 / value.shape[1])


def normalize(value):
    inverse = lax.rsqrt(row_mean(value * value) + EPSILON)
    return value * inverse, inverse


def norm_back(grad_normed, normed, inverse, gain):
    scaled = grad_normed * gain
    return inverse * (scaled - normed * row_mean(scaled * normed))


def load(sources, targets, sem):
    copies = [pltpu.make_async_copy(a, b, sem.at[k]) for k, (a, b) in enumerate(zip(sources, targets))]
    for copy in copies:
        copy.start()
    for copy in copies:
        copy.wait()


def pack_kernel(s, first, second, out, one, two, sem):
    load((first, second), (one, two), sem)
    out[...] = pack(one[...].astype(F32), two[...].astype(F32)).astype(BF16)


def row_of(ref):
    return jnp.concatenate([ref[k : k + 1] for k in range(ref.shape[0])], axis=1)


def prepare_kernel(n_dp, s, scale, *refs):
    sources, (h, x_own, grad, vectors, biases) = refs[:9], refs[9:14]
    x, cotangent, *given = refs[14:23]
    load(sources, refs[14:23], refs[23])
    ring, pair, place, length = s[0], s[1], s[2], s[3]
    value = to_own(x[...].astype(F32), ring, pair, n_dp)
    stacked = jnp.concatenate([row_of(given[k]) for k in (0, 1, 2, 3, 4, 5, 6, 6)], axis=0)
    width = biases.shape[1]
    mine = stacked[:, :width]
    for number in range(1, stacked.shape[1] // width):
        mine = jnp.where(place == number, stacked[:, number * width : (number + 1) * width], mine)
    biases[...] = mine
    biases[7:8] = scale[...]
    stacked = to_own(stacked, ring, pair, n_dp)
    normed, _ = normalize(value)
    h[...] = (normed * stacked[0:1]).astype(BF16)
    x_own[...] = value.astype(BF16)
    rows = value.shape[0]
    row = lax.broadcasted_iota(jnp.int32, value.shape, 0) + place * rows
    g = jnp.where(row < length, to_own(cotangent[...].astype(F32), ring, pair, n_dp), 0.0)
    grad[...] = g.astype(BF16)
    vectors[...] = stacked
    vectors[4:5] = jnp.sum(g, axis=0, keepdims=True)


def join(pieces, out):
    rows = pieces[0].shape[0]
    for number, piece in enumerate(pieces):
        out[pl.ds(number * rows, rows)] = piece[...]


def tiles(rows, body, size=128):
    def step(m, carry):
        body(pl.ds(pl.multiple_of(m * size, size), size), m)
        return carry

    lax.fori_loop(0, rows // size, step, 0)


def positions(shape, axis, place, local, offset=0):
    row = lax.broadcasted_iota(jnp.int32, shape, axis) + offset
    shift = local.bit_length() - 1
    block = row >> shift
    turned = ((block & 1) << 1) | (block >> 1)
    return ((place ^ turned) << shift) + (row & (local - 1))


def fetch(blocks, out, sem):
    depth = blocks[0].shape[0]
    n_ring = out.shape[0] // (2 * depth)
    copies = []

    def copy(source, row):
        copies.append(pltpu.make_async_copy(source, out.at[pl.ds(row, depth)], sem.at[len(copies)]))

    if n_ring == 0:
        copy(blocks[0], 0)
    else:
        for j in range(n_ring):
            copy(blocks[j], 2 * j * depth)
        j = 0
        for block in blocks[n_ring:]:
            for k in range(block.shape[0] // depth):
                copy(block.at[pl.ds(k * depth, depth)], (2 * j + 1) * depth)
                j += 1
    for one in copies:
        one.start()
    return copies


def stack_kernel(s, *refs):
    join(refs[:-1], refs[-1])


def of_head(value, number, head_size):
    lanes = lax.broadcasted_iota(jnp.int32, (1, value.shape[1]), 1) // head_size
    return jnp.where(lanes == number, value, jnp.zeros((), value.dtype))


def attend_kernel(n_blocks, head_size, s, p0, p1, p2, p3, biases, *refs):
    blocks, (q_raw, q_low, k_low, h, weight, turned, sem) = refs[:n_blocks], refs[n_blocks:]
    copies = fetch(blocks, weight, sem)
    join((p0, p1, p2, p3), h)
    for copy in copies:
        copy.wait()
    first, second = unpack(dot(h[...], weight[...]))
    first = first + biases[4:5]
    q_raw[...] = first
    q_low[...] = (first * biases[7:8]).astype(BF16)
    k_low[...] = second.astype(BF16)
    place, length = s[2], s[3]
    rows, local = q_low.shape[0], p0.shape[0]
    key_place = positions((rows, 1), 0, place, local)

    def head(number, carry):
        def part(at, m):
            score = dot(k_low[...], of_head(q_low[at], number, head_size), NT)
            query_place = positions((1, 128), 1, place, local, m * 128)
            last = jnp.minimum(query_place, length - 1)
            score = jnp.where(key_place <= last, score, -1e30)
            raised = jnp.exp(score - jnp.max(score, axis=0, keepdims=True))
            share = 1.0 / jnp.sum(raised, axis=0, keepdims=True)
            turned[number, :, at] = (raised * share).astype(BF16)

        tiles(rows, part)
        return carry

    lax.fori_loop(0, turned.shape[0], head, 0)


def mixed_heads(turned, value, head_size, dims):
    total = None
    for number in range(turned.shape[0]):
        term = dot(turned[number], of_head(value, number, head_size), dims)
        total = term if total is None else total + term
    return total


def split_weight(weight, one, two):
    def body(at, m):
        one[at], two[at] = unpack(weight[at])

    tiles(weight.shape[0], body)


def context_kernel(head_size, n_blocks, s, h, turned, biases, *refs):
    blocks, (v_low, context, far, near, w_value, w_output, weight, sem) = refs[:n_blocks], refs[n_blocks:]
    for copy in fetch(blocks, weight, sem):
        copy.wait()
    split_weight(weight, w_value, w_output)
    v_low[...] = (dot(h[...], w_value[...]) + biases[5:6]).astype(BF16)
    context[...] = mixed_heads(turned, v_low[...], head_size, TN).astype(BF16)
    split_product(context, w_output, far, near)


def split_product(left, right, far, near, extra=None, along=None):
    half, total = near.shape[0], None
    for start, out in ((half, far), (0, near)):
        at = pl.ds(start, half)
        value = dot(left[at], right[...], NT)
        if extra is not None:
            value = value + dot(extra[0][at], extra[1][...], NT)
        out[...] = value.astype(out.dtype)
        if along is not None:
            summed = jnp.sum(value * along[at].astype(F32), axis=0, keepdims=True)
            total = summed if total is None else total + summed
    return total


def middle_kernel(s, near, got, send, keep):
    rows = send.shape[0]
    send[...] = (near[rows:] + got[rows:].astype(F32)).astype(BF16)
    keep[...] = near[:rows] + got[:rows].astype(F32)


def second_norm_kernel(s, keep, got, x_own, vectors, x_one, h):
    value = x_own[...].astype(F32) + keep[...] + got[...].astype(F32) + vectors[2:3]
    x_one[...] = value
    normed, _ = normalize(value)
    h[...] = (normed * vectors[1:2]).astype(BF16)


def grad_act_kernel(n_blocks, s, p0, p1, p2, p3, *refs):
    blocks, (grad_act, g, w_hidden, w_down, weight, sem) = refs[:n_blocks], refs[n_blocks:]
    copies = fetch(blocks, weight, sem)
    join((p0, p1, p2, p3), g)
    for copy in copies:
        copy.wait()
    split_weight(weight, w_hidden, w_down)
    grad_act[...] = dot(g[...], w_down[...])


def hidden_kernel(s, p0, p1, p2, p3, w_hidden, biases, grad_act, out_far, out_near, act, grad_pre, h):
    join((p0, p1, p2, p3), h)
    pre = dot(h[...], w_hidden[...]) + biases[6:7]
    sigma = jax.nn.sigmoid(pre)
    act[...] = (pre * sigma).astype(BF16)
    grad_pre[...] = (grad_act[...] * (sigma * (1.0 + pre * (1.0 - sigma)))).astype(BF16)
    split_product(grad_pre, w_hidden, out_far, out_near)


def spread_terms(term, keep, sends, depth, order):
    if not sends:
        keep[...] = term[...]
        return
    half = len(order) // len(sends)
    for at, j in enumerate(order):
        keep[pl.ds(at * depth, depth)] = term[pl.ds(2 * j * depth, depth)]
        sends[at // half][pl.ds(at % half * depth, depth)] = term[pl.ds((2 * j + 1) * depth, depth)]


def two_terms(left_one, right_one, left_two, right_two, term):
    first = dot(left_one[...], right_one[...], TN)
    second = dot(left_two[...], right_two[...], TN)
    term[...] = pack(first, second).astype(BF16)


def down_kernel(depth, order, s, h, g, act, grad_pre, w_down, far, near, b_hidden, keep, *refs):
    *sends, term = refs
    two_terms(h, grad_pre, g, act, term)
    spread_terms(term, keep, sends, depth, order)
    b_hidden[...] = jnp.sum(grad_pre[...].astype(F32), axis=0, keepdims=True)
    split_product(act, w_down, far, near)


def pair_kernel(start, s, own, got, *outs):
    depth = outs[0].shape[0]
    for k, out in enumerate(outs):
        value = own[pl.ds((start + k) * depth, depth)].astype(F32) + got[pl.ds(k * depth, depth)].astype(F32)
        out[...] = value.astype(out.dtype)


def owned_kernel(n_got, s, keep, *refs):
    total = keep[...]
    for got in refs[:n_got]:
        total = total + got[...].astype(F32)
    refs[n_got][...], refs[n_got + 1][...] = unpack(total)


def grad_middle_kernel(s, keep, got, x_one, grad, vectors, grad_low, grad_full, sums):
    normed, inverse = normalize(x_one[...])
    grad_h = keep[...] + got[...].astype(F32)
    full = grad[...].astype(F32) + norm_back(grad_h, normed, inverse, vectors[1:2])
    grad_full[...] = full
    grad_low[...] = full.astype(BF16)
    sums[...] = vectors[...]
    sums[5:6] = jnp.sum(full, axis=0, keepdims=True)
    sums[6:7] = jnp.sum(grad_h * normed, axis=0, keepdims=True)


def grad_context_kernel(depth, order, head_size, s, p0, p1, p2, p3, w_output, turned, context, h, *refs):
    grad_context, grad_value, gm, keep, *sends, term = refs
    join((p0, p1, p2, p3), gm)
    grad_context[...] = dot(gm[...], w_output[...]).astype(BF16)
    grad_value[...] = mixed_heads(turned, grad_context[...], head_size, NN).astype(BF16)
    two_terms(h, grad_value, gm, context, term)
    spread_terms(term, keep, sends, depth, order)


def grad_scores_kernel(head_size, s, turned, grad_context, v_low, q_low, k_low, q_raw, biases, *refs):
    grad_qk, sums, grad_q, grad_k, scores = refs
    rows = q_low.shape[0]
    grad_q[...] = jnp.zeros_like(grad_q)
    grad_k[...] = jnp.zeros_like(grad_k)

    def head(number, carry):
        def part(at, m):
            grad_chance = dot(v_low[...], of_head(grad_context[at], number, head_size), NT)
            chance = turned[number, :, at].astype(F32)
            product = chance * grad_chance
            center = jnp.sum(product, axis=0, keepdims=True)
            scores[:, at] = (product - chance * center).astype(BF16)

        tiles(rows, part)
        grad_q[...] += dot(scores[...], of_head(k_low[...], number, head_size), TN)
        grad_k[...] += dot(scores[...], of_head(q_low[...], number, head_size))
        return carry

    lax.fori_loop(0, turned.shape[0], head, 0)
    low = grad_q[...].astype(BF16).astype(F32)
    sums[0:1] = jnp.sum(low * q_raw[...], axis=0, keepdims=True)
    low = (low * biases[7:8]).astype(BF16).astype(F32)
    grad_qk[...] = pack(low, grad_k[...]).astype(BF16)
    sums[1:2] = jnp.sum(low, axis=0, keepdims=True)


def grad_first_kernel(
    n_dp, depth, order, s, grad_qk, w_qk, grad_value, w_value, h, sums_in, sums_q, b_hidden, slope, *refs
):
    far, near, sums, keep, *sends, term = refs
    term[...] = dot(h[...], grad_qk[...], TN).astype(BF16)
    spread_terms(term, keep, sends, depth, order)
    ring, pair, place = s[0], s[1], s[2]
    gained = split_product(grad_qk, w_qk, far, near, (grad_value, w_value), h) / sums_in[0:1]
    row = lax.broadcasted_iota(jnp.int32, sums.shape, 0)
    sums[...] = from_own(jnp.where(row == 7, gained, sums_in[...]), ring, pair, n_dp)
    sums[0:4] = jnp.zeros((4, sums.shape[1]), F32)
    local_width, head_size = sums_q.shape[1], slope.shape[1]
    b_value = jnp.sum(grad_value[...].astype(F32), axis=0, keepdims=True)
    share = jnp.concatenate([sums_q[1:2], b_value, b_hidden[...]], axis=0)
    for number in range(sums.shape[1] // local_width):

        @pl.when(place == number)
        def _():
            sums[0:3, number * local_width : (number + 1) * local_width] = share

    scale = sums_q[0:1]
    total = scale[:, :head_size]
    for number in range(1, local_width // head_size):
        total = total + scale[:, number * head_size : (number + 1) * head_size]
    sums[3:4, :head_size] = total * slope[...]


def last_kernel(n_dp, s, keep, got, x_own, grad_full, sums_in, grad_in):
    normed, inverse = normalize(x_own[...].astype(F32))
    grad_h = keep[...] + got[...].astype(F32)
    full = grad_full[...] + norm_back(grad_h, normed, inverse, sums_in[0:1])
    grad_in[...] = from_own(full, s[0], s[1], n_dp).astype(BF16)


def add_kernel(s, one, two, out):
    out[...] = one[...] + two[...]


def output_kernel(n_dp, s, keep, got, x_one, vectors, out):
    value = x_one[...] + keep[...] + got[...].astype(F32) + vectors[3:4]
    out[...] = from_own(value, s[0], s[1], n_dp).astype(BF16)


def tie(*values):
    return lax.optimization_barrier(values)


class Links:
    def __init__(self, n_dp, n_tensor):
        self.n_dp, self.n_tensor = n_dp, n_tensor
        self.ring = n_dp // 2
        self.wide = self.ring > 4
        order = sorted(range(1, self.ring), key=lambda j: -min(j, self.ring - j))
        self.order = [] if self.wide else order

    def move(self, value, target):
        pairs = []
        for d in range(self.n_dp):
            for t in range(self.n_tensor):
                to_d, to_t = target(d, t)
                pairs.append((d * self.n_tensor + t, to_d * self.n_tensor + to_t))
        return lax.ppermute(value, AXES, pairs)

    def chip(self, value):
        return self.move(value, lambda d, t: (d, t ^ 2))

    def core(self, value):
        return self.move(value, lambda d, t: (d, t ^ 1))

    def pair(self, value):
        return self.move(value, lambda d, t: (d ^ 1, t))

    def shift(self, value, step):
        n = self.ring
        return self.move(value, lambda d, t: (((d // 2 + step) % n) * 2 + d % 2, t))

    def gather_tensor(self, rows):
        near = self.chip(rows)
        return rows, near, self.core(rows), self.core(near)

    def gather_ring(self, shard):
        if self.wide:
            blocks = lax.all_gather(shard, "dp", axis=0)
            place = lax.axis_index("dp")
            blocks = jnp.roll(blocks.reshape(self.ring, 2, *shard.shape), -(place >> 1), axis=0)
            blocks = jnp.where((place & 1) == 1, blocks[:, ::-1], blocks)
            return [blocks.reshape(self.n_dp * shard.shape[0], shard.shape[1])]
        got = {0: shard}
        for j in self.order:
            got[j] = self.shift(shard, -j)
        return [got[j] for j in range(self.ring)]

    def scatter_wide(self, total):
        place = lax.axis_index("dp")
        blocks = total.reshape(self.ring, 2, total.shape[0] // self.n_dp, total.shape[1])
        blocks = jnp.where((place & 1) == 1, blocks[:, ::-1], blocks)
        blocks = jnp.roll(blocks, place >> 1, axis=0).reshape(total.shape).astype(F32)
        return unpack(lax.psum_scatter(blocks, "dp", scatter_dimension=0, tiled=True))

    def steps(self):
        found, bit = [lambda d, t: (d, t ^ 1)], 2
        while bit < self.n_dp:
            found.append(lambda d, t, bit=bit: (d ^ bit, t))
            bit *= 2
        return found + [lambda d, t: (d, t ^ 2), lambda d, t: (d ^ 1, t)]


def body(
    inputs,
    weight_query,
    weight_key,
    weight_value,
    weight_output,
    weight_hidden,
    weight_down,
    bias_query,
    bias_value,
    bias_hidden,
    bias_output,
    bias_final,
    gain_attention,
    gain_mixer,
    query_scale,
    lengths,
    cotangent,
    n_dp,
    n_tensor,
):
    links = Links(n_dp, n_tensor)
    n_ring = n_dp // 2
    local_rows, width = inputs.shape
    all_rows = local_rows * n_tensor
    depth = width // n_dp
    local_width = weight_query.shape[1]
    both = 2 * local_width
    head_size = query_scale.shape[0]
    heads = local_width // head_size
    dp_index = lax.axis_index("dp")
    tensor_index = lax.axis_index("tensor")
    s = jnp.stack([dp_index >> 1, dp_index & 1, tensor_index, lengths[0]])
    product = 2 * all_rows * width * local_width
    mixed = 2 * all_rows * all_rows * local_width

    def run(name, kernel, outs, *arguments, **rest):
        return call(name, kernel, [shaped(*o) for o in outs], s, *arguments, **rest)

    def bind(kernel, *fixed):
        def bound(*refs):
            return kernel(*fixed, *refs)

        return bound

    packed = [((depth, both), BF16)]
    rows_low, rows_full = ((local_rows, width), BF16), ((local_rows, width), F32)
    split = [((all_rows // 2, width), BF16), ((all_rows // 2, width), F32)]
    part = ((all_rows, local_width), BF16)
    part_full = ((all_rows, local_width), F32)
    whole_rows = ((all_rows, width), BF16)
    weight = ((width, local_width), BF16)
    vector = ((8, width), F32)
    halves = [((width // 2, both), BF16)] * 2
    term = [pltpu.VMEM((width, both), BF16)]
    sems = [pltpu.SemaphoreType.DMA((n_dp,))]

    unit = SOFTPLUS_UNIT / jnp.sqrt(F32(head_size))
    scale_wide = jnp.tile(jax.nn.softplus(query_scale) * unit, heads)[None]
    slope = (jax.nn.sigmoid(query_scale) * unit)[None]
    loads = [pltpu.VMEM((depth, local_width), BF16)] * 2 + [pltpu.SemaphoreType.DMA((2,))]

    def apart(value):
        return pltpu.with_memory_space_constraint(value, pltpu.HBM)

    def pack_two(name, one, two):
        return run("pack_" + name, pack_kernel, packed, apart(one), apart(two), remote=2, scratch=loads)[0]

    own_qk = pack_two("qk", weight_query, weight_key)
    ring_qk = links.gather_ring(own_qk)
    given = (gain_attention, gain_mixer, bias_output, bias_final, bias_query, bias_value, bias_hidden)
    scale_wide, slope = tie(scale_wide, slope)
    tall = (width // LANES, LANES)
    h_own, x_own, grad_own, vectors, biases = run(
        "prepare",
        bind(prepare_kernel, n_dp),
        [rows_low, rows_low, rows_low, vector, ((8, local_width), F32)],
        scale_wide,
        *(apart(v) for v in (inputs, cotangent, *(v.reshape(tall) for v in given))),
        remote=9,
        scratch=[pltpu.VMEM((local_rows, width), BF16)] * 2
        + [pltpu.VMEM(tall, F32)] * 7
        + [pltpu.SemaphoreType.DMA((9,))],
    )
    own_vo = pack_two("vo", weight_value, weight_output.T)
    own_hd = pack_two("hd", weight_hidden, weight_down.T)
    order = links.order + [0]
    n_half = len(order) // 2

    def partners(blocks):
        if links.wide:
            return []
        (stacked,) = run("stack", stack_kernel, [((len(blocks) * depth, both), BF16)], *blocks)
        return [links.pair(stacked)]

    first_qk = [] if links.wide else [links.pair(own_qk)]
    h_own, ring_qk, first_qk, own_vo, own_hd = tie(h_own, ring_qk, first_qk, own_vo, own_hd)
    h_one = links.gather_tensor(h_own)
    ring_vo = links.gather_ring(own_vo)
    blocks_qk = ring_qk + first_qk + partners(ring_qk[1:])
    h_one, ring_vo, blocks_qk = tie(h_one, ring_vo, blocks_qk)
    blocks_vo = ring_vo + partners(ring_vo)
    ring_hd = links.gather_ring(own_hd)
    q_raw, q_low, k_low, h_all, w_qk, turned = run(
        "attend",
        bind(attend_kernel, len(blocks_qk), head_size),
        [
            part_full,
            part,
            part,
            whole_rows,
            ((width, both), BF16),
            ((heads, all_rows, all_rows), BF16),
        ],
        *h_one,
        biases,
        *blocks_qk,
        remote=len(blocks_qk),
        scratch=sems,
    )
    grad_own, q_low = tie(grad_own, q_low)
    grad_rows = links.gather_tensor(grad_own)
    turned, blocks_vo, ring_hd = tie(turned, blocks_vo, ring_hd)
    blocks_hd = ring_hd + partners(ring_hd)
    v_low, context, far, near, w_value, w_output = run(
        "context",
        bind(context_kernel, head_size, len(blocks_vo)),
        [part, part, *split, weight, weight],
        h_all,
        turned,
        biases,
        *blocks_vo,
        remote=len(blocks_vo),
        scratch=term + sems,
    )

    def core_half(far, near):
        return run("middle", middle_kernel, [rows_low, rows_full], near, links.core(far))

    send, keep = core_half(far, near)
    got = links.chip(send)
    got, blocks_hd, grad_rows = tie(got, blocks_hd, grad_rows)
    x_one, h_two_own = run("second_norm", second_norm_kernel, [rows_full, rows_low], keep, got, x_own, vectors)
    h_two = links.gather_tensor(h_two_own)
    grad_act, grad_all, w_hidden, w_down = run(
        "grad_act",
        bind(grad_act_kernel, len(blocks_hd)),
        [part_full, whole_rows, weight, weight],
        *grad_rows,
        *blocks_hd,
        remote=len(blocks_hd),
        scratch=term + sems,
    )
    far, near, act, grad_pre, h_two_all = run(
        "hidden",
        hidden_kernel,
        [*split, part, part, whole_rows],
        *h_two,
        w_hidden,
        biases,
        grad_act,
    )
    send, keep = core_half(far, near)
    act, send = tie(act, send)
    got = links.chip(send)
    if links.wide:
        terms = [((width, both), BF16)]
    else:
        terms = [((n_ring * depth, both), BF16)] + [((n_half * depth, both), BF16)] * 2
    far, near, grad_b_hidden, *terms_hd = run(
        "down",
        bind(down_kernel, depth, order),
        [*split, ((1, local_width), F32), *terms],
        h_two_all,
        grad_all,
        act,
        grad_pre,
        w_down,
        scratch=term,
    )
    got, terms_hd = tie(got, terms_hd)

    def pair_sum(name, start, keep, got, last):
        count = got.shape[0] // depth
        outs = packed * count
        if last:
            outs = packed * (count - 1) + [((depth, both), F32)]
        return run("pair_" + name, bind(pair_kernel, start), outs, keep, got)

    def ring_send(parts, start):
        return [links.shift(part, j) for part, j in zip(parts, links.order[start:])]

    def owned(name, parts):
        outs = [((depth, local_width), F32)] * 2
        return run("owned_" + name, bind(owned_kernel, n_ring - 1), outs, *parts)

    sent_hd = [links.pair(part) for part in terms_hd[1:]]
    grad_mid_low, grad_mid, sums = run(
        "grad_middle",
        grad_middle_kernel,
        [rows_low, rows_full, vector],
        keep,
        got,
        x_one,
        grad_own,
        vectors,
    )
    grad_mid_rows = links.gather_tensor(grad_mid_low)
    grad_mid_rows, far = tie(grad_mid_rows, far)
    if not links.wide:
        grad_mid_rows, sent_hd[0] = tie(grad_mid_rows, sent_hd[0])
        parts_hd = ring_send(pair_sum("hd_a", 0, terms_hd[0], sent_hd[0], False), 0)
    mix_send, mix_keep = core_half(far, near)
    mix_got = links.chip(mix_send)
    grad_context, grad_value, _, *terms_vo = run(
        "grad_context",
        bind(grad_context_kernel, depth, order, head_size),
        [part, part, whole_rows, *terms],
        *grad_mid_rows,
        w_output,
        turned,
        context,
        h_all,
        scratch=term,
    )
    grad_context, sent_hd[1:] = tie(grad_context, sent_hd[1:])
    sent_vo = [links.pair(part) for part in terms_vo[1:]]
    if not links.wide:
        *parts, zero_hd = pair_sum("hd_b", n_half, terms_hd[0], sent_hd[1], True)
        grad_context, parts = tie(grad_context, parts)
        parts_hd += ring_send(parts, n_half)
    grad_qk, sums_q = run(
        "grad_scores",
        bind(grad_scores_kernel, head_size),
        [((all_rows, both), BF16), ((8, local_width), F32)],
        turned,
        grad_context,
        v_low,
        q_low,
        k_low,
        q_raw,
        biases,
        scratch=[
            pltpu.VMEM((all_rows, local_width), F32),
            pltpu.VMEM((all_rows, local_width), F32),
            pltpu.VMEM((all_rows, all_rows), BF16),
        ],
    )
    grad_qk, sent_vo, mix_got = tie(grad_qk, sent_vo, mix_got)
    if not links.wide:
        grad_qk, parts_hd = tie(grad_qk, parts_hd)
        parts_vo = ring_send(pair_sum("vo_a", 0, terms_vo[0], sent_vo[0], False), 0)
        *parts, zero_vo = pair_sum("vo_b", n_half, terms_vo[0], sent_vo[1], True)
        parts_vo += ring_send(parts, n_half)
    far, near, sums, *terms_qk = run(
        "grad_first",
        bind(grad_first_kernel, n_dp, depth, order),
        [*split, vector, *terms],
        grad_qk,
        w_qk,
        grad_value,
        w_value,
        h_all,
        sums,
        sums_q,
        grad_b_hidden,
        slope,
        scratch=term,
    )
    sent_qk = [links.pair(part) for part in terms_qk[1:]]
    send, keep = core_half(far, near)
    got = links.chip(send)
    steps = links.steps()
    total = sums

    def exchange(value, step):
        return run("add", add_kernel, [vector], value, links.move(value, step))[0]

    for step in steps[:-2]:
        total = exchange(total, step)
    if not links.wide:
        got, sent_qk[0], parts_vo = tie(got, sent_qk[0], parts_vo)
        parts = pair_sum("qk_a", 0, terms_qk[0], sent_qk[0], False)
        got, parts = tie(got, parts)
        parts_qk = ring_send(parts, 0)
    (grad_in,) = run("last", bind(last_kernel, n_dp), [rows_low], keep, got, x_own, grad_mid, vectors)
    total, grad_in = tie(total, grad_in)
    total = exchange(total, steps[-2])
    if not links.wide:
        total, sent_qk[1] = tie(total, sent_qk[1])
        *parts, zero_qk = pair_sum("qk_b", n_half, terms_qk[0], sent_qk[1], True)
        total, parts = tie(total, parts)
        parts_qk += ring_send(parts, n_half)
    total = exchange(total, steps[-1])
    (output,) = run("output", bind(output_kernel, n_dp), [rows_low], mix_keep, mix_got, x_one, vectors)
    if links.wide:
        grad_hidden, grad_down = links.scatter_wide(terms_hd[0])
        grad_output_v, grad_output_o = links.scatter_wide(terms_vo[0])
        grad_query, grad_key = links.scatter_wide(terms_qk[0])
    else:
        grad_hidden, grad_down = owned("hd", [zero_hd, *parts_hd])
        grad_output_v, grad_output_o = owned("vo", [zero_vo, *parts_vo])
        grad_query, grad_key = owned("qk", [zero_qk, *parts_qk])
    return (
        output,
        grad_in,
        grad_query,
        grad_key,
        grad_output_v,
        grad_output_o.T,
        grad_hidden,
        grad_down.T,
        total[0],
        total[1],
        total[2],
        total[5],
        total[4],
        total[7],
        total[6],
        total[3, :head_size],
    )


def solution(mesh):
    n_dp, n_tensor = mesh.shape["dp"], mesh.shape["tensor"]

    def local(*arguments):
        return body(*arguments, n_dp, n_tensor)

    rows = P(("dp", "tensor"), None)
    into, out_of = P("dp", "tensor"), P("tensor", "dp")
    return jax.shard_map(
        local,
        mesh=mesh,
        in_specs=(rows, into, into, into, out_of, into, out_of, *[P()] * 8, P("dp"), rows),
        out_specs=(rows, rows, into, into, into, out_of, into, out_of, *[P()] * 8),
        check_vma=False,
    )
```

```python
import jax
import jax.numpy as jnp
from jax import lax
from jax.experimental import pallas as pl
from jax.experimental.pallas import tpu as pltpu
from jax.sharding import PartitionSpec as P

EPSILON = 1e-06
SOFTPLUS_UNIT = 1.442695041
AXES = ("dp", "tensor")
F32 = jnp.float32
BF16 = jnp.bfloat16
LANES = 128
TENSOR_ORDER = (0, 2, 1, 3)
NN, NT, TN = ((1,), (0,)), ((1,), (1,)), ((0,), (0,))


def dot(left, right, dims=NN):
    return lax.dot_general(left, right, (dims, ((), ())), preferred_element_type=F32)


def shaped(shape, kind):
    return jax.ShapeDtypeStruct(shape, kind)


def call(name, kernel, outs, scalars, *arguments, flops=1e6, scratch=(), limit=12, remote=0):
    space = pl.BlockSpec(memory_space=pltpu.VMEM)
    apart = pl.BlockSpec(memory_space=pltpu.HBM)
    moved = sum(a.size * a.dtype.itemsize for a in (*arguments, *outs))
    return pl.pallas_call(
        kernel,
        name=name,
        out_shape=outs,
        in_specs=[pl.BlockSpec(memory_space=pltpu.SMEM)]
        + [space] * (len(arguments) - remote)
        + [apart] * remote,
        out_specs=[space] * len(outs),
        scratch_shapes=scratch,
        compiler_params=pltpu.CompilerParams(vmem_limit_bytes=limit << 20),
        cost_estimate=pl.CostEstimate(flops=int(flops), bytes_accessed=moved, transcendentals=0),
    )(scalars, *arguments)


def pack(first, second):
    main = first.shape[1] // LANES * LANES
    return jnp.concatenate([first[:, :main], second[:, :main], first[:, main:], second[:, main:]], axis=1)


def unpack(both):
    width = both.shape[1] // 2
    main = width // LANES * LANES
    edge = main * 2 + width - main
    first = jnp.concatenate([both[:, :main], both[:, 2 * main : edge]], axis=1)
    rest = both[:, 2 * main :].astype(F32)[:, width - main :].astype(both.dtype)
    second = jnp.concatenate([both[:, main : 2 * main], rest], axis=1)
    return first, second


def reorder(value, place, n_dp):
    width = value.shape[1]
    lane = lax.broadcasted_iota(jnp.int32, (1, width), 1)
    span = width // n_dp
    bit = 1
    while bit < n_dp:
        low = lax.rem(lane, 2 * span) < span
        other = jnp.where(low, pltpu.roll(value, width - span, 1), pltpu.roll(value, span, 1))
        value = jnp.where((place & bit) != 0, other, value)
        bit, span = 2 * bit, 2 * span
    return value


def row_mean(value):
    return jnp.sum(value, axis=1, keepdims=True) * (1.0 / value.shape[1])


def normalize(value):
    inverse = lax.rsqrt(row_mean(value * value) + EPSILON)
    return value * inverse, inverse


def norm_back(grad_normed, normed, inverse, gain):
    scaled = grad_normed * gain
    return inverse * (scaled - normed * row_mean(scaled * normed))


def load(sources, targets, sem):
    copies = [pltpu.make_async_copy(a, b, sem.at[k]) for k, (a, b) in enumerate(zip(sources, targets))]
    for copy in copies:
        copy.start()
    for copy in copies:
        copy.wait()


def pack_kernel(s, first, second, out, one, two, sem):
    load((first, second), (one, two), sem)
    out[...] = pack(one[...].astype(F32), two[...].astype(F32)).astype(BF16)


def row_of(ref):
    return jnp.concatenate([ref[k : k + 1] for k in range(ref.shape[0])], axis=1)


def prepare_kernel(n_dp, s, scale, *refs):
    sources, (h, x_own, grad, vectors, biases) = refs[:9], refs[9:14]
    x, cotangent, *given = refs[14:23]
    load(sources, refs[14:23], refs[23])
    mine, place, length = s[0], s[1], s[2]
    value = reorder(x[...].astype(F32), mine, n_dp)
    stacked = jnp.concatenate([row_of(given[k]) for k in (0, 1, 2, 3, 4, 5, 6, 6)], axis=0)
    width = biases.shape[1]
    slices = stacked[:, :width]
    for number in range(1, stacked.shape[1] // width):
        slices = jnp.where(place == number, stacked[:, number * width : (number + 1) * width], slices)
    biases[...] = slices
    biases[7:8] = scale[...]
    stacked = reorder(stacked, mine, n_dp)
    normed, _ = normalize(value)
    h[...] = (normed * stacked[0:1]).astype(BF16)
    x_own[...] = value.astype(BF16)
    rows = value.shape[0]
    row = lax.broadcasted_iota(jnp.int32, value.shape, 0) + place * rows
    g = jnp.where(row < length, reorder(cotangent[...].astype(F32), mine, n_dp), 0.0)
    grad[...] = g.astype(BF16)
    vectors[...] = stacked
    vectors[4:5] = jnp.sum(g, axis=0, keepdims=True)


def join(pieces, out):
    rows = pieces[0].shape[0]
    for number, piece in enumerate(pieces):
        out[pl.ds(number * rows, rows)] = piece[...]


def tiles(rows, body, size=128):
    def step(m, carry):
        body(pl.ds(pl.multiple_of(m * size, size), size), m)
        return carry

    lax.fori_loop(0, rows // size, step, 0)


def positions(shape, axis, place, local, offset=0):
    row = lax.broadcasted_iota(jnp.int32, shape, axis) + offset
    shift = local.bit_length() - 1
    block = row >> shift
    turned = ((block & 1) << 1) | (block >> 1)
    return ((place ^ turned) << shift) + (row & (local - 1))


def fetch(even, odd, out, depth, sem):
    copies = []
    if not odd:
        copies.append(pltpu.make_async_copy(even[0], out, sem.at[0]))
    else:
        for start, blocks in enumerate((even, odd)):
            row = start * depth
            for block in blocks:
                for k in range(block.shape[0] // depth):
                    source, target = block.at[pl.ds(k * depth, depth)], out.at[pl.ds(row, depth)]
                    copies.append(pltpu.make_async_copy(source, target, sem.at[len(copies)]))
                    row += 2 * depth
    for one in copies:
        one.start()
    return copies


def stack_kernel(s, *refs):
    join(refs[:-1], refs[-1])


def of_head(value, number, head_size):
    lanes = lax.broadcasted_iota(jnp.int32, (1, value.shape[1]), 1) // head_size
    return jnp.where(lanes == number, value, jnp.zeros((), value.dtype))


def attend_kernel(counts, depth, head_size, s, p0, p1, p2, p3, biases, *refs):
    even, odd = refs[: counts[0]], refs[counts[0] : counts[1]]
    q_raw, q_low, k_low, h, weight, turned, sem = refs[counts[1] :]
    copies = fetch(even, odd, weight, depth, sem)
    join((p0, p1, p2, p3), h)
    for copy in copies:
        copy.wait()
    first, second = unpack(dot(h[...], weight[...]))
    first = first + biases[4:5]
    q_raw[...] = first
    q_low[...] = (first * biases[7:8]).astype(BF16)
    k_low[...] = second.astype(BF16)
    place, length = s[1], s[2]
    rows, local = q_low.shape[0], p0.shape[0]
    key_place = positions((rows, 1), 0, place, local)
    last = jnp.minimum(positions((1, rows), 1, place, local), length - 1)

    def head(number, carry):
        score = dot(k_low[...], of_head(q_low[...], number, head_size), NT)
        score = jnp.where(key_place <= last, score, -1e30)
        raised = jnp.exp(score - jnp.max(score, axis=0, keepdims=True))
        share = 1.0 / jnp.sum(raised, axis=0, keepdims=True)
        turned[number] = (raised * share).astype(BF16)
        return carry

    for number in range(turned.shape[0]):
        head(number, 0)


def mixed_heads(turned, value, head_size, dims):
    total = None
    for number in range(turned.shape[0]):
        term = dot(turned[number], of_head(value, number, head_size), dims)
        total = term if total is None else total + term
    return total


def split_weight(weight, one, two):
    one[...], two[...] = unpack(weight[...])


def context_kernel(counts, depth, head_size, s, h, turned, biases, *refs):
    even, odd = refs[: counts[0]], refs[counts[0] : counts[1]]
    v_low, context, far, near, w_value, w_output, weight, sem = refs[counts[1] :]
    for copy in fetch(even, odd, weight, depth, sem):
        copy.wait()
    split_weight(weight, w_value, w_output)
    v_low[...] = (dot(h[...], w_value[...]) + biases[5:6]).astype(BF16)
    context[...] = mixed_heads(turned, v_low[...], head_size, TN).astype(BF16)
    split_product(context, w_output, far, near)


def split_product(left, right, far, near, extra=None, along=None):
    half, total = near.shape[0], None
    for start, out in ((half, far), (0, near)):
        at = pl.ds(start, half)
        value = dot(left[at], right[...], NT)
        if extra is not None:
            value = value + dot(extra[0][at], extra[1][...], NT)
        out[...] = value.astype(out.dtype)
        if along is not None:
            summed = jnp.sum(value * along[at].astype(F32), axis=0, keepdims=True)
            total = summed if total is None else total + summed
    return total


def middle_kernel(s, near, got, send, keep):
    rows = send.shape[0]
    send[...] = (near[rows:] + got[rows:].astype(F32)).astype(BF16)
    keep[...] = near[:rows] + got[:rows].astype(F32)


def second_norm_kernel(s, keep, got, x_own, vectors, x_one, h):
    value = x_own[...].astype(F32) + keep[...] + got[...].astype(F32) + vectors[2:3]
    x_one[...] = value
    normed, _ = normalize(value)
    h[...] = (normed * vectors[1:2]).astype(BF16)


def grad_act_kernel(counts, depth, s, p0, p1, p2, p3, *refs):
    even, odd = refs[: counts[0]], refs[counts[0] : counts[1]]
    grad_act, g, w_hidden, w_down, weight, sem = refs[counts[1] :]
    copies = fetch(even, odd, weight, depth, sem)
    join((p0, p1, p2, p3), g)
    for copy in copies:
        copy.wait()
    split_weight(weight, w_hidden, w_down)
    grad_act[...] = dot(g[...], w_down[...])


def hidden_kernel(s, p0, p1, p2, p3, w_hidden, biases, grad_act, out_far, out_near, act, grad_pre, h):
    join((p0, p1, p2, p3), h)
    pre = dot(h[...], w_hidden[...]) + biases[6:7]
    sigma = jax.nn.sigmoid(pre)
    act[...] = (pre * sigma).astype(BF16)
    grad_pre[...] = (grad_act[...] * (sigma * (1.0 + pre * (1.0 - sigma)))).astype(BF16)
    split_product(grad_pre, w_hidden, out_far, out_near)


def spread_terms(term, keep, sends, depth, order):
    if not sends:
        keep[...] = term[...]
        return
    half = len(order) // len(sends)
    for at, j in enumerate(order):
        keep[pl.ds(at * depth, depth)] = term[pl.ds(2 * j * depth, depth)]
        sends[at // half][pl.ds(at % half * depth, depth)] = term[pl.ds((2 * j + 1) * depth, depth)]


def two_terms(left_one, right_one, left_two, right_two, term):
    first = dot(left_one[...], right_one[...], TN)
    second = dot(left_two[...], right_two[...], TN)
    term[...] = pack(first, second).astype(BF16)


def down_kernel(depth, order, s, h, g, act, grad_pre, w_down, far, near, b_hidden, keep, *refs):
    *sends, term = refs
    two_terms(h, grad_pre, g, act, term)
    spread_terms(term, keep, sends, depth, order)
    b_hidden[...] = jnp.sum(grad_pre[...].astype(F32), axis=0, keepdims=True)
    split_product(act, w_down, far, near)


def pair_kernel(start, count, s, own, *refs):
    gots, outs = refs[:count], refs[count:]
    row = 0
    for out in outs:
        rows = out.shape[0]
        value = own[pl.ds(start + row, rows)].astype(F32)
        for got in gots:
            value = value + got[pl.ds(row, rows)].astype(F32)
        out[...] = value.astype(out.dtype)
        row += rows


def owned_kernel(n_got, s, keep, *refs):
    total = keep[...]
    for got in refs[:n_got]:
        total = total + got[pl.ds(0, total.shape[0])].astype(F32)
    refs[n_got][...], refs[n_got + 1][...] = unpack(total)


def grad_middle_kernel(s, keep, got, x_one, grad, vectors, grad_low, grad_full, sums):
    normed, inverse = normalize(x_one[...])
    grad_h = keep[...] + got[...].astype(F32)
    full = grad[...].astype(F32) + norm_back(grad_h, normed, inverse, vectors[1:2])
    grad_full[...] = full
    grad_low[...] = full.astype(BF16)
    sums[...] = vectors[...]
    sums[5:6] = jnp.sum(full, axis=0, keepdims=True)
    sums[6:7] = jnp.sum(grad_h * normed, axis=0, keepdims=True)


def grad_context_kernel(depth, order, head_size, s, p0, p1, p2, p3, w_output, turned, context, h, *refs):
    grad_context, grad_value, gm, keep, *sends, term = refs
    join((p0, p1, p2, p3), gm)
    grad_context[...] = dot(gm[...], w_output[...]).astype(BF16)
    grad_value[...] = mixed_heads(turned, grad_context[...], head_size, NN).astype(BF16)
    two_terms(h, grad_value, gm, context, term)
    spread_terms(term, keep, sends, depth, order)


def grad_scores_kernel(head_size, s, turned, grad_context, v_low, q_low, k_low, q_raw, biases, *refs):
    grad_qk, sums, grad_q, grad_k, scores = refs
    rows = q_low.shape[0]
    grad_q[...] = jnp.zeros_like(grad_q)
    grad_k[...] = jnp.zeros_like(grad_k)

    def head(number, carry):
        grad_chance = dot(v_low[...], of_head(grad_context[...], number, head_size), NT)
        chance = turned[number].astype(F32)
        product = chance * grad_chance
        center = jnp.sum(product, axis=0, keepdims=True)
        scores[...] = (product - chance * center).astype(BF16)
        grad_q[...] += dot(scores[...], of_head(k_low[...], number, head_size), TN)
        grad_k[...] += dot(scores[...], of_head(q_low[...], number, head_size))
        return carry

    for number in range(turned.shape[0]):
        head(number, 0)
    low = grad_q[...].astype(BF16).astype(F32)
    sums[0:1] = jnp.sum(low * q_raw[...], axis=0, keepdims=True)
    low = (low * biases[7:8]).astype(BF16).astype(F32)
    grad_qk[...] = pack(low, grad_k[...]).astype(BF16)
    sums[1:2] = jnp.sum(low, axis=0, keepdims=True)


def grad_first_kernel(
    n_dp, depth, order, s, grad_qk, w_qk, grad_value, w_value, h, sums_in, sums_q, b_hidden, slope, *refs
):
    far, near, sums, keep, *sends, term = refs
    term[...] = dot(h[...], grad_qk[...], TN).astype(BF16)
    spread_terms(term, keep, sends, depth, order)
    mine, place = s[0], s[1]
    gained = split_product(grad_qk, w_qk, far, near, (grad_value, w_value), h) / sums_in[0:1]
    row = lax.broadcasted_iota(jnp.int32, sums.shape, 0)
    sums[...] = reorder(jnp.where(row == 7, gained, sums_in[...]), mine, n_dp)
    sums[0:4] = jnp.zeros((4, sums.shape[1]), F32)
    local_width, head_size = sums_q.shape[1], slope.shape[1]
    b_value = jnp.sum(grad_value[...].astype(F32), axis=0, keepdims=True)
    share = jnp.concatenate([sums_q[1:2], b_value, b_hidden[...]], axis=0)
    for number in range(sums.shape[1] // local_width):

        @pl.when(place == number)
        def _():
            sums[0:3, number * local_width : (number + 1) * local_width] = share

    scale = sums_q[0:1]
    total = scale[:, :head_size]
    for number in range(1, local_width // head_size):
        total = total + scale[:, number * head_size : (number + 1) * head_size]
    sums[3:4, :head_size] = total * slope[...]
    if sends:
        sends[0][pl.ds(sends[0].shape[0] - 16, 16)] = fold(sums[...])


def fold(vectors):
    half = vectors.shape[1] // 2
    return jnp.concatenate([vectors[:, :half], vectors[:, half:]], axis=0).astype(BF16)


def unfold(rows):
    return jnp.concatenate([rows[:8], rows[8:]], axis=1)


def pair_first_kernel(depth, s, own, got, vectors, one, two, small):
    last = got.shape[0] - 16
    low = fold(vectors[...]).astype(F32) + got[pl.ds(last, 16)].astype(F32)
    low = low.astype(BF16)
    small[...] = low
    for row, out in ((0, one), (depth, two)):
        value = own[pl.ds(row, depth)].astype(F32) + got[pl.ds(row, depth)].astype(F32)
        out[pl.ds(0, depth)] = value.astype(BF16)
        out[pl.ds(depth, 16)] = low


def pair_last_kernel(depth, start, s, own, got, small, out, zero):
    value = own[pl.ds(start, 2 * depth)].astype(F32) + got[...].astype(F32)
    out[pl.ds(0, depth)] = value[:depth].astype(BF16)
    out[pl.ds(depth, 16)] = small[...]
    zero[...] = value[depth:]


def vector_far_kernel(depth, s, three, two, out):
    at = pl.ds(depth, 16)
    out[...] = two[at].astype(F32) + three[at].astype(F32)


def vector_kernel(depth, s, small, far, one, out):
    near = small[...].astype(F32) + one[pl.ds(depth, 16)].astype(F32)
    out[...] = unfold(near + far[...])


def total_kernel(s, one, two, *outs):
    total = one[...] + two[...]
    for out, row in zip(outs[:7], (0, 1, 2, 6, 4, 5, 7)):
        for k in range(out.shape[0]):
            out[k : k + 1] = total[row : row + 1, k * LANES : (k + 1) * LANES]
    outs[7][...] = total[3:4, : outs[7].shape[1]]


def last_kernel(n_dp, s, keep, got, x_own, grad_full, sums_in, grad_in):
    normed, inverse = normalize(x_own[...].astype(F32))
    grad_h = keep[...] + got[...].astype(F32)
    full = grad_full[...] + norm_back(grad_h, normed, inverse, sums_in[0:1])
    grad_in[...] = reorder(full, s[0], n_dp).astype(BF16)


def add_kernel(s, one, two, out):
    out[...] = one[...] + two[...]


def output_kernel(n_dp, s, keep, got, x_one, vectors, out):
    value = x_one[...] + keep[...] + got[...].astype(F32) + vectors[3:4]
    out[...] = reorder(value, s[0], n_dp).astype(BF16)


def tie(*values):
    return lax.optimization_barrier(values)


class Links:
    def __init__(self, n_dp, n_tensor):
        self.n_dp, self.n_tensor = n_dp, n_tensor
        self.wide = n_dp > 8

    def move(self, value, target):
        pairs = []
        for d in range(self.n_dp):
            for t in range(self.n_tensor):
                to_d, to_t = target(d, t)
                pairs.append((d * self.n_tensor + t, to_d * self.n_tensor + to_t))
        return lax.ppermute(value, AXES, pairs)

    def chip(self, value):
        return self.move(value, lambda d, t: (d, t ^ 2))

    def core(self, value):
        return self.move(value, lambda d, t: (d, t ^ 1))

    def pair(self, value):
        return self.along(value, 1)

    def along(self, value, bits):
        return self.move(value, lambda d, t: (d ^ bits, t))

    def gather_tensor(self, rows):
        near = self.chip(rows)
        return rows, near, self.core(rows), self.core(near)

    def gather_wide(self, shard):
        blocks, place = lax.all_gather(shard, "dp", axis=0), lax.axis_index("dp")
        return jnp.take(blocks, lax.iota(jnp.int32, self.n_dp) ^ place, axis=0).reshape(-1, shard.shape[1])

    def scatter_wide(self, total):
        place = lax.axis_index("dp")
        blocks = total.reshape(self.n_dp, total.shape[0] // self.n_dp, total.shape[1])
        blocks = jnp.take(blocks, lax.iota(jnp.int32, self.n_dp) ^ place, axis=0).astype(F32)
        return unpack(lax.psum_scatter(blocks.reshape(total.shape), "dp", scatter_dimension=0, tiled=True))

    def steps(self):
        found, bit = [], 1
        while bit < self.n_dp and self.wide:
            found.append(lambda d, t, bit=bit: (d ^ bit, t))
            bit *= 2
        return found + [lambda d, t: (d, t ^ 1), lambda d, t: (d, t ^ 2)]


def body(
    inputs,
    weight_query,
    weight_key,
    weight_value,
    weight_output,
    weight_hidden,
    weight_down,
    bias_query,
    bias_value,
    bias_hidden,
    bias_output,
    bias_final,
    gain_attention,
    gain_mixer,
    query_scale,
    lengths,
    cotangent,
    n_dp,
    n_tensor,
):
    links = Links(n_dp, n_tensor)
    wide = links.wide
    local_rows, width = inputs.shape
    all_rows = local_rows * n_tensor
    depth = width // n_dp
    local_width = weight_query.shape[1]
    both = 2 * local_width
    head_size = query_scale.shape[0]
    heads = local_width // head_size
    dp_index = lax.axis_index("dp")
    tensor_index = lax.axis_index("tensor")
    s = jnp.stack([dp_index, tensor_index, lengths[0]])
    product = 2 * all_rows * width * local_width
    mixed = 2 * all_rows * all_rows * local_width

    def run(name, kernel, outs, *arguments, **rest):
        return call(name, kernel, [shaped(*o) for o in outs], s, *arguments, **rest)

    def bind(kernel, *fixed):
        def bound(*refs):
            return kernel(*fixed, *refs)

        return bound

    packed = [((depth, both), BF16)]
    rows_low, rows_full = ((local_rows, width), BF16), ((local_rows, width), F32)
    split = [((all_rows // 2, width), BF16), ((all_rows // 2, width), F32)]
    part = ((all_rows, local_width), BF16)
    part_full = ((all_rows, local_width), F32)
    whole_rows = ((all_rows, width), BF16)
    weight = ((width, local_width), BF16)
    vector = ((8, width), F32)
    halves = [((width // 2, both), BF16)] * 2
    term = [pltpu.VMEM((width, both), BF16)]
    sems = [pltpu.SemaphoreType.DMA((n_dp,))]

    unit = SOFTPLUS_UNIT / jnp.sqrt(F32(head_size))
    scale_wide = jnp.tile(jax.nn.softplus(query_scale) * unit, heads)[None]
    slope = (jax.nn.sigmoid(query_scale) * unit)[None]
    loads = [pltpu.VMEM((depth, local_width), BF16)] * 2 + [pltpu.SemaphoreType.DMA((2,))]

    def apart(value):
        return pltpu.with_memory_space_constraint(value, pltpu.HBM)

    def pack_two(name, one, two):
        return run("pack_" + name, pack_kernel, packed, apart(one), apart(two), remote=2, scratch=loads)[0]

    own_qk = pack_two("qk", weight_query, weight_key)
    given = (gain_attention, gain_mixer, bias_output, bias_final, bias_query, bias_value, bias_hidden)
    scale_wide, slope = tie(scale_wide, slope)
    tall = (width // LANES, LANES)
    h_own, x_own, grad_own, vectors, biases = run(
        "prepare",
        bind(prepare_kernel, n_dp),
        [rows_low, rows_low, rows_low, vector, ((8, local_width), F32)],
        scale_wide,
        *(apart(v) for v in (inputs, cotangent, *(v.reshape(tall) for v in given))),
        remote=9,
        scratch=[pltpu.VMEM((local_rows, width), BF16)] * 2
        + [pltpu.VMEM(tall, F32)] * 7
        + [pltpu.SemaphoreType.DMA((9,))],
    )
    own_vo = pack_two("vo", weight_value, weight_output.T)
    own_hd = pack_two("hd", weight_hidden, weight_down.T)
    order = (3, 2, 1, 0)

    def stack(*blocks):
        rows = sum(block.shape[0] for block in blocks)
        return run("stack", stack_kernel, [((rows, both), BF16)], *blocks)[0]

    if wide:
        qk, vo, hd = (([links.gather_wide(own)], []) for own in (own_qk, own_vo, own_hd))
        h_one, grad_rows = links.gather_tensor(h_own), links.gather_tensor(grad_own)
    else:
        qk_one, qk_two = links.along(own_qk, 2), links.along(own_qk, 4)
        h_own, own_vo, own_hd, qk_one, qk_two = tie(h_own, own_vo, own_hd, qk_one, qk_two)
        h_chip = links.chip(h_own)
        qk_three = links.along(qk_one, 4)
        near_qk_pair = links.pair(stack(own_qk, qk_one))
        own_vo, qk_three = tie(own_vo, qk_three)
        far_stack = stack(qk_two, qk_three)
        far_stack, near_qk_pair, h_chip = tie(far_stack, near_qk_pair, h_chip)
        h_one = h_own, h_chip, links.core(h_own), links.core(h_chip)
        far_qk_pair = links.pair(far_stack)
        vo_one, vo_two = links.along(own_vo, 2), links.along(own_vo, 4)
        qk = [own_qk, qk_one, qk_two, qk_three], [near_qk_pair, far_qk_pair]
        h_one, qk, vo_one, vo_two = tie(h_one, qk, vo_one, vo_two)
        near_vo_pair = links.pair(stack(own_vo, vo_one))
        vo_three = links.along(vo_one, 4)
        hd_one = links.along(own_hd, 2)
        grad_chip = links.chip(grad_own)
    n_qk = len(qk[0]), len(qk[0]) + len(qk[1])
    q_raw, q_low, k_low, h_all, w_qk, turned = run(
        "attend",
        bind(attend_kernel, n_qk, depth, head_size),
        [
            part_full,
            part,
            part,
            whole_rows,
            ((width, both), BF16),
            ((heads, all_rows, all_rows), BF16),
        ],
        *h_one,
        biases,
        *qk[0],
        *qk[1],
        remote=n_qk[1],
        scratch=sems,
    )
    if not wide:
        turned, near_vo_pair, vo_three, hd_one, grad_chip = tie(
            turned, near_vo_pair, vo_three, hd_one, grad_chip
        )
        far_vo_pair = links.pair(stack(vo_two, vo_three))
        hd_two = links.along(own_hd, 4)
        grad_rows = grad_own, grad_chip, links.core(grad_own), links.core(grad_chip)
        vo = [own_vo, vo_one, vo_two, vo_three], [near_vo_pair, far_vo_pair]
        grad_rows, own_hd, hd_one, hd_two = tie(grad_rows, own_hd, hd_one, hd_two)
        near_hd_pair = links.pair(stack(own_hd, hd_one))
        hd_three = links.along(hd_one, 4)
        turned, vo, grad_rows = tie(turned, vo, grad_rows)
    n_vo = len(vo[0]), len(vo[0]) + len(vo[1])
    v_low, context, far, near, w_value, w_output = run(
        "context",
        bind(context_kernel, n_vo, depth, head_size),
        [part, part, *split, weight, weight],
        h_all,
        turned,
        biases,
        *vo[0],
        *vo[1],
        remote=n_vo[1],
        scratch=term + sems,
    )

    def core_half(far, near):
        return run("middle", middle_kernel, [rows_low, rows_full], near, links.core(far))

    if not wide:
        far, hd_three, near_hd_pair = tie(far, hd_three, near_hd_pair)
    send, keep = core_half(far, near)
    got = links.chip(send)
    if not wide:
        far_hd_pair = links.pair(stack(hd_two, hd_three))
        hd = [own_hd, hd_one, hd_two, hd_three], [near_hd_pair, far_hd_pair]
        got, hd = tie(got, hd)
    n_hd = len(hd[0]), len(hd[0]) + len(hd[1])
    x_one, h_two_own = run("second_norm", second_norm_kernel, [rows_full, rows_low], keep, got, x_own, vectors)
    h_two = links.gather_tensor(h_two_own)
    grad_act, grad_all, w_hidden, w_down = run(
        "grad_act",
        bind(grad_act_kernel, n_hd, depth),
        [part_full, whole_rows, weight, weight],
        *grad_rows,
        *hd[0],
        *hd[1],
        remote=n_hd[1],
        scratch=term + sems,
    )
    far, near, act, grad_pre, h_two_all = run(
        "hidden",
        hidden_kernel,
        [*split, part, part, whole_rows],
        *h_two,
        w_hidden,
        biases,
        grad_act,
    )
    send, keep = core_half(far, near)
    act, send = tie(act, send)
    got = links.chip(send)
    half = ((n_dp // 4 * depth, both), BF16)
    ridden = ((depth + 16, both), BF16)
    terms = [((width, both), BF16)] if wide else [((n_dp // 2 * depth, both), BF16), half, half]
    far, near, grad_b_hidden, *terms_hd = run(
        "down",
        bind(down_kernel, depth, order),
        [*split, ((1, local_width), F32), *terms],
        h_two_all,
        grad_all,
        act,
        grad_pre,
        w_down,
        scratch=term,
    )
    got, terms_hd = tie(got, terms_hd)

    def pair_sum(name, start, outs, own, *gots):
        return run("pair_" + name, bind(pair_kernel, start, len(gots)), outs, own, *gots)

    def owned(name, *parts):
        outs = [((depth, local_width), F32)] * 2
        return run("owned_" + name, bind(owned_kernel, len(parts) - 1), outs, *parts)

    def first_far(name, terms, got):
        return pair_sum(name + "_a", 0, [half], terms[0], got)[0]

    def then_near(name, terms, got_pair, got_far):
        outs = packed + [((depth, both), F32)]
        sent, zero = pair_sum(name + "_b", half[0][0], outs, terms[0], got_pair, got_far)
        return zero, links.along(sent, 2)

    sent_hd = [links.pair(part) for part in terms_hd[1:]]
    grad_mid_low, grad_mid, sums = run(
        "grad_middle",
        grad_middle_kernel,
        [rows_low, rows_full, vector],
        keep,
        got,
        x_one,
        grad_own,
        vectors,
    )
    if wide:
        grad_mid_rows = links.gather_tensor(grad_mid_low)
    else:
        grad_mid_chip = links.chip(grad_mid_low)
        grad_mid_chip, sent_hd[0] = tie(grad_mid_chip, sent_hd[0])
        far_sum = links.along(first_far("hd", terms_hd, sent_hd[0]), 4)
        grad_mid_rows = grad_mid_low, grad_mid_chip, links.core(grad_mid_low), links.core(grad_mid_chip)
    grad_mid_rows, far = tie(grad_mid_rows, far)
    mix_send, mix_keep = core_half(far, near)
    mix_got = links.chip(mix_send)
    grad_context, grad_value, _, *terms_vo = run(
        "grad_context",
        bind(grad_context_kernel, depth, order, head_size),
        [part, part, whole_rows, *terms],
        *grad_mid_rows,
        w_output,
        turned,
        context,
        h_all,
        scratch=term,
    )
    grad_context, sent_hd[1:] = tie(grad_context, sent_hd[1:])
    sent_vo = [links.pair(part) for part in terms_vo[1:2]]
    grad_qk, sums_q = run(
        "grad_scores",
        bind(grad_scores_kernel, head_size),
        [((all_rows, both), BF16), ((8, local_width), F32)],
        turned,
        grad_context,
        v_low,
        q_low,
        k_low,
        q_raw,
        biases,
        scratch=[
            pltpu.VMEM((all_rows, local_width), F32),
            pltpu.VMEM((all_rows, local_width), F32),
            pltpu.VMEM((all_rows, all_rows), BF16),
        ],
    )
    if wide:
        grad_qk, mix_got = tie(grad_qk, mix_got)
    else:
        grad_qk, sent_vo[0], mix_got, far_sum = tie(grad_qk, sent_vo[0], mix_got, far_sum)
        zero_hd, part_hd = then_near("hd", terms_hd, sent_hd[1], far_sum)
        sent = first_far("vo", terms_vo, sent_vo[0])
        grad_qk, zero_hd, sent = tie(grad_qk, zero_hd, sent)
        far_sum = links.along(sent, 4)
    terms_first = list(terms)
    if not wide:
        terms_first[1] = ((half[0][0] + 16, both), BF16)
    far, near, sums, *terms_qk = run(
        "grad_first",
        bind(grad_first_kernel, n_dp, depth, order),
        [*split, vector, *terms_first],
        grad_qk,
        w_qk,
        grad_value,
        w_value,
        h_all,
        sums,
        sums_q,
        grad_b_hidden,
        slope,
        scratch=term,
    )
    def exchange(value, step):
        return run("add", add_kernel, [vector], value, links.move(value, step))[0]

    if not wide:
        far, sent_qk = tie(far, terms_qk[1:])
        sent_qk = [links.pair(part) for part in sent_qk]
        sent_qk[0], last_vo = tie(sent_qk[0], terms_vo[2])
        sent_vo.append(links.pair(last_vo))
    send, keep = core_half(far, near)
    got = links.chip(send)
    if wide:
        total = sums
    else:
        got, sent_qk[0] = tie(got, sent_qk[0])
        one, two, small = run(
            "pair_qk_a",
            bind(pair_first_kernel, depth),
            [ridden, ridden, ((16, both), BF16)],
            terms_qk[0],
            sent_qk[0],
            sums,
        )
        got, one, two = tie(got, one, two)
        three, two = links.along(one, 6), links.along(two, 4)
    (grad_in,) = run("last", bind(last_kernel, n_dp), [rows_low], keep, got, x_own, grad_mid, vectors)
    if not wide:
        grad_in, sent_qk[1] = tie(grad_in, sent_qk[1])
        one, zero_qk = run(
            "pair_qk_b",
            bind(pair_last_kernel, depth, half[0][0]),
            [ridden, ((depth, both), F32)],
            terms_qk[0],
            sent_qk[1],
            small,
        )
        one = links.along(one, 2)
        zero_qk, far_sum = tie(zero_qk, far_sum)
        zero_vo, part_vo = then_near("vo", terms_vo, sent_vo[1], far_sum)
        mix_got, zero_vo = tie(mix_got, zero_vo)
    (output,) = run("output", bind(output_kernel, n_dp), [rows_low], mix_keep, mix_got, x_one, vectors)
    if not wide:
        part_hd, output = tie(part_hd, output)
        grad_hidden, grad_down = owned("hd", zero_hd, part_hd)
        three, two, grad_hidden = tie(three, two, grad_hidden)
        (far_rows,) = run("vector_a", bind(vector_far_kernel, depth), [((16, both), F32)], three, two)
        (total,) = run("vector_b", bind(vector_kernel, depth), [vector], small, far_rows, one)
    steps = links.steps()
    for step in steps[:-1]:
        total = exchange(total, step)
    if not wide:
        total, zero_qk = tie(total, zero_qk)
    moved = links.move(total, steps[-1])
    tall_vector = (tall, F32)
    *totals, total_scale = run(
        "total", total_kernel, [tall_vector] * 7 + [((1, head_size), F32)], total, moved
    )
    totals = [v.reshape(width) for v in totals]
    if wide:
        grad_hidden, grad_down = links.scatter_wide(terms_hd[0])
        grad_output_v, grad_output_o = links.scatter_wide(terms_vo[0])
        grad_query, grad_key = links.scatter_wide(terms_qk[0])
    else:
        grad_output_v, grad_output_o = owned("vo", zero_vo, part_vo)
        grad_query, grad_key = owned("qk", zero_qk, three, two, one)
    return (
        output,
        grad_in,
        grad_query,
        grad_key,
        grad_output_v,
        grad_output_o.T,
        grad_hidden,
        grad_down.T,
        totals[0],
        totals[1],
        totals[2],
        totals[5],
        totals[4],
        totals[6],
        totals[3],
        total_scale.reshape(head_size),
    )


def solution(mesh):
    n_dp, n_tensor = mesh.shape["dp"], mesh.shape["tensor"]

    def local(*arguments):
        return body(*arguments, n_dp, n_tensor)

    rows = P(("dp", "tensor"), None)
    into, out_of = P("dp", "tensor"), P("tensor", "dp")
    return jax.shard_map(
        local,
        mesh=mesh,
        in_specs=(rows, into, into, into, out_of, into, out_of, *[P()] * 8, P("dp"), rows),
        out_specs=(rows, rows, into, into, into, out_of, into, out_of, *[P()] * 8),
        check_vma=False,
    )
```

```python
import jax
import jax.numpy as jnp
from jax import lax
from jax.experimental import pallas as pl
from jax.experimental.pallas import tpu as pltpu
from jax.sharding import PartitionSpec as P

EPSILON = 1e-06
SOFTPLUS_UNIT = 1.442695041
AXES = ("dp", "tensor")
F32 = jnp.float32
BF16 = jnp.bfloat16
LANES = 128
TENSOR_ORDER = (0, 2, 1, 3)
NN, NT, TN = ((1,), (0,)), ((1,), (1,)), ((0,), (0,))


def dot(left, right, dims=NN):
    return lax.dot_general(left, right, (dims, ((), ())), preferred_element_type=F32)


def shaped(shape, kind):
    return jax.ShapeDtypeStruct(shape, kind)


def call(name, kernel, outs, scalars, *arguments, flops=1e6, scratch=(), limit=12, remote=0):
    space = pl.BlockSpec(memory_space=pltpu.VMEM)
    apart = pl.BlockSpec(memory_space=pltpu.HBM)
    moved = sum(a.size * a.dtype.itemsize for a in (*arguments, *outs))
    return pl.pallas_call(
        kernel,
        name=name,
        out_shape=outs,
        in_specs=[pl.BlockSpec(memory_space=pltpu.SMEM)]
        + [space] * (len(arguments) - remote)
        + [apart] * remote,
        out_specs=[space] * len(outs),
        scratch_shapes=scratch,
        compiler_params=pltpu.CompilerParams(vmem_limit_bytes=limit << 20),
        cost_estimate=pl.CostEstimate(flops=int(flops), bytes_accessed=moved, transcendentals=0),
    )(scalars, *arguments)


def pack(first, second):
    main = first.shape[1] // LANES * LANES
    return jnp.concatenate([first[:, :main], second[:, :main], first[:, main:], second[:, main:]], axis=1)


def unpack(both):
    width = both.shape[1] // 2
    main = width // LANES * LANES
    edge = main * 2 + width - main
    first = jnp.concatenate([both[:, :main], both[:, 2 * main : edge]], axis=1)
    rest = both[:, 2 * main :].astype(F32)[:, width - main :].astype(both.dtype)
    second = jnp.concatenate([both[:, main : 2 * main], rest], axis=1)
    return first, second


def reorder(value, place, n_dp):
    width = value.shape[1]
    lane = lax.broadcasted_iota(jnp.int32, (1, width), 1)
    span = width // n_dp
    bit = 1
    while bit < n_dp:
        low = lax.rem(lane, 2 * span) < span
        other = jnp.where(low, pltpu.roll(value, width - span, 1), pltpu.roll(value, span, 1))
        value = jnp.where((place & bit) != 0, other, value)
        bit, span = 2 * bit, 2 * span
    return value


def row_mean(value):
    return jnp.sum(value, axis=1, keepdims=True) * (1.0 / value.shape[1])


def normalize(value):
    inverse = lax.rsqrt(row_mean(value * value) + EPSILON)
    return value * inverse, inverse


def norm_back(grad_normed, normed, inverse, gain):
    scaled = grad_normed * gain
    return inverse * (scaled - normed * row_mean(scaled * normed))


def load(sources, targets, sem):
    copies = [pltpu.make_async_copy(a, b, sem.at[k]) for k, (a, b) in enumerate(zip(sources, targets))]
    for copy in copies:
        copy.start()
    for copy in copies:
        copy.wait()


def pack_kernel(s, first, second, out, one, two, sem):
    load((first, second), (one, two), sem)
    out[...] = pack(one[...].astype(F32), two[...].astype(F32)).astype(BF16)


def row_of(ref):
    return jnp.concatenate([ref[k : k + 1] for k in range(ref.shape[0])], axis=1)


def prepare_kernel(n_dp, s, scale, *refs):
    sources, (h, x_own, grad, vectors, biases) = refs[:9], refs[9:14]
    x, cotangent, *given = refs[14:23]
    load(sources, refs[14:23], refs[23])
    mine, place, length = s[0], s[1], s[2]
    value = reorder(x[...].astype(F32), mine, n_dp)
    stacked = jnp.concatenate([row_of(given[k]) for k in (0, 1, 2, 3, 4, 5, 6, 6)], axis=0)
    width = biases.shape[1]
    slices = stacked[:, :width]
    for number in range(1, stacked.shape[1] // width):
        slices = jnp.where(place == number, stacked[:, number * width : (number + 1) * width], slices)
    biases[...] = slices
    biases[7:8] = scale[...]
    stacked = reorder(stacked, mine, n_dp)
    normed, _ = normalize(value)
    h[...] = (normed * stacked[0:1]).astype(BF16)
    x_own[...] = value.astype(BF16)
    rows = value.shape[0]
    row = lax.broadcasted_iota(jnp.int32, value.shape, 0) + place * rows
    g = jnp.where(row < length, reorder(cotangent[...].astype(F32), mine, n_dp), 0.0)
    grad[...] = g.astype(BF16)
    vectors[...] = stacked
    vectors[4:5] = jnp.sum(g, axis=0, keepdims=True)


def join(pieces, out):
    rows = pieces[0].shape[0]
    for number, piece in enumerate(pieces):
        out[pl.ds(number * rows, rows)] = piece[...]


def tiles(rows, body, size=128):
    def step(m, carry):
        body(pl.ds(pl.multiple_of(m * size, size), size), m)
        return carry

    lax.fori_loop(0, rows // size, step, 0)


def positions(shape, axis, place, local, offset=0):
    row = lax.broadcasted_iota(jnp.int32, shape, axis) + offset
    shift = local.bit_length() - 1
    block = row >> shift
    turned = ((block & 1) << 1) | (block >> 1)
    return ((place ^ turned) << shift) + (row & (local - 1))


def fetch(even, odd, out, depth, sem):
    copies = []
    if not odd:
        copies.append(pltpu.make_async_copy(even[0], out, sem.at[0]))
    else:
        for start, blocks in enumerate((even, odd)):
            row = start * depth
            for block in blocks:
                for k in range(block.shape[0] // depth):
                    source, target = block.at[pl.ds(k * depth, depth)], out.at[pl.ds(row, depth)]
                    copies.append(pltpu.make_async_copy(source, target, sem.at[len(copies)]))
                    row += 2 * depth
    for one in copies:
        one.start()
    return copies


def stack_kernel(s, *refs):
    join(refs[:-1], refs[-1])


def of_head(value, number, head_size):
    lanes = lax.broadcasted_iota(jnp.int32, (1, value.shape[1]), 1) // head_size
    return jnp.where(lanes == number, value, jnp.zeros((), value.dtype))


def attend_kernel(counts, depth, head_size, s, p0, p1, p2, p3, biases, *refs):
    even, odd = refs[: counts[0]], refs[counts[0] : counts[1]]
    q_raw, q_low, k_low, h, weight, turned, sem = refs[counts[1] :]
    copies = fetch(even, odd, weight, depth, sem)
    join((p0, p1, p2, p3), h)
    for copy in copies:
        copy.wait()
    first, second = unpack(dot(h[...], weight[...]))
    first = first + biases[4:5]
    q_raw[...] = first
    q_low[...] = (first * biases[7:8]).astype(BF16)
    k_low[...] = second.astype(BF16)
    place, length = s[1], s[2]
    rows, local = q_low.shape[0], p0.shape[0]
    key_place = positions((rows, 1), 0, place, local)
    last = jnp.minimum(positions((1, rows), 1, place, local), length - 1)

    def head(number, carry):
        score = dot(k_low[...], of_head(q_low[...], number, head_size), NT)
        score = jnp.where(key_place <= last, score, -1e30)
        raised = jnp.exp(score - jnp.max(score, axis=0, keepdims=True))
        share = 1.0 / jnp.sum(raised, axis=0, keepdims=True)
        turned[number] = (raised * share).astype(BF16)
        return carry

    for number in range(turned.shape[0]):
        head(number, 0)


def mixed_heads(turned, value, head_size, dims):
    total = None
    for number in range(turned.shape[0]):
        term = dot(turned[number], of_head(value, number, head_size), dims)
        total = term if total is None else total + term
    return total


def split_weight(weight, one, two):
    one[...], two[...] = unpack(weight[...])


def context_kernel(counts, depth, head_size, s, h, turned, biases, *refs):
    even, odd = refs[: counts[0]], refs[counts[0] : counts[1]]
    v_low, context, far, near, w_value, w_output, weight, sem = refs[counts[1] :]
    for copy in fetch(even, odd, weight, depth, sem):
        copy.wait()
    split_weight(weight, w_value, w_output)
    v_low[...] = (dot(h[...], w_value[...]) + biases[5:6]).astype(BF16)
    context[...] = mixed_heads(turned, v_low[...], head_size, TN).astype(BF16)
    split_product(context, w_output, far, near)


def split_product(left, right, far, near, extra=None, along=None):
    half, total = near.shape[0], None
    for start, out in ((half, far), (0, near)):
        at = pl.ds(start, half)
        value = dot(left[at], right[...], NT)
        if extra is not None:
            value = value + dot(extra[0][at], extra[1][...], NT)
        out[...] = value.astype(out.dtype)
        if along is not None:
            summed = jnp.sum(value * along[at].astype(F32), axis=0, keepdims=True)
            total = summed if total is None else total + summed
    return total


def middle_kernel(s, near, got, send, keep):
    rows = send.shape[0]
    send[...] = (near[rows:] + got[rows:].astype(F32)).astype(BF16)
    keep[...] = near[:rows] + got[:rows].astype(F32)


def second_norm_kernel(s, keep, got, x_own, vectors, x_one, h):
    value = x_own[...].astype(F32) + keep[...] + got[...].astype(F32) + vectors[2:3]
    x_one[...] = value
    normed, _ = normalize(value)
    h[...] = (normed * vectors[1:2]).astype(BF16)


def grad_act_kernel(counts, depth, s, p0, p1, p2, p3, *refs):
    even, odd = refs[: counts[0]], refs[counts[0] : counts[1]]
    grad_act, g, w_hidden, w_down, weight, sem = refs[counts[1] :]
    copies = fetch(even, odd, weight, depth, sem)
    join((p0, p1, p2, p3), g)
    for copy in copies:
        copy.wait()
    split_weight(weight, w_hidden, w_down)
    grad_act[...] = dot(g[...], w_down[...])


def hidden_kernel(s, p0, p1, p2, p3, w_hidden, biases, grad_act, out_far, out_near, act, grad_pre, h):
    join((p0, p1, p2, p3), h)
    pre = dot(h[...], w_hidden[...]) + biases[6:7]
    sigma = jax.nn.sigmoid(pre)
    act[...] = (pre * sigma).astype(BF16)
    grad_pre[...] = (grad_act[...] * (sigma * (1.0 + pre * (1.0 - sigma)))).astype(BF16)
    split_product(grad_pre, w_hidden, out_far, out_near)


PAIR_FIRST = (3, 1, 2, 0)
RING_SENT, RING_KEPT = ((3, 1), (1, 1), (3, 0), (1, 0)), ((2, 1), (0, 1), (2, 0), (0, 0))


def spread_terms(term, outs, depth):
    if len(outs) == 1:
        outs[0][...] = term[...]
        return
    pair_sent, pair_kept, ring_sent, ring_kept = outs
    cut = pair_kept.shape[1]

    def copy(out, at, block, columns):
        out[pl.ds(at * depth, depth)] = term[pl.ds(block * depth, depth), columns]

    for at, j in enumerate(PAIR_FIRST):
        copy(pair_sent, at, 2 * j + 1, slice(0, cut))
        copy(pair_kept, at, 2 * j, slice(0, cut))
    for at in range(4):
        (j, i), (k, m) = RING_SENT[at], RING_KEPT[at]
        copy(ring_sent, at, 2 * j + i, slice(cut, None))
        copy(ring_kept, at, 2 * k + m, slice(cut, None))


def two_terms(left_one, right_one, left_two, right_two, term):
    first = dot(left_one[...], right_one[...], TN)
    second = dot(left_two[...], right_two[...], TN)
    term[...] = pack(first, second).astype(BF16)


def down_kernel(depth, s, h, g, act, grad_pre, w_down, far, near, b_hidden, *refs):
    *outs, term = refs
    two_terms(h, grad_pre, g, act, term)
    spread_terms(term, outs, depth)
    b_hidden[...] = jnp.sum(grad_pre[...].astype(F32), axis=0, keepdims=True)
    split_product(act, w_down, far, near)


def owned_kernel(n_got, s, keep, *refs):
    total = keep[...]
    for got in refs[:n_got]:
        total = total + got[pl.ds(0, total.shape[0])].astype(F32)
    refs[n_got][...], refs[n_got + 1][...] = unpack(total)


def grad_middle_kernel(s, keep, got, x_one, grad, vectors, grad_low, grad_full, sums):
    normed, inverse = normalize(x_one[...])
    grad_h = keep[...] + got[...].astype(F32)
    full = grad[...].astype(F32) + norm_back(grad_h, normed, inverse, vectors[1:2])
    grad_full[...] = full
    grad_low[...] = full.astype(BF16)
    sums[...] = vectors[...]
    sums[5:6] = jnp.sum(full, axis=0, keepdims=True)
    sums[6:7] = jnp.sum(grad_h * normed, axis=0, keepdims=True)


def grad_context_kernel(depth, head_size, s, p0, p1, p2, p3, w_output, turned, context, h, *refs):
    grad_context, grad_value, gm, *outs, term = refs
    join((p0, p1, p2, p3), gm)
    grad_context[...] = dot(gm[...], w_output[...]).astype(BF16)
    grad_value[...] = mixed_heads(turned, grad_context[...], head_size, NN).astype(BF16)
    two_terms(h, grad_value, gm, context, term)
    spread_terms(term, outs, depth)


def grad_scores_kernel(head_size, s, turned, grad_context, v_low, q_low, k_low, q_raw, biases, *refs):
    grad_qk, sums, grad_q, grad_k, scores = refs
    rows = q_low.shape[0]
    grad_q[...] = jnp.zeros_like(grad_q)
    grad_k[...] = jnp.zeros_like(grad_k)

    def head(number, carry):
        grad_chance = dot(v_low[...], of_head(grad_context[...], number, head_size), NT)
        chance = turned[number].astype(F32)
        product = chance * grad_chance
        center = jnp.sum(product, axis=0, keepdims=True)
        scores[...] = (product - chance * center).astype(BF16)
        grad_q[...] += dot(scores[...], of_head(k_low[...], number, head_size), TN)
        grad_k[...] += dot(scores[...], of_head(q_low[...], number, head_size))
        return carry

    for number in range(turned.shape[0]):
        head(number, 0)
    low = grad_q[...].astype(BF16).astype(F32)
    sums[0:1] = jnp.sum(low * q_raw[...], axis=0, keepdims=True)
    low = (low * biases[7:8]).astype(BF16).astype(F32)
    grad_qk[...] = pack(low, grad_k[...]).astype(BF16)
    sums[1:2] = jnp.sum(low, axis=0, keepdims=True)


def grad_first_kernel(
    n_dp, depth, s, grad_qk, w_qk, grad_value, w_value, h, sums_in, sums_q, b_hidden, slope, *refs
):
    far, near, sums, *outs, term = refs
    term[...] = dot(h[...], grad_qk[...], TN).astype(BF16)
    spread_terms(term, outs, depth)
    mine, place = s[0], s[1]
    gained = split_product(grad_qk, w_qk, far, near, (grad_value, w_value), h) / sums_in[0:1]
    row = lax.broadcasted_iota(jnp.int32, sums.shape, 0)
    sums[...] = reorder(jnp.where(row == 7, gained, sums_in[...]), mine, n_dp)
    sums[0:4] = jnp.zeros((4, sums.shape[1]), F32)
    local_width, head_size = sums_q.shape[1], slope.shape[1]
    b_value = jnp.sum(grad_value[...].astype(F32), axis=0, keepdims=True)
    share = jnp.concatenate([sums_q[1:2], b_value, b_hidden[...]], axis=0)
    for number in range(sums.shape[1] // local_width):

        @pl.when(place == number)
        def _():
            sums[0:3, number * local_width : (number + 1) * local_width] = share

    scale = sums_q[0:1]
    total = scale[:, :head_size]
    for number in range(1, local_width // head_size):
        total = total + scale[:, number * head_size : (number + 1) * head_size]
    sums[3:4, :head_size] = total * slope[...]
    if len(outs) > 1:
        outs[0][pl.ds(4 * depth, 32)] = fold(sums[...], outs[0].shape[1])


def fold(vectors, width):
    part = vectors.shape[1] // 4
    rows = jnp.concatenate([vectors[:, k * part : (k + 1) * part] for k in range(4)], axis=0)
    return jnp.concatenate([rows, jnp.zeros((32, width - part), F32)], axis=1).astype(BF16)


def unfold(rows, part):
    return jnp.concatenate([rows[8 * k : 8 * k + 8, :part] for k in range(4)], axis=1)


def first_sum_kernel(s, pair_kept, pair_got, ring_kept, ring_got, *refs):
    *given, pair_out, pair_mid, ring_out, ring_mid = refs
    half = pair_mid.shape[0]
    value = pair_kept[...].astype(F32) + pair_got[pl.ds(0, 2 * half)].astype(F32)
    pair_out[pl.ds(0, half)] = value[:half].astype(BF16)
    pair_mid[...] = value[half:]
    value = ring_kept[...].astype(F32) + ring_got[...].astype(F32)
    ring_out[...] = value[:half].astype(BF16)
    ring_mid[...] = value[half:]
    if given:
        low = fold(given[0][...], pair_out.shape[1]).astype(F32) + pair_got[pl.ds(2 * half, 32)].astype(F32)
        pair_out[pl.ds(half, 32)] = low.astype(BF16)


def second_sum_kernel(s, pair_mid, pair_got, ring_mid, ring_got, *refs):
    half, depth, cut = pair_mid.shape[0], pair_mid.shape[0] // 2, pair_mid.shape[1]
    given, out, zero = refs[: len(refs) // 3], refs[len(refs) // 3], refs[len(refs) // 3 + 1]
    pair = pair_mid[...] + pair_got[pl.ds(0, half)].astype(F32)
    ring = ring_mid[...] + ring_got[...].astype(F32)
    out[:, :cut], out[:, cut:] = pair[:depth].astype(BF16), ring[:depth].astype(BF16)
    zero[:, :cut], zero[:, cut:] = pair[depth:], ring[depth:]
    if given:
        at, vectors = pl.ds(half, 32), refs[-1]
        vectors[...] = unfold(given[0][at].astype(F32) + pair_got[at].astype(F32), vectors.shape[1] // 4)


def total_kernel(s, one, two, *outs):
    total = one[...] + two[...]
    for out, row in zip(outs[:7], (0, 1, 2, 6, 4, 5, 7)):
        for k in range(out.shape[0]):
            out[k : k + 1] = total[row : row + 1, k * LANES : (k + 1) * LANES]
    outs[7][...] = total[3:4, : outs[7].shape[1]]


def last_kernel(n_dp, s, keep, got, x_own, grad_full, sums_in, grad_in):
    normed, inverse = normalize(x_own[...].astype(F32))
    grad_h = keep[...] + got[...].astype(F32)
    full = grad_full[...] + norm_back(grad_h, normed, inverse, sums_in[0:1])
    grad_in[...] = reorder(full, s[0], n_dp).astype(BF16)


def add_kernel(s, one, two, out):
    out[...] = one[...] + two[...]


def output_kernel(n_dp, s, keep, got, x_one, vectors, out):
    value = x_one[...] + keep[...] + got[...].astype(F32) + vectors[3:4]
    out[...] = reorder(value, s[0], n_dp).astype(BF16)


def tie(*values):
    return lax.optimization_barrier(values)


class Links:
    def __init__(self, n_dp, n_tensor):
        self.n_dp, self.n_tensor = n_dp, n_tensor
        self.wide = n_dp > 8

    def move(self, value, target):
        pairs = []
        for d in range(self.n_dp):
            for t in range(self.n_tensor):
                to_d, to_t = target(d, t)
                pairs.append((d * self.n_tensor + t, to_d * self.n_tensor + to_t))
        return lax.ppermute(value, AXES, pairs)

    def chip(self, value):
        return self.move(value, lambda d, t: (d, t ^ 2))

    def core(self, value):
        return self.move(value, lambda d, t: (d, t ^ 1))

    def pair(self, value):
        return self.along(value, 1)

    def along(self, value, bits):
        return self.move(value, lambda d, t: (d ^ bits, t))

    def gather_tensor(self, rows):
        near = self.chip(rows)
        return rows, near, self.core(rows), self.core(near)

    def gather_wide(self, shard):
        blocks, place = lax.all_gather(shard, "dp", axis=0), lax.axis_index("dp")
        return jnp.take(blocks, lax.iota(jnp.int32, self.n_dp) ^ place, axis=0).reshape(-1, shard.shape[1])

    def scatter_wide(self, total):
        place = lax.axis_index("dp")
        blocks = total.reshape(self.n_dp, total.shape[0] // self.n_dp, total.shape[1])
        blocks = jnp.take(blocks, lax.iota(jnp.int32, self.n_dp) ^ place, axis=0).astype(F32)
        return unpack(lax.psum_scatter(blocks.reshape(total.shape), "dp", scatter_dimension=0, tiled=True))

    def steps(self):
        found, bit = [], 1
        while bit < self.n_dp and self.wide:
            found.append(lambda d, t, bit=bit: (d ^ bit, t))
            bit *= 2
        far = [] if self.wide else [lambda d, t: (d ^ 4, t)]
        return found + [lambda d, t: (d, t ^ 1), lambda d, t: (d, t ^ 2)] + far


def body(
    inputs,
    weight_query,
    weight_key,
    weight_value,
    weight_output,
    weight_hidden,
    weight_down,
    bias_query,
    bias_value,
    bias_hidden,
    bias_output,
    bias_final,
    gain_attention,
    gain_mixer,
    query_scale,
    lengths,
    cotangent,
    n_dp,
    n_tensor,
):
    links = Links(n_dp, n_tensor)
    wide = links.wide
    local_rows, width = inputs.shape
    all_rows = local_rows * n_tensor
    depth = width // n_dp
    local_width = weight_query.shape[1]
    both = 2 * local_width
    head_size = query_scale.shape[0]
    heads = local_width // head_size
    dp_index = lax.axis_index("dp")
    tensor_index = lax.axis_index("tensor")
    s = jnp.stack([dp_index, tensor_index, lengths[0]])
    product = 2 * all_rows * width * local_width
    mixed = 2 * all_rows * all_rows * local_width

    def run(name, kernel, outs, *arguments, **rest):
        return call(name, kernel, [shaped(*o) for o in outs], s, *arguments, **rest)

    def bind(kernel, *fixed):
        def bound(*refs):
            return kernel(*fixed, *refs)

        return bound

    packed = [((depth, both), BF16)]
    rows_low, rows_full = ((local_rows, width), BF16), ((local_rows, width), F32)
    split = [((all_rows // 2, width), BF16), ((all_rows // 2, width), F32)]
    part = ((all_rows, local_width), BF16)
    part_full = ((all_rows, local_width), F32)
    whole_rows = ((all_rows, width), BF16)
    weight = ((width, local_width), BF16)
    vector = ((8, width), F32)
    halves = [((width // 2, both), BF16)] * 2
    term = [pltpu.VMEM((width, both), BF16)]
    sems = [pltpu.SemaphoreType.DMA((n_dp,))]

    unit = SOFTPLUS_UNIT / jnp.sqrt(F32(head_size))
    scale_wide = jnp.tile(jax.nn.softplus(query_scale) * unit, heads)[None]
    slope = (jax.nn.sigmoid(query_scale) * unit)[None]
    loads = [pltpu.VMEM((depth, local_width), BF16)] * 2 + [pltpu.SemaphoreType.DMA((2,))]

    def apart(value):
        return pltpu.with_memory_space_constraint(value, pltpu.HBM)

    def pack_two(name, one, two):
        return run("pack_" + name, pack_kernel, packed, apart(one), apart(two), remote=2, scratch=loads)[0]

    own_qk = pack_two("qk", weight_query, weight_key)
    given = (gain_attention, gain_mixer, bias_output, bias_final, bias_query, bias_value, bias_hidden)
    scale_wide, slope = tie(scale_wide, slope)
    tall = (width // LANES, LANES)
    h_own, x_own, grad_own, vectors, biases = run(
        "prepare",
        bind(prepare_kernel, n_dp),
        [rows_low, rows_low, rows_low, vector, ((8, local_width), F32)],
        scale_wide,
        *(apart(v) for v in (inputs, cotangent, *(v.reshape(tall) for v in given))),
        remote=9,
        scratch=[pltpu.VMEM((local_rows, width), BF16)] * 2
        + [pltpu.VMEM(tall, F32)] * 7
        + [pltpu.SemaphoreType.DMA((9,))],
    )
    own_vo = pack_two("vo", weight_value, weight_output.T)
    own_hd = pack_two("hd", weight_hidden, weight_down.T)

    def stack(*blocks):
        rows = sum(block.shape[0] for block in blocks)
        return run("stack", stack_kernel, [((rows, both), BF16)], *blocks)[0]

    if wide:
        qk, vo, hd = (([links.gather_wide(own)], []) for own in (own_qk, own_vo, own_hd))
        h_one, grad_rows = links.gather_tensor(h_own), links.gather_tensor(grad_own)
    else:
        qk_one, qk_two = links.along(own_qk, 2), links.along(own_qk, 4)
        h_own, own_vo, own_hd, qk_one, qk_two = tie(h_own, own_vo, own_hd, qk_one, qk_two)
        h_chip = links.chip(h_own)
        qk_three = links.along(qk_two, 2)
        near_qk_pair = links.pair(stack(own_qk, qk_one))
        vo_one, vo_two = links.along(own_vo, 2), links.along(own_vo, 4)
        far_stack = stack(qk_two, qk_three)
        far_stack, near_qk_pair, h_chip, vo_one, vo_two = tie(far_stack, near_qk_pair, h_chip, vo_one, vo_two)
        h_one = h_own, h_chip, links.core(h_own), links.core(h_chip)
        far_qk_pair = links.pair(far_stack)
        vo_three = links.along(vo_two, 2)
        near_vo = stack(own_vo, vo_one)
        qk = [own_qk, qk_one, qk_two, qk_three], [near_qk_pair, far_qk_pair]
        h_one, qk, vo_three, near_vo = tie(h_one, qk, vo_three, near_vo)
        near_vo_pair = links.pair(near_vo)
        hd_one, hd_two = links.along(own_hd, 2), links.along(own_hd, 4)
        grad_chip = links.chip(grad_own)
    n_qk = len(qk[0]), len(qk[0]) + len(qk[1])
    q_raw, q_low, k_low, h_all, w_qk, turned = run(
        "attend",
        bind(attend_kernel, n_qk, depth, head_size),
        [
            part_full,
            part,
            part,
            whole_rows,
            ((width, both), BF16),
            ((heads, all_rows, all_rows), BF16),
        ],
        *h_one,
        biases,
        *qk[0],
        *qk[1],
        remote=n_qk[1],
        scratch=sems,
    )
    if not wide:
        turned, near_vo_pair, hd_one, hd_two, grad_chip = tie(turned, near_vo_pair, hd_one, hd_two, grad_chip)
        far_vo_pair = links.pair(stack(vo_two, vo_three))
        hd_three = links.along(hd_two, 2)
        grad_rows = grad_own, grad_chip, links.core(grad_own), links.core(grad_chip)
        vo = [own_vo, vo_one, vo_two, vo_three], [near_vo_pair, far_vo_pair]
        turned, vo, grad_rows, hd_three = tie(turned, vo, grad_rows, hd_three)
        near_hd_pair = links.pair(stack(own_hd, hd_one))
    n_vo = len(vo[0]), len(vo[0]) + len(vo[1])
    v_low, context, far, near, w_value, w_output = run(
        "context",
        bind(context_kernel, n_vo, depth, head_size),
        [part, part, *split, weight, weight],
        h_all,
        turned,
        biases,
        *vo[0],
        *vo[1],
        remote=n_vo[1],
        scratch=term + sems,
    )

    def core_half(far, near, *extra):
        got, *extra = tie(links.core(far), *extra)
        return list(run("middle", middle_kernel, [rows_low, rows_full], near, got)) + list(extra)

    if wide:
        send, keep = core_half(far, near)
        got = links.chip(send)
    else:
        far, near_hd_pair = tie(far, near_hd_pair)
        send, keep = core_half(far, near)
        got = links.chip(send)
        far_hd_pair = links.pair(stack(hd_two, hd_three))
        hd = [own_hd, hd_one, hd_two, hd_three], [near_hd_pair, far_hd_pair]
        got, hd = tie(got, hd)
    n_hd = len(hd[0]), len(hd[0]) + len(hd[1])
    x_one, h_two_own = run("second_norm", second_norm_kernel, [rows_full, rows_low], keep, got, x_own, vectors)
    h_two = links.gather_tensor(h_two_own)
    grad_act, grad_all, w_hidden, w_down = run(
        "grad_act",
        bind(grad_act_kernel, n_hd, depth),
        [part_full, whole_rows, weight, weight],
        *grad_rows,
        *hd[0],
        *hd[1],
        remote=n_hd[1],
        scratch=term + sems,
    )
    far, near, act, grad_pre, h_two_all = run(
        "hidden",
        hidden_kernel,
        [*split, part, part, whole_rows],
        *h_two,
        w_hidden,
        biases,
        grad_act,
    )
    cut = 3 * both // 5
    tall_sent = n_dp // 2 * depth
    terms = [((width, both), BF16)]
    if not wide:
        terms = [((tall_sent, c), BF16) for c in (cut, cut, both - cut, both - cut)]
    mix_far, mix_near, grad_b_hidden, *terms_hd = run(
        "down",
        bind(down_kernel, depth),
        [*split, ((1, local_width), F32), *terms],
        h_two_all,
        grad_all,
        act,
        grad_pre,
        w_down,
        scratch=term,
    )
    send, keep, terms_hd = core_half(far, near, terms_hd)
    got = links.chip(send)

    def first_send(terms):
        return [links.pair(terms[0]), links.along(terms[2], 2)]

    def first_sum(name, terms, got, given=()):
        rows = tall_sent // 2
        extra = 32 if given else 0
        outs = [((rows + extra, cut), BF16), ((rows, cut), F32), ((rows, both - cut), BF16), ((rows, both - cut), F32)]
        return run("first_" + name, first_sum_kernel, outs, terms[1], got[0], terms[3], got[1], *given)

    def second_send(sums):
        return [links.along(sums[0], 2), links.pair(sums[2])]

    def second_sum(name, sums, got, given=False):
        outs = packed + [((depth, both), F32)] + ([vector] if given else [])
        more = sums[:1] if given else []
        return run("second_" + name, second_sum_kernel, outs, sums[1], got[0], sums[3], got[1], *more)

    def owned(name, *parts):
        outs = [((depth, local_width), F32)] * 2
        return run("owned_" + name, bind(owned_kernel, len(parts) - 1), outs, *parts)

    if not wide:
        got_hd = first_send(terms_hd)
        got, got_hd = tie(got, got_hd)
    grad_mid_low, grad_mid, sums = run(
        "grad_middle",
        grad_middle_kernel,
        [rows_low, rows_full, vector],
        keep,
        got,
        x_one,
        grad_own,
        vectors,
    )
    if wide:
        grad_mid_rows = links.gather_tensor(grad_mid_low)
    else:
        grad_mid_chip = links.chip(grad_mid_low)
        sums_hd = first_sum("hd", terms_hd, got_hd)
        got_hd = second_send(sums_hd)
        grad_mid_chip, got_hd = tie(grad_mid_chip, got_hd)
        sent_hd, zero_hd = second_sum("hd", sums_hd, got_hd)
        grad_mid_rows = grad_mid_low, grad_mid_chip, links.core(grad_mid_low), links.core(grad_mid_chip)
    grad_mid_rows, mix_far = tie(grad_mid_rows, mix_far)
    mix_send, mix_keep = core_half(mix_far, mix_near)
    mix_got = links.chip(mix_send)
    grad_context, grad_value, _, *terms_vo = run(
        "grad_context",
        bind(grad_context_kernel, depth, head_size),
        [part, part, whole_rows, *terms],
        *grad_mid_rows,
        w_output,
        turned,
        context,
        h_all,
        scratch=term,
    )
    if not wide:
        got_vo = first_send(terms_vo)
        grad_context, sent_hd = tie(grad_context, sent_hd)
        part_hd = links.along(sent_hd, 4)
    grad_qk, sums_q = run(
        "grad_scores",
        bind(grad_scores_kernel, head_size),
        [((all_rows, both), BF16), ((8, local_width), F32)],
        turned,
        grad_context,
        v_low,
        q_low,
        k_low,
        q_raw,
        biases,
        scratch=[
            pltpu.VMEM((all_rows, local_width), F32),
            pltpu.VMEM((all_rows, local_width), F32),
            pltpu.VMEM((all_rows, all_rows), BF16),
        ],
    )
    if wide:
        grad_qk, mix_got = tie(grad_qk, mix_got)
    else:
        grad_qk, mix_got, part_hd, got_vo = tie(grad_qk, mix_got, part_hd, got_vo)
        sums_vo = first_sum("vo", terms_vo, got_vo)
        grad_qk, *sums_vo = tie(grad_qk, *sums_vo)
        got_vo = second_send(sums_vo)
    terms_first = list(terms)
    if not wide:
        terms_first[0] = ((tall_sent + 32, cut), BF16)
    far, near, sums, *terms_qk = run(
        "grad_first",
        bind(grad_first_kernel, n_dp, depth),
        [*split, vector, *terms_first],
        grad_qk,
        w_qk,
        grad_value,
        w_value,
        h_all,
        sums,
        sums_q,
        grad_b_hidden,
        slope,
        scratch=term,
    )
    def exchange(value, step):
        return run("add", add_kernel, [vector], value, links.move(value, step))[0]

    total = sums
    if wide:
        send, keep = core_half(far, near)
        got = links.chip(send)
    else:
        got_qk = first_send(terms_qk)
        far, got_vo = tie(far, got_vo)
        sent_vo, zero_vo = second_sum("vo", sums_vo, got_vo)
        send, keep, sent_vo = core_half(far, near, sent_vo)
        got = links.chip(send)
        part_vo = links.along(sent_vo, 4)
        (output,) = run("output", bind(output_kernel, n_dp), [rows_low], mix_keep, mix_got, x_one, vectors)
        grad_hidden, grad_down = owned("hd", zero_hd, part_hd)
        got, output, grad_hidden = tie(got, output, grad_hidden)
        got_qk, part_vo = tie(got_qk, part_vo)
        sums_qk = first_sum("qk", terms_qk, got_qk, [sums])
        got_qk = second_send(sums_qk)
        sent_qk, zero_qk, total = second_sum("qk", sums_qk, got_qk, True)
        far_qk = links.along(sent_qk, 4)
        got, zero_vo, total = tie(got, zero_vo, total)
    (grad_in,) = run("last", bind(last_kernel, n_dp), [rows_low], keep, got, x_own, grad_mid, vectors)
    if wide:
        (output,) = run("output", bind(output_kernel, n_dp), [rows_low], mix_keep, mix_got, x_one, vectors)
    steps = links.steps()
    for step in steps[:-1]:
        total = exchange(total, step)
    moved = links.move(total, steps[-1])
    tall_vector = (tall, F32)
    *totals, total_scale = run(
        "total", total_kernel, [tall_vector] * 7 + [((1, head_size), F32)], total, moved
    )
    totals = [v.reshape(width) for v in totals]
    if wide:
        grad_hidden, grad_down = links.scatter_wide(terms_hd[0])
        grad_output_v, grad_output_o = links.scatter_wide(terms_vo[0])
        grad_query, grad_key = links.scatter_wide(terms_qk[0])
    else:
        grad_output_v, grad_output_o = owned("vo", zero_vo, part_vo)
        grad_query, grad_key = owned("qk", zero_qk, far_qk)
    return (
        output,
        grad_in,
        grad_query,
        grad_key,
        grad_output_v,
        grad_output_o.T,
        grad_hidden,
        grad_down.T,
        totals[0],
        totals[1],
        totals[2],
        totals[5],
        totals[4],
        totals[6],
        totals[3],
        total_scale.reshape(head_size),
    )


def solution(mesh):
    n_dp, n_tensor = mesh.shape["dp"], mesh.shape["tensor"]

    def local(*arguments):
        return body(*arguments, n_dp, n_tensor)

    rows = P(("dp", "tensor"), None)
    into, out_of = P("dp", "tensor"), P("tensor", "dp")
    return jax.shard_map(
        local,
        mesh=mesh,
        in_specs=(rows, into, into, into, out_of, into, out_of, *[P()] * 8, P("dp"), rows),
        out_specs=(rows, rows, into, into, into, out_of, into, out_of, *[P()] * 8),
        check_vma=False,
    )
```

```python
import jax
import jax.numpy as jnp
from jax import lax
from jax.experimental import pallas as pl
from jax.experimental.pallas import tpu as pltpu
from jax.sharding import PartitionSpec as P

EPSILON = 1e-06
SOFTPLUS_UNIT = 1.442695041
AXES = ("dp", "tensor")
F32 = jnp.float32
BF16 = jnp.bfloat16
LANES = 128
TENSOR_ORDER = (0, 2, 1, 3)
NN, NT, TN = ((1,), (0,)), ((1,), (1,)), ((0,), (0,))


def dot(left, right, dims=NN):
    return lax.dot_general(left, right, (dims, ((), ())), preferred_element_type=F32)


def shaped(shape, kind):
    return jax.ShapeDtypeStruct(shape, kind)


def call(name, kernel, outs, scalars, *arguments, flops=1e6, scratch=(), limit=12, remote=0):
    space = pl.BlockSpec(memory_space=pltpu.VMEM)
    apart = pl.BlockSpec(memory_space=pltpu.HBM)
    moved = sum(a.size * a.dtype.itemsize for a in (*arguments, *outs))
    return pl.pallas_call(
        kernel,
        name=name,
        out_shape=outs,
        in_specs=[pl.BlockSpec(memory_space=pltpu.SMEM)]
        + [space] * (len(arguments) - remote)
        + [apart] * remote,
        out_specs=[space] * len(outs),
        scratch_shapes=scratch,
        compiler_params=pltpu.CompilerParams(vmem_limit_bytes=limit << 20),
        cost_estimate=pl.CostEstimate(flops=int(flops), bytes_accessed=moved, transcendentals=0),
    )(scalars, *arguments)


def pack(first, second):
    main = first.shape[1] // LANES * LANES
    return jnp.concatenate([first[:, :main], second[:, :main], first[:, main:], second[:, main:]], axis=1)


def unpack(both):
    width = both.shape[1] // 2
    main = width // LANES * LANES
    edge = main * 2 + width - main
    first = jnp.concatenate([both[:, :main], both[:, 2 * main : edge]], axis=1)
    rest = both[:, 2 * main :].astype(F32)[:, width - main :].astype(both.dtype)
    second = jnp.concatenate([both[:, main : 2 * main], rest], axis=1)
    return first, second


def reorder(value, place, n_dp):
    width = value.shape[1]
    lane = lax.broadcasted_iota(jnp.int32, (1, width), 1)
    span = width // n_dp
    bit = 1
    while bit < n_dp:
        low = lax.rem(lane, 2 * span) < span
        other = jnp.where(low, pltpu.roll(value, width - span, 1), pltpu.roll(value, span, 1))
        value = jnp.where((place & bit) != 0, other, value)
        bit, span = 2 * bit, 2 * span
    return value


def row_mean(value):
    return jnp.sum(value, axis=1, keepdims=True) * (1.0 / value.shape[1])


def normalize(value):
    inverse = lax.rsqrt(row_mean(value * value) + EPSILON)
    return value * inverse, inverse


def norm_back(grad_normed, normed, inverse, gain):
    scaled = grad_normed * gain
    return inverse * (scaled - normed * row_mean(scaled * normed))


def load(sources, targets, sem):
    copies = [pltpu.make_async_copy(a, b, sem.at[k]) for k, (a, b) in enumerate(zip(sources, targets))]
    for copy in copies:
        copy.start()
    for copy in copies:
        copy.wait()


def pack_kernel(s, first, second, out, one, two, sem):
    load((first, second), (one, two), sem)
    out[...] = pack(one[...].astype(F32), two[...].astype(F32)).astype(BF16)


def row_of(ref):
    return jnp.concatenate([ref[k : k + 1] for k in range(ref.shape[0])], axis=1)


def prepare_kernel(n_dp, s, scale, *refs):
    sources, (h, x_own, grad, vectors, biases) = refs[:9], refs[9:14]
    x, cotangent, *given = refs[14:23]
    load(sources, refs[14:23], refs[23])
    mine, place, length = s[0], s[1], s[2]
    value = reorder(x[...].astype(F32), mine, n_dp)
    stacked = jnp.concatenate([row_of(given[k]) for k in (0, 1, 2, 3, 4, 5, 6, 6)], axis=0)
    width = biases.shape[1]
    slices = stacked[:, :width]
    for number in range(1, stacked.shape[1] // width):
        slices = jnp.where(place == number, stacked[:, number * width : (number + 1) * width], slices)
    biases[...] = slices
    biases[7:8] = scale[...]
    stacked = reorder(stacked, mine, n_dp)
    normed, _ = normalize(value)
    h[...] = (normed * stacked[0:1]).astype(BF16)
    x_own[...] = value.astype(BF16)
    rows = value.shape[0]
    row = lax.broadcasted_iota(jnp.int32, value.shape, 0) + place * rows
    g = jnp.where(row < length, reorder(cotangent[...].astype(F32), mine, n_dp), 0.0)
    grad[...] = g.astype(BF16)
    vectors[...] = stacked
    vectors[4:5] = jnp.sum(g, axis=0, keepdims=True)


def join(pieces, out):
    rows = pieces[0].shape[0]
    for number, piece in enumerate(pieces):
        out[pl.ds(number * rows, rows)] = piece[...]


def tiles(rows, body, size=128):
    def step(m, carry):
        body(pl.ds(pl.multiple_of(m * size, size), size), m)
        return carry

    lax.fori_loop(0, rows // size, step, 0)


def positions(shape, axis, place, local, offset=0):
    row = lax.broadcasted_iota(jnp.int32, shape, axis) + offset
    shift = local.bit_length() - 1
    block = row >> shift
    turned = ((block & 1) << 1) | (block >> 1)
    return ((place ^ turned) << shift) + (row & (local - 1))


def fetch(even, odd, out, depth, sem):
    copies = []
    if not odd:
        copies.append(pltpu.make_async_copy(even[0], out, sem.at[0]))
    else:
        for start, blocks in enumerate((even, odd)):
            row = start * depth
            for block in blocks:
                for k in range(block.shape[0] // depth):
                    source, target = block.at[pl.ds(k * depth, depth)], out.at[pl.ds(row, depth)]
                    copies.append(pltpu.make_async_copy(source, target, sem.at[len(copies)]))
                    row += 2 * depth
    for one in copies:
        one.start()
    return copies


def stack_kernel(s, *refs):
    join(refs[:-1], refs[-1])


def of_head(value, number, head_size):
    lanes = lax.broadcasted_iota(jnp.int32, (1, value.shape[1]), 1) // head_size
    return jnp.where(lanes == number, value, jnp.zeros((), value.dtype))


def attend_kernel(counts, depth, head_size, s, p0, p1, p2, p3, biases, *refs):
    even, odd = refs[: counts[0]], refs[counts[0] : counts[1]]
    q_raw, q_low, k_low, h, weight, turned, sem = refs[counts[1] :]
    copies = fetch(even, odd, weight, depth, sem)
    join((p0, p1, p2, p3), h)
    for copy in copies:
        copy.wait()
    first, second = unpack(dot(h[...], weight[...]))
    first = first + biases[4:5]
    q_raw[...] = first
    q_low[...] = (first * biases[7:8]).astype(BF16)
    k_low[...] = second.astype(BF16)
    place, length = s[1], s[2]
    rows, local = q_low.shape[0], p0.shape[0]
    key_place = positions((rows, 1), 0, place, local)
    last = jnp.minimum(positions((1, rows), 1, place, local), length - 1)

    def head(number, carry):
        score = dot(k_low[...], of_head(q_low[...], number, head_size), NT)
        score = jnp.where(key_place <= last, score, -1e30)
        raised = jnp.exp(score - jnp.max(score, axis=0, keepdims=True))
        share = 1.0 / jnp.sum(raised, axis=0, keepdims=True)
        turned[number] = (raised * share).astype(BF16)
        return carry

    for number in range(turned.shape[0]):
        head(number, 0)


def mixed_heads(turned, value, head_size, dims):
    total = None
    for number in range(turned.shape[0]):
        term = dot(turned[number], of_head(value, number, head_size), dims)
        total = term if total is None else total + term
    return total


def split_weight(weight, one, two):
    one[...], two[...] = unpack(weight[...])


def context_kernel(counts, depth, head_size, s, h, turned, biases, *refs):
    even, odd = refs[: counts[0]], refs[counts[0] : counts[1]]
    v_low, context, far, near, w_value, w_output, weight, sem = refs[counts[1] :]
    for copy in fetch(even, odd, weight, depth, sem):
        copy.wait()
    split_weight(weight, w_value, w_output)
    v_low[...] = (dot(h[...], w_value[...]) + biases[5:6]).astype(BF16)
    context[...] = mixed_heads(turned, v_low[...], head_size, TN).astype(BF16)
    split_product(context, w_output, far, near)


def split_product(left, right, far, near, extra=None, along=None):
    half, total = near.shape[0], None
    for start, out in ((half, far), (0, near)):
        at = pl.ds(start, half)
        value = dot(left[at], right[...], NT)
        if extra is not None:
            value = value + dot(extra[0][at], extra[1][...], NT)
        out[...] = value.astype(out.dtype)
        if along is not None:
            summed = jnp.sum(value * along[at].astype(F32), axis=0, keepdims=True)
            total = summed if total is None else total + summed
    return total


def middle_kernel(s, near, got, send, keep):
    rows = send.shape[0]
    send[...] = (near[rows:] + got[rows:].astype(F32)).astype(BF16)
    keep[...] = near[:rows] + got[:rows].astype(F32)


def second_norm_kernel(s, keep, got, x_own, vectors, x_one, h):
    value = x_own[...].astype(F32) + keep[...] + got[...].astype(F32) + vectors[2:3]
    x_one[...] = value
    normed, _ = normalize(value)
    h[...] = (normed * vectors[1:2]).astype(BF16)


def grad_act_kernel(counts, depth, s, p0, p1, p2, p3, *refs):
    even, odd = refs[: counts[0]], refs[counts[0] : counts[1]]
    grad_act, g, w_hidden, w_down, weight, sem = refs[counts[1] :]
    copies = fetch(even, odd, weight, depth, sem)
    join((p0, p1, p2, p3), g)
    for copy in copies:
        copy.wait()
    split_weight(weight, w_hidden, w_down)
    grad_act[...] = dot(g[...], w_down[...])


def hidden_kernel(s, p0, p1, p2, p3, w_hidden, biases, grad_act, out_far, out_near, act, grad_pre, h):
    join((p0, p1, p2, p3), h)
    pre = dot(h[...], w_hidden[...]) + biases[6:7]
    sigma = jax.nn.sigmoid(pre)
    act[...] = (pre * sigma).astype(BF16)
    grad_pre[...] = (grad_act[...] * (sigma * (1.0 + pre * (1.0 - sigma)))).astype(BF16)
    split_product(grad_pre, w_hidden, out_far, out_near)


PAIR_FIRST = (3, 1, 2, 0)
RING_SENT, RING_KEPT = ((3, 1), (1, 1), (3, 0), (1, 0)), ((2, 1), (0, 1), (2, 0), (0, 0))


def spread_terms(term, outs, depth):
    if len(outs) == 1:
        outs[0][...] = term[...]
        return
    pair_sent, pair_kept, ring_sent, ring_kept = outs
    cut = pair_kept.shape[1]

    def copy(out, at, block, columns):
        out[pl.ds(at * depth, depth)] = term[pl.ds(block * depth, depth), columns]

    for at, j in enumerate(PAIR_FIRST):
        copy(pair_sent, at, 2 * j + 1, slice(0, cut))
        copy(pair_kept, at, 2 * j, slice(0, cut))
    for at in range(4):
        (j, i), (k, m) = RING_SENT[at], RING_KEPT[at]
        copy(ring_sent, at, 2 * j + i, slice(cut, None))
        copy(ring_kept, at, 2 * k + m, slice(cut, None))


def two_terms(left_one, right_one, left_two, right_two, term):
    first = dot(left_one[...], right_one[...], TN)
    second = dot(left_two[...], right_two[...], TN)
    term[...] = pack(first, second).astype(BF16)


def down_kernel(depth, s, h, g, act, grad_pre, w_down, far, near, b_hidden, *refs):
    *outs, term = refs
    two_terms(h, grad_pre, g, act, term)
    spread_terms(term, outs, depth)
    b_hidden[...] = jnp.sum(grad_pre[...].astype(F32), axis=0, keepdims=True)
    split_product(act, w_down, far, near)


def owned_kernel(n_got, s, keep, *refs):
    total = keep[...]
    for got in refs[:n_got]:
        total = total + got[pl.ds(0, total.shape[0])].astype(F32)
    refs[n_got][...], refs[n_got + 1][...] = unpack(total)


def grad_middle_kernel(s, keep, got, x_one, grad, vectors, grad_low, grad_full, sums):
    normed, inverse = normalize(x_one[...])
    grad_h = keep[...] + got[...].astype(F32)
    full = grad[...].astype(F32) + norm_back(grad_h, normed, inverse, vectors[1:2])
    grad_full[...] = full
    grad_low[...] = full.astype(BF16)
    sums[...] = vectors[...]
    sums[5:6] = jnp.sum(full, axis=0, keepdims=True)
    sums[6:7] = jnp.sum(grad_h * normed, axis=0, keepdims=True)


def grad_context_kernel(depth, head_size, s, p0, p1, p2, p3, w_output, turned, context, h, *refs):
    grad_context, grad_value, gm, *outs, term = refs
    join((p0, p1, p2, p3), gm)
    grad_context[...] = dot(gm[...], w_output[...]).astype(BF16)
    grad_value[...] = mixed_heads(turned, grad_context[...], head_size, NN).astype(BF16)
    two_terms(h, grad_value, gm, context, term)
    spread_terms(term, outs, depth)


def grad_scores_kernel(head_size, s, turned, grad_context, v_low, q_low, k_low, q_raw, biases, *refs):
    grad_qk, sums, grad_q, grad_k, scores = refs
    rows = q_low.shape[0]
    grad_q[...] = jnp.zeros_like(grad_q)
    grad_k[...] = jnp.zeros_like(grad_k)

    def head(number, carry):
        grad_chance = dot(v_low[...], of_head(grad_context[...], number, head_size), NT)
        chance = turned[number].astype(F32)
        product = chance * grad_chance
        center = jnp.sum(product, axis=0, keepdims=True)
        scores[...] = (product - chance * center).astype(BF16)
        grad_q[...] += dot(scores[...], of_head(k_low[...], number, head_size), TN)
        grad_k[...] += dot(scores[...], of_head(q_low[...], number, head_size))
        return carry

    for number in range(turned.shape[0]):
        head(number, 0)
    low = grad_q[...].astype(BF16).astype(F32)
    sums[0:1] = jnp.sum(low * q_raw[...], axis=0, keepdims=True)
    low = (low * biases[7:8]).astype(BF16).astype(F32)
    grad_qk[...] = pack(low, grad_k[...]).astype(BF16)
    sums[1:2] = jnp.sum(low, axis=0, keepdims=True)


def grad_first_kernel(
    n_dp, depth, s, grad_qk, w_qk, grad_value, w_value, h, sums_in, sums_q, b_hidden, slope, *refs
):
    far, near, sums, *outs, term = refs
    term[...] = dot(h[...], grad_qk[...], TN).astype(BF16)
    spread_terms(term, outs, depth)
    mine, place = s[0], s[1]
    gained = split_product(grad_qk, w_qk, far, near, (grad_value, w_value), h) / sums_in[0:1]
    row = lax.broadcasted_iota(jnp.int32, sums.shape, 0)
    sums[...] = reorder(jnp.where(row == 7, gained, sums_in[...]), mine, n_dp)
    sums[0:4] = jnp.zeros((4, sums.shape[1]), F32)
    local_width, head_size = sums_q.shape[1], slope.shape[1]
    b_value = jnp.sum(grad_value[...].astype(F32), axis=0, keepdims=True)
    share = jnp.concatenate([sums_q[1:2], b_value, b_hidden[...]], axis=0)
    for number in range(sums.shape[1] // local_width):

        @pl.when(place == number)
        def _():
            sums[0:3, number * local_width : (number + 1) * local_width] = share

    scale = sums_q[0:1]
    total = scale[:, :head_size]
    for number in range(1, local_width // head_size):
        total = total + scale[:, number * head_size : (number + 1) * head_size]
    sums[3:4, :head_size] = total * slope[...]
    if len(outs) > 1:
        outs[0][pl.ds(4 * depth, 32)] = fold(sums[...], outs[0].shape[1])


def fold(vectors, width):
    part = vectors.shape[1] // 4
    rows = jnp.concatenate([vectors[:, k * part : (k + 1) * part] for k in range(4)], axis=0)
    return jnp.concatenate([rows, jnp.zeros((32, width - part), F32)], axis=1).astype(BF16)


def unfold(rows, part):
    return jnp.concatenate([rows[8 * k : 8 * k + 8, :part] for k in range(4)], axis=1)


def first_sum_kernel(s, pair_kept, pair_got, ring_kept, ring_got, *refs):
    *given, pair_out, pair_mid, ring_out, ring_mid = refs
    half = pair_mid.shape[0]
    value = pair_kept[...].astype(F32) + pair_got[pl.ds(0, 2 * half)].astype(F32)
    pair_out[pl.ds(0, half)] = value[:half].astype(BF16)
    pair_mid[...] = value[half:]
    value = ring_kept[...].astype(F32) + ring_got[...].astype(F32)
    ring_out[...] = value[:half].astype(BF16)
    ring_mid[...] = value[half:]
    if given:
        low = fold(given[0][...], pair_out.shape[1]).astype(F32) + pair_got[pl.ds(2 * half, 32)].astype(F32)
        pair_out[pl.ds(half, 32)] = low.astype(BF16)


def second_sum_kernel(s, pair_mid, pair_got, ring_mid, ring_got, *refs):
    half, depth, cut = pair_mid.shape[0], pair_mid.shape[0] // 2, pair_mid.shape[1]
    given, out, zero = refs[: len(refs) // 3], refs[len(refs) // 3], refs[len(refs) // 3 + 1]
    pair = pair_mid[...] + pair_got[pl.ds(0, half)].astype(F32)
    ring = ring_mid[...] + ring_got[...].astype(F32)
    out[:, :cut], out[:, cut:] = pair[:depth].astype(BF16), ring[:depth].astype(BF16)
    zero[:, :cut], zero[:, cut:] = pair[depth:], ring[depth:]
    if given:
        at, vectors = pl.ds(half, 32), refs[-1]
        vectors[...] = unfold(given[0][at].astype(F32) + pair_got[at].astype(F32), vectors.shape[1] // 4)


def total_kernel(s, one, two, *outs):
    total = one[...] + two[...]
    for out, row in zip(outs[:7], (0, 1, 2, 6, 4, 5, 7)):
        for k in range(out.shape[0]):
            out[k : k + 1] = total[row : row + 1, k * LANES : (k + 1) * LANES]
    outs[7][...] = total[3:4, : outs[7].shape[1]]


def last_kernel(n_dp, s, keep, got, x_own, grad_full, sums_in, grad_in):
    normed, inverse = normalize(x_own[...].astype(F32))
    grad_h = keep[...] + got[...].astype(F32)
    full = grad_full[...] + norm_back(grad_h, normed, inverse, sums_in[0:1])
    grad_in[...] = reorder(full, s[0], n_dp).astype(BF16)


def add_kernel(s, one, two, out):
    out[...] = one[...] + two[...]


def output_kernel(n_dp, s, keep, got, x_one, vectors, out):
    value = x_one[...] + keep[...] + got[...].astype(F32) + vectors[3:4]
    out[...] = reorder(value, s[0], n_dp).astype(BF16)


def tie(*values):
    return lax.optimization_barrier(values)


class Links:
    def __init__(self, n_dp, n_tensor):
        self.n_dp, self.n_tensor = n_dp, n_tensor
        self.wide = n_dp > 8

    def move(self, value, target):
        pairs = []
        for d in range(self.n_dp):
            for t in range(self.n_tensor):
                to_d, to_t = target(d, t)
                pairs.append((d * self.n_tensor + t, to_d * self.n_tensor + to_t))
        return lax.ppermute(value, AXES, pairs)

    def chip(self, value):
        return self.move(value, lambda d, t: (d, t ^ 2))

    def core(self, value):
        return self.move(value, lambda d, t: (d, t ^ 1))

    def pair(self, value):
        return self.along(value, 1)

    def along(self, value, bits):
        return self.move(value, lambda d, t: (d ^ bits, t))

    def gather_tensor(self, rows):
        near = self.chip(rows)
        return rows, near, self.core(rows), self.core(near)

    def gather_wide(self, shard):
        blocks, place = lax.all_gather(shard, "dp", axis=0), lax.axis_index("dp")
        return jnp.take(blocks, lax.iota(jnp.int32, self.n_dp) ^ place, axis=0).reshape(-1, shard.shape[1])

    def scatter_wide(self, total):
        place = lax.axis_index("dp")
        blocks = total.reshape(self.n_dp, total.shape[0] // self.n_dp, total.shape[1])
        blocks = jnp.take(blocks, lax.iota(jnp.int32, self.n_dp) ^ place, axis=0).astype(F32)
        return unpack(lax.psum_scatter(blocks.reshape(total.shape), "dp", scatter_dimension=0, tiled=True))

    def steps(self):
        found, bit = [], 1
        while bit < self.n_dp and self.wide:
            found.append(lambda d, t, bit=bit: (d ^ bit, t))
            bit *= 2
        far = [] if self.wide else [lambda d, t: (d ^ 4, t)]
        return found + [lambda d, t: (d, t ^ 1), lambda d, t: (d, t ^ 2)] + far


def body(
    inputs,
    weight_query,
    weight_key,
    weight_value,
    weight_output,
    weight_hidden,
    weight_down,
    bias_query,
    bias_value,
    bias_hidden,
    bias_output,
    bias_final,
    gain_attention,
    gain_mixer,
    query_scale,
    lengths,
    cotangent,
    n_dp,
    n_tensor,
):
    links = Links(n_dp, n_tensor)
    wide = links.wide
    local_rows, width = inputs.shape
    all_rows = local_rows * n_tensor
    depth = width // n_dp
    local_width = weight_query.shape[1]
    both = 2 * local_width
    head_size = query_scale.shape[0]
    heads = local_width // head_size
    dp_index = lax.axis_index("dp")
    tensor_index = lax.axis_index("tensor")
    s = jnp.stack([dp_index, tensor_index, lengths[0]])
    product = 2 * all_rows * width * local_width
    mixed = 2 * all_rows * all_rows * local_width

    def run(name, kernel, outs, *arguments, **rest):
        return call(name, kernel, [shaped(*o) for o in outs], s, *arguments, **rest)

    def bind(kernel, *fixed):
        def bound(*refs):
            return kernel(*fixed, *refs)

        return bound

    packed = [((depth, both), BF16)]
    rows_low, rows_full = ((local_rows, width), BF16), ((local_rows, width), F32)
    split = [((all_rows // 2, width), BF16), ((all_rows // 2, width), F32)]
    part = ((all_rows, local_width), BF16)
    part_full = ((all_rows, local_width), F32)
    whole_rows = ((all_rows, width), BF16)
    weight = ((width, local_width), BF16)
    vector = ((8, width), F32)
    halves = [((width // 2, both), BF16)] * 2
    term = [pltpu.VMEM((width, both), BF16)]
    sems = [pltpu.SemaphoreType.DMA((n_dp,))]

    unit = SOFTPLUS_UNIT / jnp.sqrt(F32(head_size))
    scale_wide = jnp.tile(jax.nn.softplus(query_scale) * unit, heads)[None]
    slope = (jax.nn.sigmoid(query_scale) * unit)[None]
    loads = [pltpu.VMEM((depth, local_width), BF16)] * 2 + [pltpu.SemaphoreType.DMA((2,))]

    def apart(value):
        return pltpu.with_memory_space_constraint(value, pltpu.HBM)

    def pack_two(name, one, two):
        return run("pack_" + name, pack_kernel, packed, apart(one), apart(two), remote=2, scratch=loads)[0]

    own_qk = pack_two("qk", weight_query, weight_key)
    given = (gain_attention, gain_mixer, bias_output, bias_final, bias_query, bias_value, bias_hidden)
    scale_wide, slope = tie(scale_wide, slope)
    tall = (width // LANES, LANES)
    h_own, x_own, grad_own, vectors, biases = run(
        "prepare",
        bind(prepare_kernel, n_dp),
        [rows_low, rows_low, rows_low, vector, ((8, local_width), F32)],
        scale_wide,
        *(apart(v) for v in (inputs, cotangent, *(v.reshape(tall) for v in given))),
        remote=9,
        scratch=[pltpu.VMEM((local_rows, width), BF16)] * 2
        + [pltpu.VMEM(tall, F32)] * 7
        + [pltpu.SemaphoreType.DMA((9,))],
    )
    own_vo = pack_two("vo", weight_value, weight_output.T)
    own_hd = pack_two("hd", weight_hidden, weight_down.T)

    def stack(*blocks):
        rows = sum(block.shape[0] for block in blocks)
        return run("stack", stack_kernel, [((rows, both), BF16)], *blocks)[0]

    if wide:
        qk, vo, hd = (([links.gather_wide(own)], []) for own in (own_qk, own_vo, own_hd))
        h_one, grad_rows = links.gather_tensor(h_own), links.gather_tensor(grad_own)
    else:
        qk_one, qk_two = links.along(own_qk, 2), links.along(own_qk, 4)
        h_own, own_vo, own_hd, qk_one, qk_two = tie(h_own, own_vo, own_hd, qk_one, qk_two)
        h_chip = links.chip(h_own)
        qk_three = links.along(qk_two, 2)
        near_qk_pair = links.pair(stack(own_qk, qk_one))
        vo_one, vo_two = links.along(own_vo, 2), links.along(own_vo, 4)
        far_stack = stack(qk_two, qk_three)
        far_stack, near_qk_pair, h_chip, vo_one, vo_two = tie(far_stack, near_qk_pair, h_chip, vo_one, vo_two)
        h_one = h_own, h_chip, links.core(h_own), links.core(h_chip)
        far_qk_pair = links.pair(far_stack)
        vo_three = links.along(vo_two, 2)
        near_vo = stack(own_vo, vo_one)
        qk = [own_qk, qk_one, qk_two, qk_three], [near_qk_pair, far_qk_pair]
        h_one, qk, vo_three, near_vo = tie(h_one, qk, vo_three, near_vo)
        near_vo_pair = links.pair(near_vo)
        hd_one, hd_two = links.along(own_hd, 2), links.along(own_hd, 4)
        grad_chip = links.chip(grad_own)
    n_qk = len(qk[0]), len(qk[0]) + len(qk[1])
    q_raw, q_low, k_low, h_all, w_qk, turned = run(
        "attend",
        bind(attend_kernel, n_qk, depth, head_size),
        [
            part_full,
            part,
            part,
            whole_rows,
            ((width, both), BF16),
            ((heads, all_rows, all_rows), BF16),
        ],
        *h_one,
        biases,
        *qk[0],
        *qk[1],
        remote=n_qk[1],
        scratch=sems,
    )
    if not wide:
        turned, near_vo_pair, hd_one, hd_two, grad_chip = tie(turned, near_vo_pair, hd_one, hd_two, grad_chip)
        far_vo_pair = links.pair(stack(vo_two, vo_three))
        hd_three = links.along(hd_two, 2)
        grad_rows = grad_own, grad_chip, links.core(grad_own), links.core(grad_chip)
        vo = [own_vo, vo_one, vo_two, vo_three], [near_vo_pair, far_vo_pair]
        turned, vo, grad_rows, hd_three = tie(turned, vo, grad_rows, hd_three)
        near_hd_pair = links.pair(stack(own_hd, hd_one))
    n_vo = len(vo[0]), len(vo[0]) + len(vo[1])
    v_low, context, far, near, w_value, w_output = run(
        "context",
        bind(context_kernel, n_vo, depth, head_size),
        [part, part, *split, weight, weight],
        h_all,
        turned,
        biases,
        *vo[0],
        *vo[1],
        remote=n_vo[1],
        scratch=term + sems,
    )

    def core_half(far, near, *extra):
        got, *extra = tie(links.core(far), *extra)
        return list(run("middle", middle_kernel, [rows_low, rows_full], near, got)) + list(extra)

    if wide:
        send, keep = core_half(far, near)
        got = links.chip(send)
    else:
        far, near_hd_pair = tie(far, near_hd_pair)
        send, keep = core_half(far, near)
        got = links.chip(send)
        far_hd_pair = links.pair(stack(hd_two, hd_three))
        hd = [own_hd, hd_one, hd_two, hd_three], [near_hd_pair, far_hd_pair]
        got, hd = tie(got, hd)
    n_hd = len(hd[0]), len(hd[0]) + len(hd[1])
    x_one, h_two_own = run("second_norm", second_norm_kernel, [rows_full, rows_low], keep, got, x_own, vectors)
    h_two_chip = links.chip(h_two_own)
    grad_act, grad_all, w_hidden, w_down = run(
        "grad_act",
        bind(grad_act_kernel, n_hd, depth),
        [part_full, whole_rows, weight, weight],
        *grad_rows,
        *hd[0],
        *hd[1],
        remote=n_hd[1],
        scratch=term + sems,
    )
    h_two_chip, grad_act = tie(h_two_chip, grad_act)
    h_two = h_two_own, h_two_chip, links.core(h_two_own), links.core(h_two_chip)
    far, near, act, grad_pre, h_two_all = run(
        "hidden",
        hidden_kernel,
        [*split, part, part, whole_rows],
        *h_two,
        w_hidden,
        biases,
        grad_act,
    )
    cut = 3 * both // 5
    tall_sent = n_dp // 2 * depth
    terms = [((width, both), BF16)]
    if not wide:
        terms = [((tall_sent, c), BF16) for c in (cut, cut, both - cut, both - cut)]
    mix_far, mix_near, grad_b_hidden, *terms_hd = run(
        "down",
        bind(down_kernel, depth),
        [*split, ((1, local_width), F32), *terms],
        h_two_all,
        grad_all,
        act,
        grad_pre,
        w_down,
        scratch=term,
    )
    send, keep, terms_hd = core_half(far, near, terms_hd)
    got = links.chip(send)

    def first_send(terms):
        return [links.pair(terms[0]), links.along(terms[2], 2)]

    def first_sum(name, terms, got, given=()):
        rows = tall_sent // 2
        extra = 32 if given else 0
        outs = [((rows + extra, cut), BF16), ((rows, cut), F32), ((rows, both - cut), BF16), ((rows, both - cut), F32)]
        return run("first_" + name, first_sum_kernel, outs, terms[1], got[0], terms[3], got[1], *given)

    def second_send(sums):
        return [links.along(sums[0], 2), links.pair(sums[2])]

    def second_sum(name, sums, got, given=False):
        outs = packed + [((depth, both), F32)] + ([vector] if given else [])
        more = sums[:1] if given else []
        return run("second_" + name, second_sum_kernel, outs, sums[1], got[0], sums[3], got[1], *more)

    def owned(name, *parts):
        outs = [((depth, local_width), F32)] * 2
        return run("owned_" + name, bind(owned_kernel, len(parts) - 1), outs, *parts)

    if not wide:
        got_hd = first_send(terms_hd)
        got, got_hd = tie(got, got_hd)
    grad_mid_low, grad_mid, sums = run(
        "grad_middle",
        grad_middle_kernel,
        [rows_low, rows_full, vector],
        keep,
        got,
        x_one,
        grad_own,
        vectors,
    )
    if wide:
        grad_mid_rows = links.gather_tensor(grad_mid_low)
    else:
        grad_mid_chip = links.chip(grad_mid_low)
        sums_hd = first_sum("hd", terms_hd, got_hd)
        got_hd = second_send(sums_hd)
        grad_mid_chip, got_hd = tie(grad_mid_chip, got_hd)
        sent_hd, zero_hd = second_sum("hd", sums_hd, got_hd)
        grad_mid_rows = grad_mid_low, grad_mid_chip, links.core(grad_mid_low), links.core(grad_mid_chip)
    grad_mid_rows, mix_far = tie(grad_mid_rows, mix_far)
    mix_send, mix_keep = core_half(mix_far, mix_near)
    mix_got = links.chip(mix_send)
    grad_context, grad_value, _, *terms_vo = run(
        "grad_context",
        bind(grad_context_kernel, depth, head_size),
        [part, part, whole_rows, *terms],
        *grad_mid_rows,
        w_output,
        turned,
        context,
        h_all,
        scratch=term,
    )
    if not wide:
        got_vo = first_send(terms_vo)
        grad_context, sent_hd = tie(grad_context, sent_hd)
        part_hd = links.along(sent_hd, 4)
    grad_qk, sums_q = run(
        "grad_scores",
        bind(grad_scores_kernel, head_size),
        [((all_rows, both), BF16), ((8, local_width), F32)],
        turned,
        grad_context,
        v_low,
        q_low,
        k_low,
        q_raw,
        biases,
        scratch=[
            pltpu.VMEM((all_rows, local_width), F32),
            pltpu.VMEM((all_rows, local_width), F32),
            pltpu.VMEM((all_rows, all_rows), BF16),
        ],
    )
    if wide:
        grad_qk, mix_got = tie(grad_qk, mix_got)
    else:
        grad_qk, mix_got, part_hd, got_vo = tie(grad_qk, mix_got, part_hd, got_vo)
    terms_first = list(terms)
    if not wide:
        terms_first[0] = ((tall_sent + 32, cut), BF16)
    far, near, sums, *terms_qk = run(
        "grad_first",
        bind(grad_first_kernel, n_dp, depth),
        [*split, vector, *terms_first],
        grad_qk,
        w_qk,
        grad_value,
        w_value,
        h_all,
        sums,
        sums_q,
        grad_b_hidden,
        slope,
        scratch=term,
    )
    def exchange(value, step):
        return run("add", add_kernel, [vector], value, links.move(value, step))[0]

    total = sums
    if wide:
        send, keep = core_half(far, near)
        got = links.chip(send)
    else:
        got_qk = first_send(terms_qk)
        far, *got_vo = tie(far, *got_vo)
        sums_vo = first_sum("vo", terms_vo, got_vo)
        send, keep, *sums_vo = core_half(far, near, *sums_vo)
        got_vo = second_send(sums_vo)
        got = links.chip(send)
        (output,) = run("output", bind(output_kernel, n_dp), [rows_low], mix_keep, mix_got, x_one, vectors)
        grad_hidden, grad_down = owned("hd", zero_hd, part_hd)
        got_qk, got, output, grad_hidden = tie(got_qk, got, output, grad_hidden)
        got_qk, got_vo = tie(got_qk, got_vo)
        sums_qk = first_sum("qk", terms_qk, got_qk, [sums])
        got_qk = second_send(sums_qk)
        (grad_in,) = run("last", bind(last_kernel, n_dp), [rows_low], keep, got, x_own, grad_mid, vectors)
        got_qk, grad_in = tie(got_qk, grad_in)
        sent_vo, zero_vo = second_sum("vo", sums_vo, got_vo)
        part_vo = links.along(sent_vo, 4)
        sent_qk, zero_qk, total = second_sum("qk", sums_qk, got_qk, True)
        far_qk = links.along(sent_qk, 4)
        zero_vo, total = tie(zero_vo, total)
    if wide:
        (grad_in,) = run("last", bind(last_kernel, n_dp), [rows_low], keep, got, x_own, grad_mid, vectors)
    if wide:
        (output,) = run("output", bind(output_kernel, n_dp), [rows_low], mix_keep, mix_got, x_one, vectors)
    steps = links.steps()
    for step in steps[:-1]:
        total = exchange(total, step)
    moved = links.move(total, steps[-1])
    if not wide:
        grad_query, grad_key = owned("qk", zero_qk, far_qk)
        moved, grad_query = tie(moved, grad_query)
    tall_vector = (tall, F32)
    *totals, total_scale = run(
        "total", total_kernel, [tall_vector] * 7 + [((1, head_size), F32)], total, moved
    )
    totals = [v.reshape(width) for v in totals]
    if wide:
        grad_hidden, grad_down = links.scatter_wide(terms_hd[0])
        grad_output_v, grad_output_o = links.scatter_wide(terms_vo[0])
        grad_query, grad_key = links.scatter_wide(terms_qk[0])
    else:
        grad_output_v, grad_output_o = owned("vo", zero_vo, part_vo)
    return (
        output,
        grad_in,
        grad_query,
        grad_key,
        grad_output_v,
        grad_output_o.T,
        grad_hidden,
        grad_down.T,
        totals[0],
        totals[1],
        totals[2],
        totals[5],
        totals[4],
        totals[6],
        totals[3],
        total_scale.reshape(head_size),
    )


def solution(mesh):
    n_dp, n_tensor = mesh.shape["dp"], mesh.shape["tensor"]

    def local(*arguments):
        return body(*arguments, n_dp, n_tensor)

    rows = P(("dp", "tensor"), None)
    into, out_of = P("dp", "tensor"), P("tensor", "dp")
    return jax.shard_map(
        local,
        mesh=mesh,
        in_specs=(rows, into, into, into, out_of, into, out_of, *[P()] * 8, P("dp"), rows),
        out_specs=(rows, rows, into, into, into, out_of, into, out_of, *[P()] * 8),
        check_vma=False,
    )
```

```python
import jax
import jax.numpy as jnp
from jax import lax
from jax.experimental import pallas as pl
from jax.experimental.pallas import tpu as pltpu
from jax.sharding import PartitionSpec as P

EPSILON = 1e-06
SOFTPLUS_UNIT = 1.442695041
AXES = ("dp", "tensor")
F32 = jnp.float32
BF16 = jnp.bfloat16
LANES = 128
TENSOR_ORDER = (0, 2, 1, 3)
NN, NT, TN = ((1,), (0,)), ((1,), (1,)), ((0,), (0,))


def dot(left, right, dims=NN):
    return lax.dot_general(left, right, (dims, ((), ())), preferred_element_type=F32)


def shaped(shape, kind):
    return jax.ShapeDtypeStruct(shape, kind)


def call(name, kernel, outs, scalars, *arguments, flops=1e6, scratch=(), limit=12, remote=0):
    space = pl.BlockSpec(memory_space=pltpu.VMEM)
    apart = pl.BlockSpec(memory_space=pltpu.HBM)
    moved = sum(a.size * a.dtype.itemsize for a in (*arguments, *outs))
    return pl.pallas_call(
        kernel,
        name=name,
        out_shape=outs,
        in_specs=[pl.BlockSpec(memory_space=pltpu.SMEM)]
        + [space] * (len(arguments) - remote)
        + [apart] * remote,
        out_specs=[space] * len(outs),
        scratch_shapes=scratch,
        compiler_params=pltpu.CompilerParams(vmem_limit_bytes=limit << 20),
        cost_estimate=pl.CostEstimate(flops=int(flops), bytes_accessed=moved, transcendentals=0),
    )(scalars, *arguments)


def pack(first, second):
    main = first.shape[1] // LANES * LANES
    return jnp.concatenate([first[:, :main], second[:, :main], first[:, main:], second[:, main:]], axis=1)


def unpack(both):
    width = both.shape[1] // 2
    main = width // LANES * LANES
    edge = main * 2 + width - main
    first = jnp.concatenate([both[:, :main], both[:, 2 * main : edge]], axis=1)
    rest = both[:, 2 * main :].astype(F32)[:, width - main :].astype(both.dtype)
    second = jnp.concatenate([both[:, main : 2 * main], rest], axis=1)
    return first, second


def reorder(value, place, n_dp):
    width = value.shape[1]
    lane = lax.broadcasted_iota(jnp.int32, (1, width), 1)
    span = width // n_dp
    bit = 1
    while bit < n_dp:
        low = lax.rem(lane, 2 * span) < span
        other = jnp.where(low, pltpu.roll(value, width - span, 1), pltpu.roll(value, span, 1))
        value = jnp.where((place & bit) != 0, other, value)
        bit, span = 2 * bit, 2 * span
    return value


def row_mean(value):
    return jnp.sum(value, axis=1, keepdims=True) * (1.0 / value.shape[1])


def normalize(value):
    inverse = lax.rsqrt(row_mean(value * value) + EPSILON)
    return value * inverse, inverse


def norm_back(grad_normed, normed, inverse, gain):
    scaled = grad_normed * gain
    return inverse * (scaled - normed * row_mean(scaled * normed))


def load(sources, targets, sem):
    copies = [pltpu.make_async_copy(a, b, sem.at[k]) for k, (a, b) in enumerate(zip(sources, targets))]
    for copy in copies:
        copy.start()
    for copy in copies:
        copy.wait()


def pack_kernel(s, *refs):
    sources, outs, loaded = refs[:6], refs[6:9], refs[9:15]
    load(sources, loaded, refs[15])
    for k, out in enumerate(outs):
        out[...] = pack(loaded[2 * k][...].astype(F32), loaded[2 * k + 1][...].astype(F32)).astype(BF16)


def row_of(ref):
    return jnp.concatenate([ref[k : k + 1] for k in range(ref.shape[0])], axis=1)


def prepare_kernel(n_dp, s, scale, *refs):
    sources, (h, x_own, grad, vectors, biases) = refs[:9], refs[9:14]
    x, cotangent, *given = refs[14:23]
    load(sources, refs[14:23], refs[23])
    mine, place, length = s[0], s[1], s[2]
    value = reorder(x[...].astype(F32), mine, n_dp)
    stacked = jnp.concatenate([row_of(given[k]) for k in (0, 1, 2, 3, 4, 5, 6, 6)], axis=0)
    width = biases.shape[1]
    slices = stacked[:, :width]
    for number in range(1, stacked.shape[1] // width):
        slices = jnp.where(place == number, stacked[:, number * width : (number + 1) * width], slices)
    biases[...] = slices
    biases[7:8] = scale[...]
    stacked = reorder(stacked, mine, n_dp)
    normed, _ = normalize(value)
    h[...] = (normed * stacked[0:1]).astype(BF16)
    x_own[...] = value.astype(BF16)
    rows = value.shape[0]
    row = lax.broadcasted_iota(jnp.int32, value.shape, 0) + place * rows
    g = jnp.where(row < length, reorder(cotangent[...].astype(F32), mine, n_dp), 0.0)
    grad[...] = g.astype(BF16)
    vectors[...] = stacked
    vectors[4:5] = jnp.sum(g, axis=0, keepdims=True)


def join(pieces, out):
    rows = pieces[0].shape[0]
    for number, piece in enumerate(pieces):
        out[pl.ds(number * rows, rows)] = piece[...]


def tiles(rows, body, size=128):
    def step(m, carry):
        body(pl.ds(pl.multiple_of(m * size, size), size), m)
        return carry

    lax.fori_loop(0, rows // size, step, 0)


def positions(shape, axis, place, local, offset=0):
    row = lax.broadcasted_iota(jnp.int32, shape, axis) + offset
    shift = local.bit_length() - 1
    block = row >> shift
    turned = ((block & 1) << 1) | (block >> 1)
    return ((place ^ turned) << shift) + (row & (local - 1))


def fetch(even, odd, out, depth, sem):
    copies = []
    if not odd:
        copies.append(pltpu.make_async_copy(even[0], out, sem.at[0]))
    else:
        for start, blocks in enumerate((even, odd)):
            row = start * depth
            for block in blocks:
                for k in range(block.shape[0] // depth):
                    source, target = block.at[pl.ds(k * depth, depth)], out.at[pl.ds(row, depth)]
                    copies.append(pltpu.make_async_copy(source, target, sem.at[len(copies)]))
                    row += 2 * depth
    for one in copies:
        one.start()
    return copies


def stack_kernel(s, *refs):
    join(refs[:-1], refs[-1])


def of_head(value, number, head_size):
    lanes = lax.broadcasted_iota(jnp.int32, (1, value.shape[1]), 1) // head_size
    return jnp.where(lanes == number, value, jnp.zeros((), value.dtype))


def attend_kernel(counts, depth, head_size, s, p0, p1, p2, p3, biases, *refs):
    even, odd = refs[: counts[0]], refs[counts[0] : counts[1]]
    q_raw, q_low, k_low, h, weight, turned, sem = refs[counts[1] :]
    copies = fetch(even, odd, weight, depth, sem)
    join((p0, p1, p2, p3), h)
    for copy in copies:
        copy.wait()
    first, second = unpack(dot(h[...], weight[...]))
    first = first + biases[4:5]
    q_raw[...] = first
    q_low[...] = (first * biases[7:8]).astype(BF16)
    k_low[...] = second.astype(BF16)
    place, length = s[1], s[2]
    rows, local = q_low.shape[0], p0.shape[0]
    key_place = positions((rows, 1), 0, place, local)
    last = jnp.minimum(positions((1, rows), 1, place, local), length - 1)

    def head(number, carry):
        score = dot(k_low[...], of_head(q_low[...], number, head_size), NT)
        score = jnp.where(key_place <= last, score, -1e30)
        raised = jnp.exp(score - jnp.max(score, axis=0, keepdims=True))
        share = 1.0 / jnp.sum(raised, axis=0, keepdims=True)
        turned[number] = (raised * share).astype(BF16)
        return carry

    for number in range(turned.shape[0]):
        head(number, 0)


def mixed_heads(turned, value, head_size, dims):
    total = None
    for number in range(turned.shape[0]):
        term = dot(turned[number], of_head(value, number, head_size), dims)
        total = term if total is None else total + term
    return total


def split_weight(weight, one, two):
    one[...], two[...] = unpack(weight[...])


def context_kernel(counts, depth, head_size, s, h, turned, biases, *refs):
    even, odd = refs[: counts[0]], refs[counts[0] : counts[1]]
    v_low, context, far, near, w_value, w_output, weight, sem = refs[counts[1] :]
    for copy in fetch(even, odd, weight, depth, sem):
        copy.wait()
    split_weight(weight, w_value, w_output)
    v_low[...] = (dot(h[...], w_value[...]) + biases[5:6]).astype(BF16)
    context[...] = mixed_heads(turned, v_low[...], head_size, TN).astype(BF16)
    split_product(context, w_output, far, near)


def split_product(left, right, far, near, extra=None, along=None):
    half, total = near.shape[0], None
    for start, out in ((half, far), (0, near)):
        at = pl.ds(start, half)
        value = dot(left[at], right[...], NT)
        if extra is not None:
            value = value + dot(extra[0][at], extra[1][...], NT)
        out[...] = value.astype(out.dtype)
        if along is not None:
            summed = jnp.sum(value * along[at].astype(F32), axis=0, keepdims=True)
            total = summed if total is None else total + summed
    return total


def middle_kernel(s, near, got, send, keep):
    rows = send.shape[0]
    send[...] = (near[rows:] + got[rows:].astype(F32)).astype(BF16)
    keep[...] = near[:rows] + got[:rows].astype(F32)


def second_norm_kernel(s, keep, got, x_own, vectors, x_one, h):
    value = x_own[...].astype(F32) + keep[...] + got[...].astype(F32) + vectors[2:3]
    x_one[...] = value
    normed, _ = normalize(value)
    h[...] = (normed * vectors[1:2]).astype(BF16)


def grad_act_kernel(counts, depth, s, p0, p1, p2, p3, *refs):
    even, odd = refs[: counts[0]], refs[counts[0] : counts[1]]
    grad_act, g, w_hidden, w_down, weight, sem = refs[counts[1] :]
    copies = fetch(even, odd, weight, depth, sem)
    join((p0, p1, p2, p3), g)
    for copy in copies:
        copy.wait()
    split_weight(weight, w_hidden, w_down)
    grad_act[...] = dot(g[...], w_down[...])


def hidden_kernel(s, p0, p1, p2, p3, w_hidden, biases, grad_act, out_far, out_near, act, grad_pre, h):
    join((p0, p1, p2, p3), h)
    pre = dot(h[...], w_hidden[...]) + biases[6:7]
    sigma = jax.nn.sigmoid(pre)
    act[...] = (pre * sigma).astype(BF16)
    grad_pre[...] = (grad_act[...] * (sigma * (1.0 + pre * (1.0 - sigma)))).astype(BF16)
    split_product(grad_pre, w_hidden, out_far, out_near)


PAIR_FIRST = (3, 1, 2, 0)
RING_SENT, RING_KEPT = ((3, 1), (1, 1), (3, 0), (1, 0)), ((2, 1), (0, 1), (2, 0), (0, 0))


def spread_terms(term, outs, depth):
    if len(outs) == 1:
        outs[0][...] = term[...]
        return
    pair_sent, pair_kept, ring_sent, ring_kept = outs
    cut = pair_kept.shape[1]

    def copy(out, at, block, columns):
        out[pl.ds(at * depth, depth)] = term[pl.ds(block * depth, depth), columns]

    for at, j in enumerate(PAIR_FIRST):
        copy(pair_sent, at, 2 * j + 1, slice(0, cut))
        copy(pair_kept, at, 2 * j, slice(0, cut))
    for at in range(4):
        (j, i), (k, m) = RING_SENT[at], RING_KEPT[at]
        copy(ring_sent, at, 2 * j + i, slice(cut, None))
        copy(ring_kept, at, 2 * k + m, slice(cut, None))


def two_terms(left_one, right_one, left_two, right_two, term):
    first = dot(left_one[...], right_one[...], TN)
    second = dot(left_two[...], right_two[...], TN)
    term[...] = pack(first, second).astype(BF16)


def down_kernel(depth, s, h, g, act, grad_pre, w_down, far, near, b_hidden, *refs):
    *outs, term = refs
    two_terms(h, grad_pre, g, act, term)
    spread_terms(term, outs, depth)
    b_hidden[...] = jnp.sum(grad_pre[...].astype(F32), axis=0, keepdims=True)
    split_product(act, w_down, far, near)


def owned_kernel(n_got, s, keep, *refs):
    total = keep[...]
    for got in refs[:n_got]:
        total = total + got[pl.ds(0, total.shape[0])].astype(F32)
    refs[n_got][...], refs[n_got + 1][...] = unpack(total)


def grad_middle_kernel(s, keep, got, x_one, grad, vectors, grad_low, grad_full, sums):
    normed, inverse = normalize(x_one[...])
    grad_h = keep[...] + got[...].astype(F32)
    full = grad[...].astype(F32) + norm_back(grad_h, normed, inverse, vectors[1:2])
    grad_full[...] = full
    grad_low[...] = full.astype(BF16)
    sums[...] = vectors[...]
    sums[5:6] = jnp.sum(full, axis=0, keepdims=True)
    sums[6:7] = jnp.sum(grad_h * normed, axis=0, keepdims=True)


def grad_context_kernel(depth, head_size, s, p0, p1, p2, p3, w_output, turned, context, h, *refs):
    grad_context, grad_value, gm, *outs, term = refs
    join((p0, p1, p2, p3), gm)
    grad_context[...] = dot(gm[...], w_output[...]).astype(BF16)
    grad_value[...] = mixed_heads(turned, grad_context[...], head_size, NN).astype(BF16)
    two_terms(h, grad_value, gm, context, term)
    spread_terms(term, outs, depth)


def grad_scores_kernel(head_size, s, turned, grad_context, v_low, q_low, k_low, q_raw, biases, *refs):
    grad_qk, sums, grad_q, grad_k, scores = refs
    rows = q_low.shape[0]
    grad_q[...] = jnp.zeros_like(grad_q)
    grad_k[...] = jnp.zeros_like(grad_k)

    def head(number, carry):
        grad_chance = dot(v_low[...], of_head(grad_context[...], number, head_size), NT)
        chance = turned[number].astype(F32)
        product = chance * grad_chance
        center = jnp.sum(product, axis=0, keepdims=True)
        scores[...] = (product - chance * center).astype(BF16)
        grad_q[...] += dot(scores[...], of_head(k_low[...], number, head_size), TN)
        grad_k[...] += dot(scores[...], of_head(q_low[...], number, head_size))
        return carry

    for number in range(turned.shape[0]):
        head(number, 0)
    low = grad_q[...].astype(BF16).astype(F32)
    sums[0:1] = jnp.sum(low * q_raw[...], axis=0, keepdims=True)
    low = (low * biases[7:8]).astype(BF16).astype(F32)
    grad_qk[...] = pack(low, grad_k[...]).astype(BF16)
    sums[1:2] = jnp.sum(low, axis=0, keepdims=True)


def grad_first_kernel(
    n_dp, depth, s, grad_qk, w_qk, grad_value, w_value, h, sums_in, sums_q, b_hidden, slope, *refs
):
    far, near, sums, *outs, term = refs
    term[...] = dot(h[...], grad_qk[...], TN).astype(BF16)
    spread_terms(term, outs, depth)
    mine, place = s[0], s[1]
    gained = split_product(grad_qk, w_qk, far, near, (grad_value, w_value), h) / sums_in[0:1]
    row = lax.broadcasted_iota(jnp.int32, sums.shape, 0)
    sums[...] = reorder(jnp.where(row == 7, gained, sums_in[...]), mine, n_dp)
    sums[0:4] = jnp.zeros((4, sums.shape[1]), F32)
    local_width, head_size = sums_q.shape[1], slope.shape[1]
    b_value = jnp.sum(grad_value[...].astype(F32), axis=0, keepdims=True)
    share = jnp.concatenate([sums_q[1:2], b_value, b_hidden[...]], axis=0)
    for number in range(sums.shape[1] // local_width):

        @pl.when(place == number)
        def _():
            sums[0:3, number * local_width : (number + 1) * local_width] = share

    scale = sums_q[0:1]
    total = scale[:, :head_size]
    for number in range(1, local_width // head_size):
        total = total + scale[:, number * head_size : (number + 1) * head_size]
    sums[3:4, :head_size] = total * slope[...]
    if len(outs) > 1:
        outs[0][pl.ds(4 * depth, 32)] = fold(sums[...], outs[0].shape[1])


def fold(vectors, width):
    part = vectors.shape[1] // 4
    rows = jnp.concatenate([vectors[:, k * part : (k + 1) * part] for k in range(4)], axis=0)
    return jnp.concatenate([rows, jnp.zeros((32, width - part), F32)], axis=1).astype(BF16)


def unfold(rows, part):
    return jnp.concatenate([rows[8 * k : 8 * k + 8, :part] for k in range(4)], axis=1)


def first_sum_kernel(s, pair_kept, pair_got, ring_kept, ring_got, *refs):
    *given, pair_out, pair_mid, ring_out, ring_mid = refs
    half = pair_mid.shape[0]
    value = pair_kept[...].astype(F32) + pair_got[pl.ds(0, 2 * half)].astype(F32)
    pair_out[pl.ds(0, half)] = value[:half].astype(BF16)
    pair_mid[...] = value[half:]
    value = ring_kept[...].astype(F32) + ring_got[...].astype(F32)
    ring_out[...] = value[:half].astype(BF16)
    ring_mid[...] = value[half:]
    if given:
        low = fold(given[0][...], pair_out.shape[1]).astype(F32) + pair_got[pl.ds(2 * half, 32)].astype(F32)
        pair_out[pl.ds(half, 32)] = low.astype(BF16)


def second_sum_kernel(s, pair_mid, pair_got, ring_mid, ring_got, *refs):
    half, depth, cut = pair_mid.shape[0], pair_mid.shape[0] // 2, pair_mid.shape[1]
    given, out, zero = refs[: len(refs) // 3], refs[len(refs) // 3], refs[len(refs) // 3 + 1]
    pair = pair_mid[...] + pair_got[pl.ds(0, half)].astype(F32)
    ring = ring_mid[...] + ring_got[...].astype(F32)
    out[:, :cut], out[:, cut:] = pair[:depth].astype(BF16), ring[:depth].astype(BF16)
    zero[:, :cut], zero[:, cut:] = pair[depth:], ring[depth:]
    if given:
        at, vectors = pl.ds(half, 32), refs[-1]
        vectors[...] = unfold(given[0][at].astype(F32) + pair_got[at].astype(F32), vectors.shape[1] // 4)


def total_kernel(s, one, two, *outs):
    total = one[...] + two[...]
    for out, row in zip(outs[:7], (0, 1, 2, 6, 4, 5, 7)):
        for k in range(out.shape[0]):
            out[k : k + 1] = total[row : row + 1, k * LANES : (k + 1) * LANES]
    outs[7][...] = total[3:4, : outs[7].shape[1]]


def last_kernel(n_dp, s, keep, got, x_own, grad_full, sums_in, grad_in):
    normed, inverse = normalize(x_own[...].astype(F32))
    grad_h = keep[...] + got[...].astype(F32)
    full = grad_full[...] + norm_back(grad_h, normed, inverse, sums_in[0:1])
    grad_in[...] = reorder(full, s[0], n_dp).astype(BF16)


def add_kernel(s, one, two, out):
    out[...] = one[...] + two[...]


def output_kernel(n_dp, s, keep, got, x_one, vectors, out):
    value = x_one[...] + keep[...] + got[...].astype(F32) + vectors[3:4]
    out[...] = reorder(value, s[0], n_dp).astype(BF16)


def tie(*values):
    return lax.optimization_barrier(values)


class Links:
    def __init__(self, n_dp, n_tensor):
        self.n_dp, self.n_tensor = n_dp, n_tensor
        self.wide = n_dp > 8

    def move(self, value, target):
        pairs = []
        for d in range(self.n_dp):
            for t in range(self.n_tensor):
                to_d, to_t = target(d, t)
                pairs.append((d * self.n_tensor + t, to_d * self.n_tensor + to_t))
        return lax.ppermute(value, AXES, pairs)

    def chip(self, value):
        return self.move(value, lambda d, t: (d, t ^ 2))

    def core(self, value):
        return self.move(value, lambda d, t: (d, t ^ 1))

    def pair(self, value):
        return self.along(value, 1)

    def along(self, value, bits):
        return self.move(value, lambda d, t: (d ^ bits, t))

    def gather_tensor(self, rows):
        near = self.chip(rows)
        return rows, near, self.core(rows), self.core(near)

    def gather_wide(self, shard):
        blocks, place = lax.all_gather(shard, "dp", axis=0), lax.axis_index("dp")
        return jnp.take(blocks, lax.iota(jnp.int32, self.n_dp) ^ place, axis=0).reshape(-1, shard.shape[1])

    def scatter_wide(self, total):
        place = lax.axis_index("dp")
        blocks = total.reshape(self.n_dp, total.shape[0] // self.n_dp, total.shape[1])
        blocks = jnp.take(blocks, lax.iota(jnp.int32, self.n_dp) ^ place, axis=0).astype(F32)
        return unpack(lax.psum_scatter(blocks.reshape(total.shape), "dp", scatter_dimension=0, tiled=True))

    def steps(self):
        found, bit = [], 1
        while bit < self.n_dp and self.wide:
            found.append(lambda d, t, bit=bit: (d ^ bit, t))
            bit *= 2
        far = [] if self.wide else [lambda d, t: (d ^ 4, t)]
        return found + [lambda d, t: (d, t ^ 1), lambda d, t: (d, t ^ 2)] + far


def body(
    inputs,
    weight_query,
    weight_key,
    weight_value,
    weight_output,
    weight_hidden,
    weight_down,
    bias_query,
    bias_value,
    bias_hidden,
    bias_output,
    bias_final,
    gain_attention,
    gain_mixer,
    query_scale,
    lengths,
    cotangent,
    n_dp,
    n_tensor,
):
    links = Links(n_dp, n_tensor)
    wide = links.wide
    local_rows, width = inputs.shape
    all_rows = local_rows * n_tensor
    depth = width // n_dp
    local_width = weight_query.shape[1]
    both = 2 * local_width
    head_size = query_scale.shape[0]
    heads = local_width // head_size
    dp_index = lax.axis_index("dp")
    tensor_index = lax.axis_index("tensor")
    s = jnp.stack([dp_index, tensor_index, lengths[0]])
    product = 2 * all_rows * width * local_width
    mixed = 2 * all_rows * all_rows * local_width

    def run(name, kernel, outs, *arguments, **rest):
        return call(name, kernel, [shaped(*o) for o in outs], s, *arguments, **rest)

    def bind(kernel, *fixed):
        def bound(*refs):
            return kernel(*fixed, *refs)

        return bound

    packed = [((depth, both), BF16)]
    rows_low, rows_full = ((local_rows, width), BF16), ((local_rows, width), F32)
    split = [((all_rows // 2, width), BF16), ((all_rows // 2, width), F32)]
    part = ((all_rows, local_width), BF16)
    part_full = ((all_rows, local_width), F32)
    whole_rows = ((all_rows, width), BF16)
    weight = ((width, local_width), BF16)
    vector = ((8, width), F32)
    halves = [((width // 2, both), BF16)] * 2
    term = [pltpu.VMEM((width, both), BF16)]
    sems = [pltpu.SemaphoreType.DMA((n_dp,))]

    unit = SOFTPLUS_UNIT / jnp.sqrt(F32(head_size))
    scale_wide = jnp.tile(jax.nn.softplus(query_scale) * unit, heads)[None]
    slope = (jax.nn.sigmoid(query_scale) * unit)[None]
    def apart(value):
        return pltpu.with_memory_space_constraint(value, pltpu.HBM)

    weights = (weight_query, weight_key, weight_value, weight_output.T, weight_hidden, weight_down.T)
    own_qk, own_vo, own_hd = run(
        "pack",
        pack_kernel,
        packed * 3,
        *(apart(w) for w in weights),
        remote=6,
        scratch=[pltpu.VMEM((depth, local_width), BF16)] * 6 + [pltpu.SemaphoreType.DMA((6,))],
    )
    given = (gain_attention, gain_mixer, bias_output, bias_final, bias_query, bias_value, bias_hidden)
    scale_wide, slope = tie(scale_wide, slope)
    tall = (width // LANES, LANES)
    h_own, x_own, grad_own, vectors, biases = run(
        "prepare",
        bind(prepare_kernel, n_dp),
        [rows_low, rows_low, rows_low, vector, ((8, local_width), F32)],
        scale_wide,
        *(apart(v) for v in (inputs, cotangent, *(v.reshape(tall) for v in given))),
        remote=9,
        scratch=[pltpu.VMEM((local_rows, width), BF16)] * 2
        + [pltpu.VMEM(tall, F32)] * 7
        + [pltpu.SemaphoreType.DMA((9,))],
    )

    def stack(*blocks):
        rows = sum(block.shape[0] for block in blocks)
        return run("stack", stack_kernel, [((rows, both), BF16)], *blocks)[0]

    if wide:
        qk, vo, hd = (([links.gather_wide(own)], []) for own in (own_qk, own_vo, own_hd))
        h_one, grad_rows = links.gather_tensor(h_own), links.gather_tensor(grad_own)
    else:
        qk_one, qk_two = links.along(own_qk, 2), links.along(own_qk, 4)
        hd_pair = links.pair(own_hd)
        h_own, own_vo, own_hd, qk_one, qk_two, hd_pair = tie(h_own, own_vo, own_hd, qk_one, qk_two, hd_pair)
        h_chip = links.chip(h_own)
        qk_three = links.along(qk_two, 2)
        near_qk_pair = links.pair(stack(own_qk, qk_one))
        vo_two, vo_pair = links.along(own_vo, 4), links.pair(own_vo)
        far_stack = stack(qk_two, qk_three)
        far_stack, near_qk_pair = tie(far_stack, near_qk_pair)
        h_chip, vo_two, vo_pair, own_vo = tie(h_chip, vo_two, vo_pair, own_vo)
        h_one = h_own, h_chip, links.core(h_own), links.core(h_chip)
        far_qk_pair = links.pair(far_stack)
        vo_one, vo_three = links.along(own_vo, 2), links.along(vo_two, 2)
        qk = [own_qk, qk_one, qk_two, qk_three], [near_qk_pair, far_qk_pair]
        h_one, qk, vo_three, own_hd = tie(h_one, qk, vo_three, own_hd)
        near_vo_pair = links.pair(vo_one)
        hd_one, hd_two = links.along(own_hd, 2), links.along(own_hd, 4)
        grad_chip = links.chip(grad_own)
    n_qk = len(qk[0]), len(qk[0]) + len(qk[1])
    q_raw, q_low, k_low, h_all, w_qk, turned = run(
        "attend",
        bind(attend_kernel, n_qk, depth, head_size),
        [
            part_full,
            part,
            part,
            whole_rows,
            ((width, both), BF16),
            ((heads, all_rows, all_rows), BF16),
        ],
        *h_one,
        biases,
        *qk[0],
        *qk[1],
        remote=n_qk[1],
        scratch=sems,
    )
    if not wide:
        turned, near_vo_pair, hd_one, hd_two, grad_chip = tie(turned, near_vo_pair, hd_one, hd_two, grad_chip)
        far_vo_pair = links.pair(stack(vo_two, vo_three))
        hd_three = links.along(hd_two, 2)
        grad_rows = grad_own, grad_chip, links.core(grad_own), links.core(grad_chip)
        vo = [own_vo, vo_one, vo_two, vo_three], [vo_pair, near_vo_pair, far_vo_pair]
        turned, vo, grad_rows = tie(turned, vo, grad_rows)
        near_hd_pair = links.pair(hd_one)
    n_vo = len(vo[0]), len(vo[0]) + len(vo[1])
    v_low, context, far, near, w_value, w_output = run(
        "context",
        bind(context_kernel, n_vo, depth, head_size),
        [part, part, *split, weight, weight],
        h_all,
        turned,
        biases,
        *vo[0],
        *vo[1],
        remote=n_vo[1],
        scratch=term + sems,
    )

    def core_half(far, near, *extra):
        got, *extra = tie(links.core(far), *extra)
        return list(run("middle", middle_kernel, [rows_low, rows_full], near, got)) + list(extra)

    if wide:
        send, keep = core_half(far, near)
        got = links.chip(send)
    else:
        far, near_hd_pair, hd_three = tie(far, near_hd_pair, hd_three)
        send, keep = core_half(far, near)
        got = links.chip(send)
        far_hd_pair = links.pair(stack(hd_two, hd_three))
        hd = [own_hd, hd_one, hd_two, hd_three], [hd_pair, near_hd_pair, far_hd_pair]
        got, hd = tie(got, hd)
    n_hd = len(hd[0]), len(hd[0]) + len(hd[1])
    x_one, h_two_own = run("second_norm", second_norm_kernel, [rows_full, rows_low], keep, got, x_own, vectors)
    h_two_chip = links.chip(h_two_own)
    grad_act, grad_all, w_hidden, w_down = run(
        "grad_act",
        bind(grad_act_kernel, n_hd, depth),
        [part_full, whole_rows, weight, weight],
        *grad_rows,
        *hd[0],
        *hd[1],
        remote=n_hd[1],
        scratch=term + sems,
    )
    h_two_chip, grad_act = tie(h_two_chip, grad_act)
    h_two = h_two_own, h_two_chip, links.core(h_two_own), links.core(h_two_chip)
    far, near, act, grad_pre, h_two_all = run(
        "hidden",
        hidden_kernel,
        [*split, part, part, whole_rows],
        *h_two,
        w_hidden,
        biases,
        grad_act,
    )
    cut = 3 * both // 5
    tall_sent = n_dp // 2 * depth
    terms = [((width, both), BF16)]
    if not wide:
        terms = [((tall_sent, c), BF16) for c in (cut, cut, both - cut, both - cut)]
    mix_far, mix_near, grad_b_hidden, *terms_hd = run(
        "down",
        bind(down_kernel, depth),
        [*split, ((1, local_width), F32), *terms],
        h_two_all,
        grad_all,
        act,
        grad_pre,
        w_down,
        scratch=term,
    )
    send, keep, terms_hd = core_half(far, near, terms_hd)
    got = links.chip(send)

    def first_send(terms):
        return [links.pair(terms[0]), links.along(terms[2], 2)]

    def first_sum(name, terms, got, given=()):
        rows = tall_sent // 2
        extra = 32 if given else 0
        outs = [((rows + extra, cut), BF16), ((rows, cut), F32), ((rows, both - cut), BF16), ((rows, both - cut), F32)]
        return run("first_" + name, first_sum_kernel, outs, terms[1], got[0], terms[3], got[1], *given)

    def second_send(sums):
        return [links.along(sums[0], 2), links.pair(sums[2])]

    def second_sum(name, sums, got, given=False):
        outs = packed + [((depth, both), F32)] + ([vector] if given else [])
        more = sums[:1] if given else []
        return run("second_" + name, second_sum_kernel, outs, sums[1], got[0], sums[3], got[1], *more)

    def owned(name, *parts):
        outs = [((depth, local_width), F32)] * 2
        return run("owned_" + name, bind(owned_kernel, len(parts) - 1), outs, *parts)

    if not wide:
        got_hd = first_send(terms_hd)
        got, got_hd = tie(got, got_hd)
    grad_mid_low, grad_mid, sums = run(
        "grad_middle",
        grad_middle_kernel,
        [rows_low, rows_full, vector],
        keep,
        got,
        x_one,
        grad_own,
        vectors,
    )
    if wide:
        grad_mid_rows = links.gather_tensor(grad_mid_low)
    else:
        grad_mid_chip = links.chip(grad_mid_low)
        sums_hd = first_sum("hd", terms_hd, got_hd)
        got_hd = second_send(sums_hd)
        grad_mid_chip, got_hd = tie(grad_mid_chip, got_hd)
        sent_hd, zero_hd = second_sum("hd", sums_hd, got_hd)
        grad_mid_rows = grad_mid_low, grad_mid_chip, links.core(grad_mid_low), links.core(grad_mid_chip)
    grad_mid_rows, mix_far = tie(grad_mid_rows, mix_far)
    mix_send, mix_keep = core_half(mix_far, mix_near)
    mix_got = links.chip(mix_send)
    grad_context, grad_value, _, *terms_vo = run(
        "grad_context",
        bind(grad_context_kernel, depth, head_size),
        [part, part, whole_rows, *terms],
        *grad_mid_rows,
        w_output,
        turned,
        context,
        h_all,
        scratch=term,
    )
    if not wide:
        got_vo = first_send(terms_vo)
        grad_context, sent_hd = tie(grad_context, sent_hd)
        part_hd = links.along(sent_hd, 4)
    grad_qk, sums_q = run(
        "grad_scores",
        bind(grad_scores_kernel, head_size),
        [((all_rows, both), BF16), ((8, local_width), F32)],
        turned,
        grad_context,
        v_low,
        q_low,
        k_low,
        q_raw,
        biases,
        scratch=[
            pltpu.VMEM((all_rows, local_width), F32),
            pltpu.VMEM((all_rows, local_width), F32),
            pltpu.VMEM((all_rows, all_rows), BF16),
        ],
    )
    if wide:
        grad_qk, mix_got = tie(grad_qk, mix_got)
    else:
        grad_qk, mix_got, part_hd, got_vo = tie(grad_qk, mix_got, part_hd, got_vo)
    terms_first = list(terms)
    if not wide:
        terms_first[0] = ((tall_sent + 32, cut), BF16)
    far, near, sums, *terms_qk = run(
        "grad_first",
        bind(grad_first_kernel, n_dp, depth),
        [*split, vector, *terms_first],
        grad_qk,
        w_qk,
        grad_value,
        w_value,
        h_all,
        sums,
        sums_q,
        grad_b_hidden,
        slope,
        scratch=term,
    )
    def exchange(value, step):
        return run("add", add_kernel, [vector], value, links.move(value, step))[0]

    total = sums
    if wide:
        send, keep = core_half(far, near)
        got = links.chip(send)
    else:
        got_qk = first_send(terms_qk)
        far, *got_vo = tie(far, *got_vo)
        sums_vo = first_sum("vo", terms_vo, got_vo)
        send, keep, *sums_vo = core_half(far, near, *sums_vo)
        got_vo = second_send(sums_vo)
        got = links.chip(send)
        (output,) = run("output", bind(output_kernel, n_dp), [rows_low], mix_keep, mix_got, x_one, vectors)
        grad_hidden, grad_down = owned("hd", zero_hd, part_hd)
        got_qk, got, output, grad_hidden = tie(got_qk, got, output, grad_hidden)
        got_qk, got_vo = tie(got_qk, got_vo)
        sums_qk = first_sum("qk", terms_qk, got_qk, [sums])
        got_qk = second_send(sums_qk)
        (grad_in,) = run("last", bind(last_kernel, n_dp), [rows_low], keep, got, x_own, grad_mid, vectors)
        got_qk, grad_in = tie(got_qk, grad_in)
        sent_vo, zero_vo = second_sum("vo", sums_vo, got_vo)
        part_vo = links.along(sent_vo, 4)
        sent_qk, zero_qk, total = second_sum("qk", sums_qk, got_qk, True)
        far_qk = links.along(sent_qk, 4)
        zero_vo, total = tie(zero_vo, total)
    if wide:
        (grad_in,) = run("last", bind(last_kernel, n_dp), [rows_low], keep, got, x_own, grad_mid, vectors)
    if wide:
        (output,) = run("output", bind(output_kernel, n_dp), [rows_low], mix_keep, mix_got, x_one, vectors)
    steps = links.steps()
    for step in steps[:-1]:
        total = exchange(total, step)
    moved = links.move(total, steps[-1])
    if not wide:
        grad_query, grad_key = owned("qk", zero_qk, far_qk)
        moved, grad_query = tie(moved, grad_query)
    tall_vector = (tall, F32)
    *totals, total_scale = run(
        "total", total_kernel, [tall_vector] * 7 + [((1, head_size), F32)], total, moved
    )
    totals = [v.reshape(width) for v in totals]
    if wide:
        grad_hidden, grad_down = links.scatter_wide(terms_hd[0])
        grad_output_v, grad_output_o = links.scatter_wide(terms_vo[0])
        grad_query, grad_key = links.scatter_wide(terms_qk[0])
    else:
        grad_output_v, grad_output_o = owned("vo", zero_vo, part_vo)
    return (
        output,
        grad_in,
        grad_query,
        grad_key,
        grad_output_v,
        grad_output_o.T,
        grad_hidden,
        grad_down.T,
        totals[0],
        totals[1],
        totals[2],
        totals[5],
        totals[4],
        totals[6],
        totals[3],
        total_scale.reshape(head_size),
    )


def solution(mesh):
    n_dp, n_tensor = mesh.shape["dp"], mesh.shape["tensor"]

    def local(*arguments):
        return body(*arguments, n_dp, n_tensor)

    rows = P(("dp", "tensor"), None)
    into, out_of = P("dp", "tensor"), P("tensor", "dp")
    return jax.shard_map(
        local,
        mesh=mesh,
        in_specs=(rows, into, into, into, out_of, into, out_of, *[P()] * 8, P("dp"), rows),
        out_specs=(rows, rows, into, into, into, out_of, into, out_of, *[P()] * 8),
        check_vma=False,
    )
```

```python
import jax
import jax.numpy as jnp
from jax import lax
from jax.experimental import pallas as pl
from jax.experimental.pallas import tpu as pltpu
from jax.sharding import PartitionSpec as P

EPSILON = 1e-06
SOFTPLUS_UNIT = 1.442695041
AXES = ("dp", "tensor")
F32 = jnp.float32
BF16 = jnp.bfloat16
LANES = 128
TENSOR_ORDER = (0, 2, 1, 3)
NN, NT, TN = ((1,), (0,)), ((1,), (1,)), ((0,), (0,))


def dot(left, right, dims=NN):
    return lax.dot_general(left, right, (dims, ((), ())), preferred_element_type=F32)


def shaped(shape, kind):
    return jax.ShapeDtypeStruct(shape, kind)


def call(name, kernel, outs, scalars, *arguments, flops=1e6, scratch=(), limit=12, remote=0):
    space = pl.BlockSpec(memory_space=pltpu.VMEM)
    apart = pl.BlockSpec(memory_space=pltpu.HBM)
    moved = sum(a.size * a.dtype.itemsize for a in (*arguments, *outs))
    return pl.pallas_call(
        kernel,
        name=name,
        out_shape=outs,
        in_specs=[pl.BlockSpec(memory_space=pltpu.SMEM)]
        + [space] * (len(arguments) - remote)
        + [apart] * remote,
        out_specs=[space] * len(outs),
        scratch_shapes=scratch,
        compiler_params=pltpu.CompilerParams(vmem_limit_bytes=limit << 20),
        cost_estimate=pl.CostEstimate(flops=int(flops), bytes_accessed=moved, transcendentals=0),
    )(scalars, *arguments)


def pack(first, second):
    main = first.shape[1] // LANES * LANES
    return jnp.concatenate([first[:, :main], second[:, :main], first[:, main:], second[:, main:]], axis=1)


def unpack(both):
    width = both.shape[1] // 2
    main = width // LANES * LANES
    edge = main * 2 + width - main
    first = jnp.concatenate([both[:, :main], both[:, 2 * main : edge]], axis=1)
    rest = both[:, 2 * main :].astype(F32)[:, width - main :].astype(both.dtype)
    second = jnp.concatenate([both[:, main : 2 * main], rest], axis=1)
    return first, second


def reorder(value, place, n_dp):
    width = value.shape[1]
    lane = lax.broadcasted_iota(jnp.int32, (1, width), 1)
    span = width // n_dp
    bit = 1
    while bit < n_dp:
        low = lax.rem(lane, 2 * span) < span
        other = jnp.where(low, pltpu.roll(value, width - span, 1), pltpu.roll(value, span, 1))
        value = jnp.where((place & bit) != 0, other, value)
        bit, span = 2 * bit, 2 * span
    return value


def row_mean(value):
    return jnp.sum(value, axis=1, keepdims=True) * (1.0 / value.shape[1])


def normalize(value):
    inverse = lax.rsqrt(row_mean(value * value) + EPSILON)
    return value * inverse, inverse


def norm_back(grad_normed, normed, inverse, gain):
    scaled = grad_normed * gain
    return inverse * (scaled - normed * row_mean(scaled * normed))


def load(sources, targets, sem):
    copies = [pltpu.make_async_copy(a, b, sem.at[k]) for k, (a, b) in enumerate(zip(sources, targets))]
    for copy in copies:
        copy.start()
    for copy in copies:
        copy.wait()


def pack_kernel(s, *refs):
    sources, outs, loaded = refs[:6], refs[6:9], refs[9:15]
    load(sources, loaded, refs[15])
    for k, out in enumerate(outs):
        out[...] = pack(loaded[2 * k][...].astype(F32), loaded[2 * k + 1][...].astype(F32)).astype(BF16)


def row_of(ref):
    return jnp.concatenate([ref[k : k + 1] for k in range(ref.shape[0])], axis=1)


def prepare_kernel(n_dp, s, scale, *refs):
    sources, (h, x_own, grad, vectors, biases) = refs[:9], refs[9:14]
    x, cotangent, *given = refs[14:23]
    load(sources, refs[14:23], refs[23])
    mine, place, length = s[0], s[1], s[2]
    value = reorder(x[...].astype(F32), mine, n_dp)
    stacked = jnp.concatenate([row_of(given[k]) for k in (0, 1, 2, 3, 4, 5, 6, 6)], axis=0)
    width = biases.shape[1]
    slices = stacked[:, :width]
    for number in range(1, stacked.shape[1] // width):
        slices = jnp.where(place == number, stacked[:, number * width : (number + 1) * width], slices)
    biases[...] = slices
    biases[7:8] = scale[...]
    stacked = reorder(stacked, mine, n_dp)
    normed, _ = normalize(value)
    h[...] = (normed * stacked[0:1]).astype(BF16)
    x_own[...] = value.astype(BF16)
    rows = value.shape[0]
    row = lax.broadcasted_iota(jnp.int32, value.shape, 0) + place * rows
    g = jnp.where(row < length, reorder(cotangent[...].astype(F32), mine, n_dp), 0.0)
    grad[...] = g.astype(BF16)
    vectors[...] = stacked
    vectors[4:5] = jnp.sum(g, axis=0, keepdims=True)


def join(pieces, out):
    rows = pieces[0].shape[0]
    for number, piece in enumerate(pieces):
        out[pl.ds(number * rows, rows)] = piece[...]


def tiles(rows, body, size=128):
    def step(m, carry):
        body(pl.ds(pl.multiple_of(m * size, size), size), m)
        return carry

    lax.fori_loop(0, rows // size, step, 0)


def positions(shape, axis, place, local, offset=0):
    row = lax.broadcasted_iota(jnp.int32, shape, axis) + offset
    shift = local.bit_length() - 1
    block = row >> shift
    turned = ((block & 1) << 1) | (block >> 1)
    return ((place ^ turned) << shift) + (row & (local - 1))


def fetch(even, odd, out, depth, sem):
    copies = []
    if not odd:
        copies.append(pltpu.make_async_copy(even[0], out, sem.at[0]))
    else:
        for start, blocks in enumerate((even, odd)):
            row = start * depth
            for block in blocks:
                for k in range(block.shape[0] // depth):
                    source, target = block.at[pl.ds(k * depth, depth)], out.at[pl.ds(row, depth)]
                    copies.append(pltpu.make_async_copy(source, target, sem.at[len(copies)]))
                    row += 2 * depth
    for one in copies:
        one.start()
    return copies


def stack_kernel(s, *refs):
    join(refs[:-1], refs[-1])


def of_head(value, number, head_size):
    lanes = lax.broadcasted_iota(jnp.int32, (1, value.shape[1]), 1) // head_size
    return jnp.where(lanes == number, value, jnp.zeros((), value.dtype))


def attend_kernel(counts, depth, head_size, s, p0, p1, p2, p3, biases, *refs):
    even, odd = refs[: counts[0]], refs[counts[0] : counts[1]]
    q_raw, q_low, k_low, h, weight, turned, sem = refs[counts[1] :]
    copies = fetch(even, odd, weight, depth, sem)
    join((p0, p1, p2, p3), h)
    for copy in copies:
        copy.wait()
    first, second = unpack(dot(h[...], weight[...]))
    first = first + biases[4:5]
    q_raw[...] = first
    q_low[...] = (first * biases[7:8]).astype(BF16)
    k_low[...] = second.astype(BF16)
    place, length = s[1], s[2]
    rows, local = q_low.shape[0], p0.shape[0]
    key_place = positions((rows, 1), 0, place, local)
    last = jnp.minimum(positions((1, rows), 1, place, local), length - 1)

    def head(number, carry):
        score = dot(k_low[...], of_head(q_low[...], number, head_size), NT)
        score = jnp.where(key_place <= last, score, -1e30)
        raised = jnp.exp(score - jnp.max(score, axis=0, keepdims=True))
        share = 1.0 / jnp.sum(raised, axis=0, keepdims=True)
        turned[number] = (raised * share).astype(BF16)
        return carry

    for number in range(turned.shape[0]):
        head(number, 0)


def mixed_heads(turned, value, head_size, dims):
    total = None
    for number in range(turned.shape[0]):
        term = dot(turned[number], of_head(value, number, head_size), dims)
        total = term if total is None else total + term
    return total


def split_weight(weight, one, two):
    one[...], two[...] = unpack(weight[...])


def context_kernel(counts, depth, head_size, s, h, turned, biases, *refs):
    even, odd = refs[: counts[0]], refs[counts[0] : counts[1]]
    v_low, context, far, near, w_value, w_output, weight, sem = refs[counts[1] :]
    for copy in fetch(even, odd, weight, depth, sem):
        copy.wait()
    split_weight(weight, w_value, w_output)
    v_low[...] = (dot(h[...], w_value[...]) + biases[5:6]).astype(BF16)
    context[...] = mixed_heads(turned, v_low[...], head_size, TN).astype(BF16)
    split_product(context, w_output, far, near)


def split_product(left, right, far, near, extra=None, along=None):
    half, total = near.shape[0], None
    for start, out in ((half, far), (0, near)):
        at = pl.ds(start, half)
        value = dot(left[at], right[...], NT)
        if extra is not None:
            value = value + dot(extra[0][at], extra[1][...], NT)
        out[...] = value.astype(out.dtype)
        if along is not None:
            summed = jnp.sum(value * along[at].astype(F32), axis=0, keepdims=True)
            total = summed if total is None else total + summed
    return total


def middle_kernel(s, near, got, send, keep):
    rows = send.shape[0]
    send[...] = (near[rows:] + got[rows:].astype(F32)).astype(BF16)
    keep[...] = near[:rows] + got[:rows].astype(F32)


def second_norm_kernel(s, keep, got, x_own, vectors, x_one, h):
    value = x_own[...].astype(F32) + keep[...] + got[...].astype(F32) + vectors[2:3]
    x_one[...] = value
    normed, _ = normalize(value)
    h[...] = (normed * vectors[1:2]).astype(BF16)


def grad_act_kernel(counts, depth, s, p0, p1, p2, p3, *refs):
    even, odd = refs[: counts[0]], refs[counts[0] : counts[1]]
    grad_act, g, w_hidden, w_down, weight, sem = refs[counts[1] :]
    copies = fetch(even, odd, weight, depth, sem)
    join((p0, p1, p2, p3), g)
    for copy in copies:
        copy.wait()
    split_weight(weight, w_hidden, w_down)
    grad_act[...] = dot(g[...], w_down[...])


def hidden_kernel(s, p0, p1, p2, p3, w_hidden, biases, grad_act, out_far, out_near, act, grad_pre, h):
    join((p0, p1, p2, p3), h)
    pre = dot(h[...], w_hidden[...]) + biases[6:7]
    sigma = jax.nn.sigmoid(pre)
    act[...] = (pre * sigma).astype(BF16)
    grad_pre[...] = (grad_act[...] * (sigma * (1.0 + pre * (1.0 - sigma)))).astype(BF16)
    split_product(grad_pre, w_hidden, out_far, out_near)


PAIR_FIRST = (3, 1, 2, 0)
RING_SENT, RING_KEPT = ((3, 1), (1, 1), (3, 0), (1, 0)), ((2, 1), (0, 1), (2, 0), (0, 0))


def spread_terms(term, outs, depth):
    if len(outs) == 1:
        outs[0][...] = term
        return
    pair_sent, pair_kept, ring_sent, ring_kept = outs
    cut = pair_kept.shape[1]

    def copy(out, at, block, columns):
        out[pl.ds(at * depth, depth)] = term[block * depth : (block + 1) * depth, columns]

    for at, j in enumerate(PAIR_FIRST):
        copy(pair_sent, at, 2 * j + 1, slice(0, cut))
        copy(pair_kept, at, 2 * j, slice(0, cut))
    for at in range(4):
        (j, i), (k, m) = RING_SENT[at], RING_KEPT[at]
        copy(ring_sent, at, 2 * j + i, slice(cut, None))
        copy(ring_kept, at, 2 * k + m, slice(cut, None))


def two_terms(left_one, right_one, left_two, right_two):
    first = dot(left_one[...], right_one[...], TN)
    second = dot(left_two[...], right_two[...], TN)
    return pack(first, second).astype(BF16)


def down_kernel(depth, s, h, g, act, grad_pre, b_hidden, *outs):
    spread_terms(two_terms(h, grad_pre, g, act), outs, depth)
    b_hidden[...] = jnp.sum(grad_pre[...].astype(F32), axis=0, keepdims=True)


def mixer_kernel(s, act, w_down, far, near):
    split_product(act, w_down, far, near)


def owned_kernel(n_got, s, keep, *refs):
    total = keep[...]
    for got in refs[:n_got]:
        total = total + got[pl.ds(0, total.shape[0])].astype(F32)
    refs[n_got][...], refs[n_got + 1][...] = unpack(total)


def grad_middle_kernel(s, keep, got, x_one, grad, vectors, grad_low, grad_full, sums):
    normed, inverse = normalize(x_one[...])
    grad_h = keep[...] + got[...].astype(F32)
    full = grad[...].astype(F32) + norm_back(grad_h, normed, inverse, vectors[1:2])
    grad_full[...] = full
    grad_low[...] = full.astype(BF16)
    sums[...] = vectors[...]
    sums[5:6] = jnp.sum(full, axis=0, keepdims=True)
    sums[6:7] = jnp.sum(grad_h * normed, axis=0, keepdims=True)


def grad_context_kernel(depth, head_size, s, p0, p1, p2, p3, w_output, turned, context, h, *refs):
    grad_context, grad_value, gm, *outs = refs
    join((p0, p1, p2, p3), gm)
    grad_context[...] = dot(gm[...], w_output[...]).astype(BF16)
    grad_value[...] = mixed_heads(turned, grad_context[...], head_size, NN).astype(BF16)
    spread_terms(two_terms(h, grad_value, gm, context), outs, depth)


def grad_scores_kernel(head_size, s, turned, grad_context, v_low, q_low, k_low, q_raw, biases, *refs):
    grad_qk, sums, scores = refs
    rows = q_low.shape[0]
    grad_q = grad_k = 0.0
    for number in range(turned.shape[0]):
        grad_chance = dot(v_low[...], of_head(grad_context[...], number, head_size), NT)
        chance = turned[number].astype(F32)
        product = chance * grad_chance
        center = jnp.sum(product, axis=0, keepdims=True)
        scores[...] = (product - chance * center).astype(BF16)
        grad_q = grad_q + dot(scores[...], of_head(k_low[...], number, head_size), TN)
        grad_k = grad_k + dot(scores[...], of_head(q_low[...], number, head_size))
    low = grad_q.astype(BF16).astype(F32)
    sums[0:1] = jnp.sum(low * q_raw[...], axis=0, keepdims=True)
    low = (low * biases[7:8]).astype(BF16).astype(F32)
    grad_qk[...] = pack(low, grad_k).astype(BF16)
    sums[1:2] = jnp.sum(low, axis=0, keepdims=True)


def grad_first_kernel(
    n_dp, depth, s, grad_qk, w_qk, grad_value, w_value, h, sums_in, sums_q, b_hidden, slope, *refs
):
    far, near, sums, *outs = refs
    spread_terms(dot(h[...], grad_qk[...], TN).astype(BF16), outs, depth)
    mine, place = s[0], s[1]
    gained = split_product(grad_qk, w_qk, far, near, (grad_value, w_value), h) / sums_in[0:1]
    row = lax.broadcasted_iota(jnp.int32, sums.shape, 0)
    sums[...] = reorder(jnp.where(row == 7, gained, sums_in[...]), mine, n_dp)
    sums[0:4] = jnp.zeros((4, sums.shape[1]), F32)
    local_width, head_size = sums_q.shape[1], slope.shape[1]
    b_value = jnp.sum(grad_value[...].astype(F32), axis=0, keepdims=True)
    share = jnp.concatenate([sums_q[1:2], b_value, b_hidden[...]], axis=0)
    for number in range(sums.shape[1] // local_width):

        @pl.when(place == number)
        def _():
            sums[0:3, number * local_width : (number + 1) * local_width] = share

    scale = sums_q[0:1]
    total = scale[:, :head_size]
    for number in range(1, local_width // head_size):
        total = total + scale[:, number * head_size : (number + 1) * head_size]
    sums[3:4, :head_size] = total * slope[...]
    if len(outs) > 1:
        outs[0][pl.ds(4 * depth, 32)] = fold(sums[...], outs[0].shape[1])


def fold(vectors, width):
    part = vectors.shape[1] // 4
    rows = jnp.concatenate([vectors[:, k * part : (k + 1) * part] for k in range(4)], axis=0)
    return jnp.concatenate([rows, jnp.zeros((32, width - part), F32)], axis=1).astype(BF16)


def unfold(rows, part):
    return jnp.concatenate([rows[8 * k : 8 * k + 8, :part] for k in range(4)], axis=1)


def first_sum_kernel(s, pair_kept, pair_got, ring_kept, ring_got, *refs):
    *given, pair_out, pair_mid, ring_out, ring_mid = refs
    half = pair_mid.shape[0]
    value = pair_kept[...].astype(F32) + pair_got[pl.ds(0, 2 * half)].astype(F32)
    pair_out[pl.ds(0, half)] = value[:half].astype(BF16)
    pair_mid[...] = value[half:]
    value = ring_kept[...].astype(F32) + ring_got[...].astype(F32)
    ring_out[...] = value[:half].astype(BF16)
    ring_mid[...] = value[half:]
    if given:
        low = fold(given[0][...], pair_out.shape[1]).astype(F32) + pair_got[pl.ds(2 * half, 32)].astype(F32)
        pair_out[pl.ds(half, 32)] = low.astype(BF16)


def second_sum_kernel(s, pair_mid, pair_got, ring_mid, ring_got, *refs):
    half, depth, cut = pair_mid.shape[0], pair_mid.shape[0] // 2, pair_mid.shape[1]
    given, out, zero = refs[: len(refs) // 3], refs[len(refs) // 3], refs[len(refs) // 3 + 1]
    pair = pair_mid[...] + pair_got[pl.ds(0, half)].astype(F32)
    ring = ring_mid[...] + ring_got[...].astype(F32)
    out[:, :cut], out[:, cut:] = pair[:depth].astype(BF16), ring[:depth].astype(BF16)
    zero[:, :cut], zero[:, cut:] = pair[depth:], ring[depth:]
    if given:
        at, vectors = pl.ds(half, 32), refs[-1]
        vectors[...] = unfold(given[0][at].astype(F32) + pair_got[at].astype(F32), vectors.shape[1] // 4)


def total_kernel(s, one, two, *outs):
    total = one[...] + two[...]
    for out, row in zip(outs[:7], (0, 1, 2, 6, 4, 5, 7)):
        for k in range(out.shape[0]):
            out[k : k + 1] = total[row : row + 1, k * LANES : (k + 1) * LANES]
    outs[7][...] = total[3:4, : outs[7].shape[1]]


def last_kernel(n_dp, s, keep, got, x_own, grad_full, sums_in, grad_in):
    normed, inverse = normalize(x_own[...].astype(F32))
    grad_h = keep[...] + got[...].astype(F32)
    full = grad_full[...] + norm_back(grad_h, normed, inverse, sums_in[0:1])
    grad_in[...] = reorder(full, s[0], n_dp).astype(BF16)


def add_kernel(s, one, two, out):
    out[...] = one[...] + two[...]


def output_kernel(n_dp, s, keep, got, x_one, vectors, out):
    value = x_one[...] + keep[...] + got[...].astype(F32) + vectors[3:4]
    out[...] = reorder(value, s[0], n_dp).astype(BF16)


def tie(*values):
    return lax.optimization_barrier(values)


class Links:
    def __init__(self, n_dp, n_tensor):
        self.n_dp, self.n_tensor = n_dp, n_tensor
        self.wide = n_dp > 8

    def move(self, value, target):
        pairs = []
        for d in range(self.n_dp):
            for t in range(self.n_tensor):
                to_d, to_t = target(d, t)
                pairs.append((d * self.n_tensor + t, to_d * self.n_tensor + to_t))
        return lax.ppermute(value, AXES, pairs)

    def chip(self, value):
        return self.move(value, lambda d, t: (d, t ^ 2))

    def core(self, value):
        return self.move(value, lambda d, t: (d, t ^ 1))

    def pair(self, value):
        return self.along(value, 1)

    def along(self, value, bits):
        return self.move(value, lambda d, t: (d ^ bits, t))

    def gather_tensor(self, rows):
        near = self.chip(rows)
        return rows, near, self.core(rows), self.core(near)

    def gather_wide(self, shard):
        blocks, place = lax.all_gather(shard, "dp", axis=0), lax.axis_index("dp")
        return jnp.take(blocks, lax.iota(jnp.int32, self.n_dp) ^ place, axis=0).reshape(-1, shard.shape[1])

    def scatter_wide(self, total):
        place = lax.axis_index("dp")
        blocks = total.reshape(self.n_dp, total.shape[0] // self.n_dp, total.shape[1])
        blocks = jnp.take(blocks, lax.iota(jnp.int32, self.n_dp) ^ place, axis=0).astype(F32)
        return unpack(lax.psum_scatter(blocks.reshape(total.shape), "dp", scatter_dimension=0, tiled=True))

    def steps(self):
        found, bit = [], 1
        while bit < self.n_dp and self.wide:
            found.append(lambda d, t, bit=bit: (d ^ bit, t))
            bit *= 2
        far = [] if self.wide else [lambda d, t: (d ^ 4, t)]
        return found + [lambda d, t: (d, t ^ 1), lambda d, t: (d, t ^ 2)] + far


def body(
    inputs,
    weight_query,
    weight_key,
    weight_value,
    weight_output,
    weight_hidden,
    weight_down,
    bias_query,
    bias_value,
    bias_hidden,
    bias_output,
    bias_final,
    gain_attention,
    gain_mixer,
    query_scale,
    lengths,
    cotangent,
    n_dp,
    n_tensor,
):
    links = Links(n_dp, n_tensor)
    wide = links.wide
    local_rows, width = inputs.shape
    all_rows = local_rows * n_tensor
    depth = width // n_dp
    local_width = weight_query.shape[1]
    both = 2 * local_width
    head_size = query_scale.shape[0]
    heads = local_width // head_size
    dp_index = lax.axis_index("dp")
    tensor_index = lax.axis_index("tensor")
    s = jnp.stack([dp_index, tensor_index, lengths[0]])
    product = 2 * all_rows * width * local_width
    mixed = 2 * all_rows * all_rows * local_width

    def run(name, kernel, outs, *arguments, **rest):
        return call(name, kernel, [shaped(*o) for o in outs], s, *arguments, **rest)

    def bind(kernel, *fixed):
        def bound(*refs):
            return kernel(*fixed, *refs)

        return bound

    packed = [((depth, both), BF16)]
    rows_low, rows_full = ((local_rows, width), BF16), ((local_rows, width), F32)
    split = [((all_rows // 2, width), BF16), ((all_rows // 2, width), F32)]
    part = ((all_rows, local_width), BF16)
    part_full = ((all_rows, local_width), F32)
    whole_rows = ((all_rows, width), BF16)
    weight = ((width, local_width), BF16)
    vector = ((8, width), F32)
    halves = [((width // 2, both), BF16)] * 2
    term = [pltpu.VMEM((width, both), BF16)]
    sems = [pltpu.SemaphoreType.DMA((n_dp,))]

    unit = SOFTPLUS_UNIT / jnp.sqrt(F32(head_size))
    scale_wide = jnp.tile(jax.nn.softplus(query_scale) * unit, heads)[None]
    slope = (jax.nn.sigmoid(query_scale) * unit)[None]
    def apart(value):
        return pltpu.with_memory_space_constraint(value, pltpu.HBM)

    weights = (weight_query, weight_key, weight_value, weight_output.T, weight_hidden, weight_down.T)
    own_qk, own_vo, own_hd = run(
        "pack",
        pack_kernel,
        packed * 3,
        *(apart(w) for w in weights),
        remote=6,
        scratch=[pltpu.VMEM((depth, local_width), BF16)] * 6 + [pltpu.SemaphoreType.DMA((6,))],
    )
    given = (gain_attention, gain_mixer, bias_output, bias_final, bias_query, bias_value, bias_hidden)
    scale_wide, slope = tie(scale_wide, slope)
    tall = (width // LANES, LANES)
    h_own, x_own, grad_own, vectors, biases = run(
        "prepare",
        bind(prepare_kernel, n_dp),
        [rows_low, rows_low, rows_low, vector, ((8, local_width), F32)],
        scale_wide,
        *(apart(v) for v in (inputs, cotangent, *(v.reshape(tall) for v in given))),
        remote=9,
        scratch=[pltpu.VMEM((local_rows, width), BF16)] * 2
        + [pltpu.VMEM(tall, F32)] * 7
        + [pltpu.SemaphoreType.DMA((9,))],
    )

    def stack(*blocks):
        rows = sum(block.shape[0] for block in blocks)
        return run("stack", stack_kernel, [((rows, both), BF16)], *blocks)[0]

    if wide:
        qk, vo, hd = (([links.gather_wide(own)], []) for own in (own_qk, own_vo, own_hd))
        h_one, grad_rows = links.gather_tensor(h_own), links.gather_tensor(grad_own)
    else:
        qk_one, qk_two = links.along(own_qk, 2), links.along(own_qk, 4)
        hd_pair = links.pair(own_hd)
        h_own, own_vo, own_hd, qk_one, qk_two, hd_pair = tie(h_own, own_vo, own_hd, qk_one, qk_two, hd_pair)
        h_chip = links.chip(h_own)
        qk_three = links.along(qk_two, 2)
        near_qk_pair = links.pair(stack(own_qk, qk_one))
        vo_two, vo_pair = links.along(own_vo, 4), links.pair(own_vo)
        far_stack = stack(qk_two, qk_three)
        far_stack, near_qk_pair = tie(far_stack, near_qk_pair)
        h_chip, vo_two, vo_pair, own_vo = tie(h_chip, vo_two, vo_pair, own_vo)
        h_one = h_own, h_chip, links.core(h_own), links.core(h_chip)
        far_qk_pair = links.pair(far_stack)
        vo_one, vo_three = links.along(own_vo, 2), links.along(vo_two, 2)
        qk = [own_qk, qk_one, qk_two, qk_three], [near_qk_pair, far_qk_pair]
        h_one, qk, vo_three, own_hd = tie(h_one, qk, vo_three, own_hd)
        near_vo_pair = links.pair(vo_one)
        hd_one, hd_two = links.along(own_hd, 2), links.along(own_hd, 4)
        grad_chip = links.chip(grad_own)
    n_qk = len(qk[0]), len(qk[0]) + len(qk[1])
    q_raw, q_low, k_low, h_all, w_qk, turned = run(
        "attend",
        bind(attend_kernel, n_qk, depth, head_size),
        [
            part_full,
            part,
            part,
            whole_rows,
            ((width, both), BF16),
            ((heads, all_rows, all_rows), BF16),
        ],
        *h_one,
        biases,
        *qk[0],
        *qk[1],
        remote=n_qk[1],
        scratch=sems,
    )
    if not wide:
        turned, near_vo_pair, hd_one, hd_two, grad_chip = tie(turned, near_vo_pair, hd_one, hd_two, grad_chip)
        far_vo_pair = links.pair(stack(vo_two, vo_three))
        hd_three = links.along(hd_two, 2)
        grad_rows = grad_own, grad_chip, links.core(grad_own), links.core(grad_chip)
        vo = [own_vo, vo_one, vo_two, vo_three], [vo_pair, near_vo_pair, far_vo_pair]
        turned, vo, grad_rows = tie(turned, vo, grad_rows)
        near_hd_pair = links.pair(hd_one)
    n_vo = len(vo[0]), len(vo[0]) + len(vo[1])
    v_low, context, far, near, w_value, w_output = run(
        "context",
        bind(context_kernel, n_vo, depth, head_size),
        [part, part, *split, weight, weight],
        h_all,
        turned,
        biases,
        *vo[0],
        *vo[1],
        remote=n_vo[1],
        scratch=term + sems,
    )

    def core_half(far, near, *extra):
        got, *extra = tie(links.core(far), *extra)
        return list(run("middle", middle_kernel, [rows_low, rows_full], near, got)) + list(extra)

    if wide:
        send, keep = core_half(far, near)
        got = links.chip(send)
    else:
        far, near_hd_pair, hd_three = tie(far, near_hd_pair, hd_three)
        send, keep = core_half(far, near)
        got = links.chip(send)
        far_hd_pair = links.pair(stack(hd_two, hd_three))
        hd = [own_hd, hd_one, hd_two, hd_three], [hd_pair, near_hd_pair, far_hd_pair]
        got, hd = tie(got, hd)
    n_hd = len(hd[0]), len(hd[0]) + len(hd[1])
    x_one, h_two_own = run("second_norm", second_norm_kernel, [rows_full, rows_low], keep, got, x_own, vectors)
    h_two_chip = links.chip(h_two_own)
    grad_act, grad_all, w_hidden, w_down = run(
        "grad_act",
        bind(grad_act_kernel, n_hd, depth),
        [part_full, whole_rows, weight, weight],
        *grad_rows,
        *hd[0],
        *hd[1],
        remote=n_hd[1],
        scratch=term + sems,
    )
    h_two_chip, grad_act = tie(h_two_chip, grad_act)
    h_two = h_two_own, h_two_chip, links.core(h_two_own), links.core(h_two_chip)
    far, near, act, grad_pre, h_two_all = run(
        "hidden",
        hidden_kernel,
        [*split, part, part, whole_rows],
        *h_two,
        w_hidden,
        biases,
        grad_act,
    )
    cut = 3 * both // 5
    tall_sent = n_dp // 2 * depth
    terms = [((width, both), BF16)]
    if not wide:
        terms = [((tall_sent, c), BF16) for c in (cut, cut, both - cut, both - cut)]
    grad_b_hidden, *terms_hd = run(
        "down",
        bind(down_kernel, depth),
        [((1, local_width), F32), *terms],
        h_two_all,
        grad_all,
        act,
        grad_pre,
    )
    send, keep, terms_hd = core_half(far, near, terms_hd)
    got = links.chip(send)
    act, keep = tie(act, keep)
    mix_far, mix_near = run("mixer", mixer_kernel, split, act, w_down)
    got, mix_far = tie(got, mix_far)

    def first_send(terms):
        return [links.pair(terms[0]), links.along(terms[2], 2)]

    def first_sum(name, terms, got, given=()):
        rows = tall_sent // 2
        extra = 32 if given else 0
        outs = [((rows + extra, cut), BF16), ((rows, cut), F32), ((rows, both - cut), BF16), ((rows, both - cut), F32)]
        return run("first_" + name, first_sum_kernel, outs, terms[1], got[0], terms[3], got[1], *given)

    def second_send(sums):
        return [links.along(sums[0], 2), links.pair(sums[2])]

    def second_sum(name, sums, got, given=False):
        outs = packed + [((depth, both), F32)] + ([vector] if given else [])
        more = sums[:1] if given else []
        return run("second_" + name, second_sum_kernel, outs, sums[1], got[0], sums[3], got[1], *more)

    def owned(name, *parts):
        outs = [((depth, local_width), F32)] * 2
        return run("owned_" + name, bind(owned_kernel, len(parts) - 1), outs, *parts)

    if not wide:
        got_hd = first_send(terms_hd)
        got, got_hd = tie(got, got_hd)
    grad_mid_low, grad_mid, sums = run(
        "grad_middle",
        grad_middle_kernel,
        [rows_low, rows_full, vector],
        keep,
        got,
        x_one,
        grad_own,
        vectors,
    )
    if wide:
        grad_mid_rows = links.gather_tensor(grad_mid_low)
    else:
        grad_mid_chip = links.chip(grad_mid_low)
        sums_hd = first_sum("hd", terms_hd, got_hd)
        got_hd = second_send(sums_hd)
        grad_mid_chip, got_hd = tie(grad_mid_chip, got_hd)
        sent_hd, zero_hd = second_sum("hd", sums_hd, got_hd)
        grad_mid_rows = grad_mid_low, grad_mid_chip, links.core(grad_mid_low), links.core(grad_mid_chip)
    if wide:
        grad_mid_rows, mix_far = tie(grad_mid_rows, mix_far)
    else:
        grad_mid_rows, mix_far, sent_hd = tie(grad_mid_rows, mix_far, sent_hd)
    mix_send, mix_keep = core_half(mix_far, mix_near)
    mix_got = links.chip(mix_send)
    grad_context, grad_value, _, *terms_vo = run(
        "grad_context",
        bind(grad_context_kernel, depth, head_size),
        [part, part, whole_rows, *terms],
        *grad_mid_rows,
        w_output,
        turned,
        context,
        h_all,
    )
    if not wide:
        got_vo = first_send(terms_vo)
        grad_context, sent_hd = tie(grad_context, sent_hd)
        part_hd = links.along(sent_hd, 4)
    grad_qk, sums_q = run(
        "grad_scores",
        bind(grad_scores_kernel, head_size),
        [((all_rows, both), BF16), ((8, local_width), F32)],
        turned,
        grad_context,
        v_low,
        q_low,
        k_low,
        q_raw,
        biases,
        scratch=[pltpu.VMEM((all_rows, all_rows), BF16)],
    )
    if wide:
        grad_qk, mix_got = tie(grad_qk, mix_got)
    else:
        grad_qk, mix_got, part_hd, got_vo = tie(grad_qk, mix_got, part_hd, got_vo)
    terms_first = list(terms)
    if not wide:
        terms_first[0] = ((tall_sent + 32, cut), BF16)
    far, near, sums, *terms_qk = run(
        "grad_first",
        bind(grad_first_kernel, n_dp, depth),
        [*split, vector, *terms_first],
        grad_qk,
        w_qk,
        grad_value,
        w_value,
        h_all,
        sums,
        sums_q,
        grad_b_hidden,
        slope,
    )
    def exchange(value, step):
        return run("add", add_kernel, [vector], value, links.move(value, step))[0]

    total = sums
    if wide:
        send, keep = core_half(far, near)
        got = links.chip(send)
    else:
        got_qk = first_send(terms_qk)
        far, *got_vo = tie(far, *got_vo)
        sums_vo = first_sum("vo", terms_vo, got_vo)
        send, keep, *sums_vo = core_half(far, near, *sums_vo)
        got_vo = second_send(sums_vo)
        got = links.chip(send)
        (output,) = run("output", bind(output_kernel, n_dp), [rows_low], mix_keep, mix_got, x_one, vectors)
        grad_hidden, grad_down = owned("hd", zero_hd, part_hd)
        got_qk, got, output, grad_hidden = tie(got_qk, got, output, grad_hidden)
        got_qk, got_vo = tie(got_qk, got_vo)
        sums_qk = first_sum("qk", terms_qk, got_qk, [sums])
        got_qk = second_send(sums_qk)
        (grad_in,) = run("last", bind(last_kernel, n_dp), [rows_low], keep, got, x_own, grad_mid, vectors)
        got_qk, grad_in = tie(got_qk, grad_in)
        sent_vo, zero_vo = second_sum("vo", sums_vo, got_vo)
        part_vo = links.along(sent_vo, 4)
        sent_qk, zero_qk, total = second_sum("qk", sums_qk, got_qk, True)
        far_qk = links.along(sent_qk, 4)
        zero_vo, total = tie(zero_vo, total)
    if wide:
        (grad_in,) = run("last", bind(last_kernel, n_dp), [rows_low], keep, got, x_own, grad_mid, vectors)
    if wide:
        (output,) = run("output", bind(output_kernel, n_dp), [rows_low], mix_keep, mix_got, x_one, vectors)
    steps = links.steps()
    for step in steps[:-1]:
        total = exchange(total, step)
    moved = links.move(total, steps[-1])
    if not wide:
        grad_query, grad_key = owned("qk", zero_qk, far_qk)
        moved, grad_query = tie(moved, grad_query)
    tall_vector = (tall, F32)
    *totals, total_scale = run(
        "total", total_kernel, [tall_vector] * 7 + [((1, head_size), F32)], total, moved
    )
    totals = [v.reshape(width) for v in totals]
    if wide:
        grad_hidden, grad_down = links.scatter_wide(terms_hd[0])
        grad_output_v, grad_output_o = links.scatter_wide(terms_vo[0])
        grad_query, grad_key = links.scatter_wide(terms_qk[0])
    else:
        grad_output_v, grad_output_o = owned("vo", zero_vo, part_vo)
    return (
        output,
        grad_in,
        grad_query,
        grad_key,
        grad_output_v,
        grad_output_o.T,
        grad_hidden,
        grad_down.T,
        totals[0],
        totals[1],
        totals[2],
        totals[5],
        totals[4],
        totals[6],
        totals[3],
        total_scale.reshape(head_size),
    )


def solution(mesh):
    n_dp, n_tensor = mesh.shape["dp"], mesh.shape["tensor"]

    def local(*arguments):
        return body(*arguments, n_dp, n_tensor)

    rows = P(("dp", "tensor"), None)
    into, out_of = P("dp", "tensor"), P("tensor", "dp")
    return jax.shard_map(
        local,
        mesh=mesh,
        in_specs=(rows, into, into, into, out_of, into, out_of, *[P()] * 8, P("dp"), rows),
        out_specs=(rows, rows, into, into, into, out_of, into, out_of, *[P()] * 8),
        check_vma=False,
    )
```

```python
import jax
import jax.numpy as jnp
from jax import lax
from jax.experimental import pallas as pl
from jax.experimental.pallas import tpu as pltpu
from jax.sharding import PartitionSpec as P

EPSILON = 1e-06
SOFTPLUS_UNIT = 1.442695041
AXES = ("dp", "tensor")
F32 = jnp.float32
BF16 = jnp.bfloat16
LANES = 128
TENSOR_ORDER = (0, 2, 1, 3)
NN, NT, TN = ((1,), (0,)), ((1,), (1,)), ((0,), (0,))


def dot(left, right, dims=NN):
    return lax.dot_general(left, right, (dims, ((), ())), preferred_element_type=F32)


def shaped(shape, kind):
    return jax.ShapeDtypeStruct(shape, kind)


def call(name, kernel, outs, scalars, *arguments, flops=1e6, scratch=(), limit=12, remote=0):
    space = pl.BlockSpec(memory_space=pltpu.VMEM)
    apart = pl.BlockSpec(memory_space=pltpu.HBM)
    moved = sum(a.size * a.dtype.itemsize for a in (*arguments, *outs))
    return pl.pallas_call(
        kernel,
        name=name,
        out_shape=outs,
        in_specs=[pl.BlockSpec(memory_space=pltpu.SMEM)]
        + [space] * (len(arguments) - remote)
        + [apart] * remote,
        out_specs=[space] * len(outs),
        scratch_shapes=scratch,
        compiler_params=pltpu.CompilerParams(vmem_limit_bytes=limit << 20),
        cost_estimate=pl.CostEstimate(flops=int(flops), bytes_accessed=moved, transcendentals=0),
    )(scalars, *arguments)


def pack(first, second):
    main = first.shape[1] // LANES * LANES
    return jnp.concatenate([first[:, :main], second[:, :main], first[:, main:], second[:, main:]], axis=1)


def unpack(both):
    width = both.shape[1] // 2
    main = width // LANES * LANES
    edge = main * 2 + width - main
    first = jnp.concatenate([both[:, :main], both[:, 2 * main : edge]], axis=1)
    rest = both[:, 2 * main :].astype(F32)[:, width - main :].astype(both.dtype)
    second = jnp.concatenate([both[:, main : 2 * main], rest], axis=1)
    return first, second


def reorder(value, place, n_dp):
    width = value.shape[1]
    lane = lax.broadcasted_iota(jnp.int32, (1, width), 1)
    span = width // n_dp
    bit = 1
    while bit < n_dp:
        low = lax.rem(lane, 2 * span) < span
        other = jnp.where(low, pltpu.roll(value, width - span, 1), pltpu.roll(value, span, 1))
        value = jnp.where((place & bit) != 0, other, value)
        bit, span = 2 * bit, 2 * span
    return value


def row_mean(value):
    return jnp.sum(value, axis=1, keepdims=True) * (1.0 / value.shape[1])


def normalize(value):
    inverse = lax.rsqrt(row_mean(value * value) + EPSILON)
    return value * inverse, inverse


def norm_back(grad_normed, normed, inverse, gain):
    scaled = grad_normed * gain
    return inverse * (scaled - normed * row_mean(scaled * normed))


def load(sources, targets, sem):
    copies = [pltpu.make_async_copy(a, b, sem.at[k]) for k, (a, b) in enumerate(zip(sources, targets))]
    for copy in copies:
        copy.start()
    for copy in copies:
        copy.wait()


def pack_kernel(s, *refs):
    sources, outs, loaded = refs[:6], refs[6:9], refs[9:15]
    load(sources, loaded, refs[15])
    for k, out in enumerate(outs):
        out[...] = pack(loaded[2 * k][...].astype(F32), loaded[2 * k + 1][...].astype(F32)).astype(BF16)


def row_of(ref):
    return jnp.concatenate([ref[k : k + 1] for k in range(ref.shape[0])], axis=1)


def prepare_kernel(n_dp, s, scale, *refs):
    sources, (h, x_own, grad, vectors, biases) = refs[:9], refs[9:14]
    x, cotangent, *given = refs[14:23]
    load(sources, refs[14:23], refs[23])
    mine, place, length = s[0], s[1], s[2]
    value = reorder(x[...].astype(F32), mine, n_dp)
    stacked = jnp.concatenate([row_of(given[k]) for k in (0, 1, 2, 3, 4, 5, 6, 6)], axis=0)
    width = biases.shape[1]
    slices = stacked[:, :width]
    for number in range(1, stacked.shape[1] // width):
        slices = jnp.where(place == number, stacked[:, number * width : (number + 1) * width], slices)
    biases[...] = slices
    biases[7:8] = scale[...]
    stacked = reorder(stacked, mine, n_dp)
    normed, _ = normalize(value)
    h[...] = (normed * stacked[0:1]).astype(BF16)
    x_own[...] = value.astype(BF16)
    rows = value.shape[0]
    row = lax.broadcasted_iota(jnp.int32, value.shape, 0) + place * rows
    g = jnp.where(row < length, reorder(cotangent[...].astype(F32), mine, n_dp), 0.0)
    grad[...] = g.astype(BF16)
    vectors[...] = stacked
    vectors[4:5] = jnp.sum(g, axis=0, keepdims=True)


def join(pieces, out):
    rows = pieces[0].shape[0]
    for number, piece in enumerate(pieces):
        out[pl.ds(number * rows, rows)] = piece[...]


def tiles(rows, body, size=128):
    def step(m, carry):
        body(pl.ds(pl.multiple_of(m * size, size), size), m)
        return carry

    lax.fori_loop(0, rows // size, step, 0)


def positions(shape, axis, place, local, offset=0):
    row = lax.broadcasted_iota(jnp.int32, shape, axis) + offset
    shift = local.bit_length() - 1
    block = row >> shift
    turned = ((block & 1) << 1) | (block >> 1)
    return ((place ^ turned) << shift) + (row & (local - 1))


def fetch(even, odd, out, depth, sem):
    copies = []
    if not odd:
        copies.append(pltpu.make_async_copy(even[0], out, sem.at[0]))
    else:
        for start, blocks in enumerate((even, odd)):
            row = start * depth
            for block in blocks:
                for k in range(block.shape[0] // depth):
                    source, target = block.at[pl.ds(k * depth, depth)], out.at[pl.ds(row, depth)]
                    copies.append(pltpu.make_async_copy(source, target, sem.at[len(copies)]))
                    row += 2 * depth
    for one in copies:
        one.start()
    return copies


def stack_kernel(s, *refs):
    join(refs[:-1], refs[-1])


def of_head(value, number, head_size):
    lanes = lax.broadcasted_iota(jnp.int32, (1, value.shape[1]), 1) // head_size
    return jnp.where(lanes == number, value, jnp.zeros((), value.dtype))


def attend_kernel(counts, depth, head_size, s, p0, p1, p2, p3, biases, *refs):
    even, odd = refs[: counts[0]], refs[counts[0] : counts[1]]
    q_raw, q_low, k_low, h, weight, turned, sem = refs[counts[1] :]
    copies = fetch(even, odd, weight, depth, sem)
    join((p0, p1, p2, p3), h)
    for copy in copies:
        copy.wait()
    first, second = unpack(dot(h[...], weight[...]))
    first = first + biases[4:5]
    q_raw[...] = first
    q_low[...] = (first * biases[7:8]).astype(BF16)
    k_low[...] = second.astype(BF16)
    place, length = s[1], s[2]
    rows, local = q_low.shape[0], p0.shape[0]
    key_place = positions((rows, 1), 0, place, local)
    last = jnp.minimum(positions((1, rows), 1, place, local), length - 1)

    def head(number, carry):
        score = dot(k_low[...], of_head(q_low[...], number, head_size), NT)
        score = jnp.where(key_place <= last, score, -1e30)
        raised = jnp.exp(score - jnp.max(score, axis=0, keepdims=True))
        share = 1.0 / jnp.sum(raised, axis=0, keepdims=True)
        turned[number] = (raised * share).astype(BF16)
        return carry

    for number in range(turned.shape[0]):
        head(number, 0)


def mixed_heads(turned, value, head_size, dims):
    total = None
    for number in range(turned.shape[0]):
        term = dot(turned[number], of_head(value, number, head_size), dims)
        total = term if total is None else total + term
    return total


def split_weight(weight, one, two):
    one[...], two[...] = unpack(weight[...])


def context_kernel(counts, depth, head_size, s, h, turned, biases, *refs):
    even, odd = refs[: counts[0]], refs[counts[0] : counts[1]]
    v_low, context, far, near, w_value, w_output, weight, sem = refs[counts[1] :]
    for copy in fetch(even, odd, weight, depth, sem):
        copy.wait()
    split_weight(weight, w_value, w_output)
    v_low[...] = (dot(h[...], w_value[...]) + biases[5:6]).astype(BF16)
    context[...] = mixed_heads(turned, v_low[...], head_size, TN).astype(BF16)
    split_product(context, w_output, far, near)


def split_product(left, right, far, near, extra=None, along=None):
    half, total = near.shape[0], None
    for start, out in ((half, far), (0, near)):
        at = pl.ds(start, half)
        value = dot(left[at], right[...], NT)
        if extra is not None:
            value = value + dot(extra[0][at], extra[1][...], NT)
        out[...] = value.astype(out.dtype)
        if along is not None:
            summed = jnp.sum(value * along[at].astype(F32), axis=0, keepdims=True)
            total = summed if total is None else total + summed
    return total


def middle_kernel(s, near, got, send, keep):
    rows = send.shape[0]
    send[...] = (near[rows:] + got[rows:].astype(F32)).astype(BF16)
    keep[...] = near[:rows] + got[:rows].astype(F32)


def second_norm_kernel(s, keep, got, x_own, vectors, x_one, h):
    value = x_own[...].astype(F32) + keep[...] + got[...].astype(F32) + vectors[2:3]
    x_one[...] = value
    normed, _ = normalize(value)
    h[...] = (normed * vectors[1:2]).astype(BF16)


def grad_act_kernel(counts, depth, s, p0, p1, p2, p3, *refs):
    even, odd = refs[: counts[0]], refs[counts[0] : counts[1]]
    grad_act, g, w_hidden, w_down, weight, sem = refs[counts[1] :]
    copies = fetch(even, odd, weight, depth, sem)
    join((p0, p1, p2, p3), g)
    for copy in copies:
        copy.wait()
    split_weight(weight, w_hidden, w_down)
    grad_act[...] = dot(g[...], w_down[...])


def hidden_kernel(s, p0, p1, p2, p3, w_hidden, biases, grad_act, out_far, out_near, act, grad_pre, h):
    join((p0, p1, p2, p3), h)
    pre = dot(h[...], w_hidden[...]) + biases[6:7]
    sigma = jax.nn.sigmoid(pre)
    act[...] = (pre * sigma).astype(BF16)
    grad_pre[...] = (grad_act[...] * (sigma * (1.0 + pre * (1.0 - sigma)))).astype(BF16)
    split_product(grad_pre, w_hidden, out_far, out_near)


PAIR_FIRST = (3, 1, 2, 0)
RING_SENT, RING_KEPT = ((3, 1), (1, 1), (3, 0), (1, 0)), ((2, 1), (0, 1), (2, 0), (0, 0))


def spread_terms(term, outs, depth):
    if len(outs) == 1:
        outs[0][...] = term
        return
    pair_sent, pair_kept, ring_sent, ring_kept = outs
    cut = pair_kept.shape[1]

    def copy(out, at, block, columns):
        out[pl.ds(at * depth, depth)] = term[block * depth : (block + 1) * depth, columns]

    for at, j in enumerate(PAIR_FIRST):
        copy(pair_sent, at, 2 * j + 1, slice(0, cut))
        copy(pair_kept, at, 2 * j, slice(0, cut))
    for at in range(4):
        (j, i), (k, m) = RING_SENT[at], RING_KEPT[at]
        copy(ring_sent, at, 2 * j + i, slice(cut, None))
        copy(ring_kept, at, 2 * k + m, slice(cut, None))


def two_terms(left_one, right_one, left_two, right_two):
    first = dot(left_one[...], right_one[...], TN)
    second = dot(left_two[...], right_two[...], TN)
    return pack(first, second).astype(BF16)


def down_kernel(depth, s, h, g, act, grad_pre, b_hidden, *outs):
    spread_terms(two_terms(h, grad_pre, g, act), outs, depth)
    b_hidden[...] = jnp.sum(grad_pre[...].astype(F32), axis=0, keepdims=True)


def mixer_kernel(s, act, w_down, far, near):
    split_product(act, w_down, far, near)


def owned_kernel(n_got, s, keep, *refs):
    total = keep[...]
    for got in refs[:n_got]:
        total = total + got[pl.ds(0, total.shape[0])].astype(F32)
    refs[n_got][...], refs[n_got + 1][...] = unpack(total)


def grad_middle_kernel(s, keep, got, x_one, grad, vectors, grad_low, grad_full, sums):
    normed, inverse = normalize(x_one[...])
    grad_h = keep[...] + got[...].astype(F32)
    full = grad[...].astype(F32) + norm_back(grad_h, normed, inverse, vectors[1:2])
    grad_full[...] = full
    grad_low[...] = full.astype(BF16)
    sums[...] = vectors[...]
    sums[5:6] = jnp.sum(full, axis=0, keepdims=True)
    sums[6:7] = jnp.sum(grad_h * normed, axis=0, keepdims=True)


def grad_context_kernel(depth, head_size, s, p0, p1, p2, p3, w_output, turned, context, h, *refs):
    grad_context, grad_value, gm, *outs = refs
    join((p0, p1, p2, p3), gm)
    grad_context[...] = dot(gm[...], w_output[...]).astype(BF16)
    grad_value[...] = mixed_heads(turned, grad_context[...], head_size, NN).astype(BF16)
    spread_terms(two_terms(h, grad_value, gm, context), outs, depth)


def grad_scores_kernel(head_size, s, turned, grad_context, v_low, q_low, k_low, q_raw, biases, *refs):
    grad_qk, sums, scores = refs
    rows = q_low.shape[0]
    grad_q = grad_k = 0.0
    for number in range(turned.shape[0]):
        grad_chance = dot(v_low[...], of_head(grad_context[...], number, head_size), NT)
        chance = turned[number].astype(F32)
        product = chance * grad_chance
        center = jnp.sum(product, axis=0, keepdims=True)
        scores[...] = (product - chance * center).astype(BF16)
        grad_q = grad_q + dot(scores[...], of_head(k_low[...], number, head_size), TN)
        grad_k = grad_k + dot(scores[...], of_head(q_low[...], number, head_size))
    low = grad_q.astype(BF16).astype(F32)
    sums[0:1] = jnp.sum(low * q_raw[...], axis=0, keepdims=True)
    low = (low * biases[7:8]).astype(BF16).astype(F32)
    grad_qk[...] = pack(low, grad_k).astype(BF16)
    sums[1:2] = jnp.sum(low, axis=0, keepdims=True)


def grad_first_kernel(
    n_dp, depth, s, grad_qk, w_qk, grad_value, w_value, h, sums_in, sums_q, b_hidden, slope, *refs
):
    far, near, sums, *outs = refs
    spread_terms(dot(h[...], grad_qk[...], TN).astype(BF16), outs, depth)
    mine, place = s[0], s[1]
    gained = split_product(grad_qk, w_qk, far, near, (grad_value, w_value), h) / sums_in[0:1]
    row = lax.broadcasted_iota(jnp.int32, sums.shape, 0)
    sums[...] = reorder(jnp.where(row == 7, gained, sums_in[...]), mine, n_dp)
    sums[0:4] = jnp.zeros((4, sums.shape[1]), F32)
    local_width, head_size = sums_q.shape[1], slope.shape[1]
    b_value = jnp.sum(grad_value[...].astype(F32), axis=0, keepdims=True)
    share = jnp.concatenate([sums_q[1:2], b_value, b_hidden[...]], axis=0)
    for number in range(sums.shape[1] // local_width):

        @pl.when(place == number)
        def _():
            sums[0:3, number * local_width : (number + 1) * local_width] = share

    scale = sums_q[0:1]
    total = scale[:, :head_size]
    for number in range(1, local_width // head_size):
        total = total + scale[:, number * head_size : (number + 1) * head_size]
    sums[3:4, :head_size] = total * slope[...]
    if len(outs) > 1:
        outs[0][pl.ds(4 * depth, 32)] = fold(sums[...], outs[0].shape[1])


def fold(vectors, width):
    part = vectors.shape[1] // 4
    rows = jnp.concatenate([vectors[:, k * part : (k + 1) * part] for k in range(4)], axis=0)
    return jnp.concatenate([rows, jnp.zeros((32, width - part), F32)], axis=1).astype(BF16)


def unfold(rows, part):
    return jnp.concatenate([rows[8 * k : 8 * k + 8, :part] for k in range(4)], axis=1)


def first_sum_kernel(s, pair_kept, pair_got, ring_kept, ring_got, *refs):
    *given, pair_out, pair_mid, ring_out, ring_mid = refs
    half = pair_mid.shape[0]
    value = pair_kept[...].astype(F32) + pair_got[pl.ds(0, 2 * half)].astype(F32)
    pair_out[pl.ds(0, half)] = value[:half].astype(BF16)
    pair_mid[...] = value[half:]
    value = ring_kept[...].astype(F32) + ring_got[...].astype(F32)
    ring_out[...] = value[:half].astype(BF16)
    ring_mid[...] = value[half:]
    if given:
        low = fold(given[0][...], pair_out.shape[1]).astype(F32) + pair_got[pl.ds(2 * half, 32)].astype(F32)
        pair_out[pl.ds(half, 32)] = low.astype(BF16)


def second_sum_kernel(s, pair_mid, pair_got, ring_mid, ring_got, *refs):
    half, depth, cut = pair_mid.shape[0], pair_mid.shape[0] // 2, pair_mid.shape[1]
    given, out, zero = refs[: len(refs) // 3], refs[len(refs) // 3], refs[len(refs) // 3 + 1]
    pair = pair_mid[...] + pair_got[pl.ds(0, half)].astype(F32)
    ring = ring_mid[...] + ring_got[...].astype(F32)
    out[:, :cut], out[:, cut:] = pair[:depth].astype(BF16), ring[:depth].astype(BF16)
    zero[:, :cut], zero[:, cut:] = pair[depth:], ring[depth:]
    if given:
        at, vectors = pl.ds(half, 32), refs[-1]
        vectors[...] = unfold(given[0][at].astype(F32) + pair_got[at].astype(F32), vectors.shape[1] // 4)


def total_kernel(s, one, two, *outs):
    total = one[...] + two[...]
    for out, row in zip(outs[:7], (0, 1, 2, 6, 4, 5, 7)):
        for k in range(out.shape[0]):
            out[k : k + 1] = total[row : row + 1, k * LANES : (k + 1) * LANES]
    outs[7][...] = total[3:4, : outs[7].shape[1]]


def last_kernel(n_dp, s, keep, got, x_own, grad_full, sums_in, grad_in):
    normed, inverse = normalize(x_own[...].astype(F32))
    grad_h = keep[...] + got[...].astype(F32)
    full = grad_full[...] + norm_back(grad_h, normed, inverse, sums_in[0:1])
    grad_in[...] = reorder(full, s[0], n_dp).astype(BF16)


def add_kernel(s, one, two, out):
    out[...] = one[...] + two[...]


def output_kernel(n_dp, s, keep, got, x_one, vectors, out):
    value = x_one[...] + keep[...] + got[...].astype(F32) + vectors[3:4]
    out[...] = reorder(value, s[0], n_dp).astype(BF16)


def tie(*values):
    return lax.optimization_barrier(values)


class Links:
    def __init__(self, n_dp, n_tensor):
        self.n_dp, self.n_tensor = n_dp, n_tensor
        self.wide = n_dp > 8

    def move(self, value, target):
        pairs = []
        for d in range(self.n_dp):
            for t in range(self.n_tensor):
                to_d, to_t = target(d, t)
                pairs.append((d * self.n_tensor + t, to_d * self.n_tensor + to_t))
        return lax.ppermute(value, AXES, pairs)

    def chip(self, value):
        return self.move(value, lambda d, t: (d, t ^ 2))

    def core(self, value):
        return self.move(value, lambda d, t: (d, t ^ 1))

    def pair(self, value):
        return self.along(value, 1)

    def along(self, value, bits):
        return self.move(value, lambda d, t: (d ^ bits, t))

    def gather_tensor(self, rows):
        near = self.chip(rows)
        return rows, near, self.core(rows), self.core(near)

    def gather_wide(self, shard):
        blocks, place = lax.all_gather(shard, "dp", axis=0), lax.axis_index("dp")
        return jnp.take(blocks, lax.iota(jnp.int32, self.n_dp) ^ place, axis=0).reshape(-1, shard.shape[1])

    def scatter_wide(self, total):
        place = lax.axis_index("dp")
        blocks = total.reshape(self.n_dp, total.shape[0] // self.n_dp, total.shape[1])
        blocks = jnp.take(blocks, lax.iota(jnp.int32, self.n_dp) ^ place, axis=0).astype(F32)
        return unpack(lax.psum_scatter(blocks.reshape(total.shape), "dp", scatter_dimension=0, tiled=True))

    def steps(self):
        found, bit = [], 1
        while bit < self.n_dp and self.wide:
            found.append(lambda d, t, bit=bit: (d ^ bit, t))
            bit *= 2
        far = [] if self.wide else [lambda d, t: (d ^ 4, t)]
        return found + [lambda d, t: (d, t ^ 1), lambda d, t: (d, t ^ 2)] + far


def body(
    inputs,
    weight_query,
    weight_key,
    weight_value,
    weight_output,
    weight_hidden,
    weight_down,
    bias_query,
    bias_value,
    bias_hidden,
    bias_output,
    bias_final,
    gain_attention,
    gain_mixer,
    query_scale,
    lengths,
    cotangent,
    n_dp,
    n_tensor,
):
    links = Links(n_dp, n_tensor)
    wide = links.wide
    local_rows, width = inputs.shape
    all_rows = local_rows * n_tensor
    depth = width // n_dp
    local_width = weight_query.shape[1]
    both = 2 * local_width
    head_size = query_scale.shape[0]
    heads = local_width // head_size
    dp_index = lax.axis_index("dp")
    tensor_index = lax.axis_index("tensor")
    s = jnp.stack([dp_index, tensor_index, lengths[0]])
    product = 2 * all_rows * width * local_width
    mixed = 2 * all_rows * all_rows * local_width

    def run(name, kernel, outs, *arguments, **rest):
        return call(name, kernel, [shaped(*o) for o in outs], s, *arguments, **rest)

    def bind(kernel, *fixed):
        def bound(*refs):
            return kernel(*fixed, *refs)

        return bound

    packed = [((depth, both), BF16)]
    rows_low, rows_full = ((local_rows, width), BF16), ((local_rows, width), F32)
    split = [((all_rows // 2, width), BF16), ((all_rows // 2, width), F32)]
    part = ((all_rows, local_width), BF16)
    part_full = ((all_rows, local_width), F32)
    whole_rows = ((all_rows, width), BF16)
    weight = ((width, local_width), BF16)
    vector = ((8, width), F32)
    halves = [((width // 2, both), BF16)] * 2
    term = [pltpu.VMEM((width, both), BF16)]
    sems = [pltpu.SemaphoreType.DMA((n_dp,))]

    unit = SOFTPLUS_UNIT / jnp.sqrt(F32(head_size))
    scale_wide = jnp.tile(jax.nn.softplus(query_scale) * unit, heads)[None]
    slope = (jax.nn.sigmoid(query_scale) * unit)[None]
    def apart(value):
        return pltpu.with_memory_space_constraint(value, pltpu.HBM)

    weights = (weight_query, weight_key, weight_value, weight_output.T, weight_hidden, weight_down.T)
    own_qk, own_vo, own_hd = run(
        "pack",
        pack_kernel,
        packed * 3,
        *(apart(w) for w in weights),
        remote=6,
        scratch=[pltpu.VMEM((depth, local_width), BF16)] * 6 + [pltpu.SemaphoreType.DMA((6,))],
    )
    given = (gain_attention, gain_mixer, bias_output, bias_final, bias_query, bias_value, bias_hidden)
    scale_wide, slope = tie(scale_wide, slope)
    tall = (width // LANES, LANES)
    h_own, x_own, grad_own, vectors, biases = run(
        "prepare",
        bind(prepare_kernel, n_dp),
        [rows_low, rows_low, rows_low, vector, ((8, local_width), F32)],
        scale_wide,
        *(apart(v) for v in (inputs, cotangent, *(v.reshape(tall) for v in given))),
        remote=9,
        scratch=[pltpu.VMEM((local_rows, width), BF16)] * 2
        + [pltpu.VMEM(tall, F32)] * 7
        + [pltpu.SemaphoreType.DMA((9,))],
    )

    def stack(*blocks):
        rows = sum(block.shape[0] for block in blocks)
        return run("stack", stack_kernel, [((rows, both), BF16)], *blocks)[0]

    if wide:
        qk, vo, hd = (([links.gather_wide(own)], []) for own in (own_qk, own_vo, own_hd))
        h_one, grad_rows = links.gather_tensor(h_own), links.gather_tensor(grad_own)
    else:
        qk_one, qk_two = links.along(own_qk, 2), links.along(own_qk, 4)
        hd_pair = links.pair(own_hd)
        h_own, own_vo, own_hd, qk_one, qk_two, hd_pair = tie(h_own, own_vo, own_hd, qk_one, qk_two, hd_pair)
        h_chip = links.chip(h_own)
        qk_three = links.along(qk_two, 2)
        near_qk_pair = links.pair(stack(own_qk, qk_one))
        vo_two, vo_pair = links.along(own_vo, 4), links.pair(own_vo)
        far_stack = stack(qk_two, qk_three)
        far_stack, near_qk_pair = tie(far_stack, near_qk_pair)
        h_chip, vo_two, vo_pair, own_vo = tie(h_chip, vo_two, vo_pair, own_vo)
        h_one = h_own, h_chip, links.core(h_own), links.core(h_chip)
        far_qk_pair = links.pair(far_stack)
        vo_one, vo_three = links.along(own_vo, 2), links.along(vo_two, 2)
        qk = [own_qk, qk_one, qk_two, qk_three], [near_qk_pair, far_qk_pair]
        h_one, qk, vo_three, own_hd = tie(h_one, qk, vo_three, own_hd)
        near_vo_pair = links.pair(vo_one)
        hd_one, hd_two = links.along(own_hd, 2), links.along(own_hd, 4)
        grad_chip = links.chip(grad_own)
    n_qk = len(qk[0]), len(qk[0]) + len(qk[1])
    q_raw, q_low, k_low, h_all, w_qk, turned = run(
        "attend",
        bind(attend_kernel, n_qk, depth, head_size),
        [
            part_full,
            part,
            part,
            whole_rows,
            ((width, both), BF16),
            ((heads, all_rows, all_rows), BF16),
        ],
        *h_one,
        biases,
        *qk[0],
        *qk[1],
        remote=n_qk[1],
        scratch=sems,
    )
    if not wide:
        turned, near_vo_pair, hd_one, hd_two, grad_chip = tie(turned, near_vo_pair, hd_one, hd_two, grad_chip)
        far_vo_pair = links.pair(stack(vo_two, vo_three))
        hd_three = links.along(hd_two, 2)
        grad_rows = grad_own, grad_chip, links.core(grad_own), links.core(grad_chip)
        vo = [own_vo, vo_one, vo_two, vo_three], [vo_pair, near_vo_pair, far_vo_pair]
        turned, vo, grad_rows = tie(turned, vo, grad_rows)
        near_hd_pair = links.pair(hd_one)
    n_vo = len(vo[0]), len(vo[0]) + len(vo[1])
    v_low, context, far, near, w_value, w_output = run(
        "context",
        bind(context_kernel, n_vo, depth, head_size),
        [part, part, *split, weight, weight],
        h_all,
        turned,
        biases,
        *vo[0],
        *vo[1],
        remote=n_vo[1],
        scratch=term + sems,
    )

    def core_half(far, near, *extra):
        got, *extra = tie(links.core(far), *extra)
        return list(run("middle", middle_kernel, [rows_low, rows_full], near, got)) + list(extra)

    if wide:
        send, keep = core_half(far, near)
        got = links.chip(send)
    else:
        far, near_hd_pair, hd_three = tie(far, near_hd_pair, hd_three)
        send, keep = core_half(far, near)
        got = links.chip(send)
        far_hd_pair = links.pair(stack(hd_two, hd_three))
        hd = [own_hd, hd_one, hd_two, hd_three], [hd_pair, near_hd_pair, far_hd_pair]
        got, hd = tie(got, hd)
    n_hd = len(hd[0]), len(hd[0]) + len(hd[1])
    x_one, h_two_own = run("second_norm", second_norm_kernel, [rows_full, rows_low], keep, got, x_own, vectors)
    h_two_chip = links.chip(h_two_own)
    grad_act, grad_all, w_hidden, w_down = run(
        "grad_act",
        bind(grad_act_kernel, n_hd, depth),
        [part_full, whole_rows, weight, weight],
        *grad_rows,
        *hd[0],
        *hd[1],
        remote=n_hd[1],
        scratch=term + sems,
    )
    h_two_chip, grad_act = tie(h_two_chip, grad_act)
    h_two = h_two_own, h_two_chip, links.core(h_two_own), links.core(h_two_chip)
    far, near, act, grad_pre, h_two_all = run(
        "hidden",
        hidden_kernel,
        [*split, part, part, whole_rows],
        *h_two,
        w_hidden,
        biases,
        grad_act,
    )
    cut = 3 * both // 5
    tall_sent = n_dp // 2 * depth
    terms = [((width, both), BF16)]
    if not wide:
        terms = [((tall_sent, c), BF16) for c in (cut, cut, both - cut, both - cut)]
    grad_b_hidden, *terms_hd = run(
        "down",
        bind(down_kernel, depth),
        [((1, local_width), F32), *terms],
        h_two_all,
        grad_all,
        act,
        grad_pre,
    )
    send, keep, terms_hd = core_half(far, near, terms_hd)
    got = links.chip(send)
    act, keep = tie(act, keep)
    mix_far, mix_near = run("mixer", mixer_kernel, split, act, w_down)
    got, mix_far = tie(got, mix_far)

    def first_send(terms):
        return [links.pair(terms[0]), links.along(terms[2], 2)]

    def first_sum(name, terms, got, given=()):
        rows = tall_sent // 2
        extra = 32 if given else 0
        outs = [((rows + extra, cut), BF16), ((rows, cut), F32), ((rows, both - cut), BF16), ((rows, both - cut), F32)]
        return run("first_" + name, first_sum_kernel, outs, terms[1], got[0], terms[3], got[1], *given)

    def second_send(sums):
        return [links.along(sums[0], 2), links.pair(sums[2])]

    def second_sum(name, sums, got, given=False):
        outs = packed + [((depth, both), F32)] + ([vector] if given else [])
        more = sums[:1] if given else []
        return run("second_" + name, second_sum_kernel, outs, sums[1], got[0], sums[3], got[1], *more)

    def owned(name, *parts):
        outs = [((depth, local_width), F32)] * 2
        return run("owned_" + name, bind(owned_kernel, len(parts) - 1), outs, *parts)

    if not wide:
        got_hd = first_send(terms_hd)
        got, got_hd = tie(got, got_hd)
    grad_mid_low, grad_mid, sums = run(
        "grad_middle",
        grad_middle_kernel,
        [rows_low, rows_full, vector],
        keep,
        got,
        x_one,
        grad_own,
        vectors,
    )
    if wide:
        grad_mid_rows = links.gather_tensor(grad_mid_low)
    else:
        grad_mid_chip = links.chip(grad_mid_low)
        sums_hd = first_sum("hd", terms_hd, got_hd)
        got_hd = second_send(sums_hd)
        grad_mid_chip, got_hd = tie(grad_mid_chip, got_hd)
        sent_hd, zero_hd = second_sum("hd", sums_hd, got_hd)
        grad_mid_rows = grad_mid_low, grad_mid_chip, links.core(grad_mid_low), links.core(grad_mid_chip)
    if wide:
        grad_mid_rows, mix_far = tie(grad_mid_rows, mix_far)
    else:
        grad_mid_rows, mix_far, sent_hd = tie(grad_mid_rows, mix_far, sent_hd)
    mix_send, mix_keep = core_half(mix_far, mix_near)
    mix_got = links.chip(mix_send)
    grad_context, grad_value, _, *terms_vo = run(
        "grad_context",
        bind(grad_context_kernel, depth, head_size),
        [part, part, whole_rows, *terms],
        *grad_mid_rows,
        w_output,
        turned,
        context,
        h_all,
    )
    if not wide:
        got_vo = first_send(terms_vo)
        grad_context, sent_hd = tie(grad_context, sent_hd)
        part_hd = links.along(sent_hd, 4)
    grad_qk, sums_q = run(
        "grad_scores",
        bind(grad_scores_kernel, head_size),
        [((all_rows, both), BF16), ((8, local_width), F32)],
        turned,
        grad_context,
        v_low,
        q_low,
        k_low,
        q_raw,
        biases,
        scratch=[pltpu.VMEM((all_rows, all_rows), BF16)],
    )
    if wide:
        grad_qk, mix_got = tie(grad_qk, mix_got)
    else:
        grad_qk, mix_got, got_vo = tie(grad_qk, mix_got, got_vo)
    terms_first = list(terms)
    if not wide:
        terms_first[0] = ((tall_sent + 32, cut), BF16)
    far, near, sums, *terms_qk = run(
        "grad_first",
        bind(grad_first_kernel, n_dp, depth),
        [*split, vector, *terms_first],
        grad_qk,
        w_qk,
        grad_value,
        w_value,
        h_all,
        sums,
        sums_q,
        grad_b_hidden,
        slope,
    )
    def exchange(value, step):
        return run("add", add_kernel, [vector], value, links.move(value, step))[0]

    total = sums
    if wide:
        send, keep = core_half(far, near)
        got = links.chip(send)
    else:
        got_qk = first_send(terms_qk)
        far, part_hd, *got_vo = tie(far, part_hd, *got_vo)
        sums_vo = first_sum("vo", terms_vo, got_vo)
        send, keep, *sums_vo = core_half(far, near, *sums_vo)
        got_vo = second_send(sums_vo)
        got = links.chip(send)
        (output,) = run("output", bind(output_kernel, n_dp), [rows_low], mix_keep, mix_got, x_one, vectors)
        grad_hidden, grad_down = owned("hd", zero_hd, part_hd)
        got_qk, got, output, grad_hidden = tie(got_qk, got, output, grad_hidden)
        got_qk, got_vo = tie(got_qk, got_vo)
        sums_qk = first_sum("qk", terms_qk, got_qk, [sums])
        got_qk = second_send(sums_qk)
        (grad_in,) = run("last", bind(last_kernel, n_dp), [rows_low], keep, got, x_own, grad_mid, vectors)
        got_qk, grad_in = tie(got_qk, grad_in)
        sent_vo, zero_vo = second_sum("vo", sums_vo, got_vo)
        part_vo = links.along(sent_vo, 4)
        sent_qk, zero_qk, total = second_sum("qk", sums_qk, got_qk, True)
        far_qk = links.along(sent_qk, 4)
        zero_vo, total = tie(zero_vo, total)
    if wide:
        (grad_in,) = run("last", bind(last_kernel, n_dp), [rows_low], keep, got, x_own, grad_mid, vectors)
    if wide:
        (output,) = run("output", bind(output_kernel, n_dp), [rows_low], mix_keep, mix_got, x_one, vectors)
    steps = links.steps()
    for step in steps[:-1]:
        total = exchange(total, step)
    moved = links.move(total, steps[-1])
    if not wide:
        grad_query, grad_key = owned("qk", zero_qk, far_qk)
        moved, grad_query = tie(moved, grad_query)
    tall_vector = (tall, F32)
    *totals, total_scale = run(
        "total", total_kernel, [tall_vector] * 7 + [((1, head_size), F32)], total, moved
    )
    totals = [v.reshape(width) for v in totals]
    if wide:
        grad_hidden, grad_down = links.scatter_wide(terms_hd[0])
        grad_output_v, grad_output_o = links.scatter_wide(terms_vo[0])
        grad_query, grad_key = links.scatter_wide(terms_qk[0])
    else:
        grad_output_v, grad_output_o = owned("vo", zero_vo, part_vo)
    return (
        output,
        grad_in,
        grad_query,
        grad_key,
        grad_output_v,
        grad_output_o.T,
        grad_hidden,
        grad_down.T,
        totals[0],
        totals[1],
        totals[2],
        totals[5],
        totals[4],
        totals[6],
        totals[3],
        total_scale.reshape(head_size),
    )


def solution(mesh):
    n_dp, n_tensor = mesh.shape["dp"], mesh.shape["tensor"]

    def local(*arguments):
        return body(*arguments, n_dp, n_tensor)

    rows = P(("dp", "tensor"), None)
    into, out_of = P("dp", "tensor"), P("tensor", "dp")
    return jax.shard_map(
        local,
        mesh=mesh,
        in_specs=(rows, into, into, into, out_of, into, out_of, *[P()] * 8, P("dp"), rows),
        out_specs=(rows, rows, into, into, into, out_of, into, out_of, *[P()] * 8),
        check_vma=False,
    )
```

```python
import jax
import jax.numpy as jnp
from jax import lax
from jax.experimental import pallas as pl
from jax.experimental.pallas import tpu as pltpu
from jax.sharding import PartitionSpec as P

EPSILON = 1e-06
SOFTPLUS_UNIT = 1.442695041
AXES = ("dp", "tensor")
F32 = jnp.float32
BF16 = jnp.bfloat16
LANES = 128
TENSOR_ORDER = (0, 2, 1, 3)
NN, NT, TN = ((1,), (0,)), ((1,), (1,)), ((0,), (0,))


def dot(left, right, dims=NN):
    return lax.dot_general(left, right, (dims, ((), ())), preferred_element_type=F32)


def shaped(shape, kind):
    return jax.ShapeDtypeStruct(shape, kind)


def call(name, kernel, outs, scalars, *arguments, flops=1e6, scratch=(), limit=12, remote=0):
    space = pl.BlockSpec(memory_space=pltpu.VMEM)
    apart = pl.BlockSpec(memory_space=pltpu.HBM)
    moved = sum(a.size * a.dtype.itemsize for a in (*arguments, *outs))
    return pl.pallas_call(
        kernel,
        name=name,
        out_shape=outs,
        in_specs=[pl.BlockSpec(memory_space=pltpu.SMEM)]
        + [space] * (len(arguments) - remote)
        + [apart] * remote,
        out_specs=[space] * len(outs),
        scratch_shapes=scratch,
        compiler_params=pltpu.CompilerParams(vmem_limit_bytes=limit << 20),
        cost_estimate=pl.CostEstimate(flops=int(flops), bytes_accessed=moved, transcendentals=0),
    )(scalars, *arguments)


def pack(first, second):
    main = first.shape[1] // LANES * LANES
    return jnp.concatenate([first[:, :main], second[:, :main], first[:, main:], second[:, main:]], axis=1)


def unpack(both):
    width = both.shape[1] // 2
    main = width // LANES * LANES
    edge = main * 2 + width - main
    first = jnp.concatenate([both[:, :main], both[:, 2 * main : edge]], axis=1)
    rest = both[:, 2 * main :].astype(F32)[:, width - main :].astype(both.dtype)
    second = jnp.concatenate([both[:, main : 2 * main], rest], axis=1)
    return first, second


def reorder(value, place, n_dp):
    width = value.shape[1]
    lane = lax.broadcasted_iota(jnp.int32, (1, width), 1)
    span = width // n_dp
    bit = 1
    while bit < n_dp:
        low = lax.rem(lane, 2 * span) < span
        other = jnp.where(low, pltpu.roll(value, width - span, 1), pltpu.roll(value, span, 1))
        value = jnp.where((place & bit) != 0, other, value)
        bit, span = 2 * bit, 2 * span
    return value


def row_mean(value):
    return jnp.sum(value, axis=1, keepdims=True) * (1.0 / value.shape[1])


def normalize(value):
    inverse = lax.rsqrt(row_mean(value * value) + EPSILON)
    return value * inverse, inverse


def norm_back(grad_normed, normed, inverse, gain):
    scaled = grad_normed * gain
    return inverse * (scaled - normed * row_mean(scaled * normed))


def load(sources, targets, sem):
    copies = [pltpu.make_async_copy(a, b, sem.at[k]) for k, (a, b) in enumerate(zip(sources, targets))]
    for copy in copies:
        copy.start()
    for copy in copies:
        copy.wait()


def pack_kernel(s, *refs):
    sources, outs, loaded = refs[:6], refs[6:9], refs[9:15]
    load(sources, loaded, refs[15])
    for k, out in enumerate(outs):
        out[...] = pack(loaded[2 * k][...].astype(F32), loaded[2 * k + 1][...].astype(F32)).astype(BF16)


def row_of(ref):
    return jnp.concatenate([ref[k : k + 1] for k in range(ref.shape[0])], axis=1)


def prepare_kernel(n_dp, s, scale, *refs):
    sources, (h, x_own, grad, vectors, biases) = refs[:9], refs[9:14]
    x, cotangent, *given = refs[14:23]
    load(sources, refs[14:23], refs[23])
    mine, place, length = s[0], s[1], s[2]
    value = reorder(x[...].astype(F32), mine, n_dp)
    stacked = jnp.concatenate([row_of(given[k]) for k in (0, 1, 2, 3, 4, 5, 6, 6)], axis=0)
    width = biases.shape[1]
    slices = stacked[:, :width]
    for number in range(1, stacked.shape[1] // width):
        slices = jnp.where(place == number, stacked[:, number * width : (number + 1) * width], slices)
    biases[...] = slices
    biases[7:8] = scale[...]
    stacked = reorder(stacked, mine, n_dp)
    normed, _ = normalize(value)
    h[...] = (normed * stacked[0:1]).astype(BF16)
    x_own[...] = value.astype(BF16)
    rows = value.shape[0]
    row = lax.broadcasted_iota(jnp.int32, value.shape, 0) + place * rows
    g = jnp.where(row < length, reorder(cotangent[...].astype(F32), mine, n_dp), 0.0)
    grad[...] = g.astype(BF16)
    vectors[...] = stacked
    vectors[4:5] = jnp.sum(g, axis=0, keepdims=True)


def join(pieces, out):
    rows = pieces[0].shape[0]
    for number, piece in enumerate(pieces):
        out[pl.ds(number * rows, rows)] = piece[...]


def tiles(rows, body, size=128):
    def step(m, carry):
        body(pl.ds(pl.multiple_of(m * size, size), size), m)
        return carry

    lax.fori_loop(0, rows // size, step, 0)


def positions(shape, axis, place, local, offset=0):
    row = lax.broadcasted_iota(jnp.int32, shape, axis) + offset
    shift = local.bit_length() - 1
    block = row >> shift
    turned = ((block & 1) << 1) | (block >> 1)
    return ((place ^ turned) << shift) + (row & (local - 1))


def fetch(even, odd, out, depth, sem):
    copies = []
    if not odd:
        copies.append(pltpu.make_async_copy(even[0], out, sem.at[0]))
    else:
        for start, blocks in enumerate((even, odd)):
            row = start * depth
            for block in blocks:
                for k in range(block.shape[0] // depth):
                    source, target = block.at[pl.ds(k * depth, depth)], out.at[pl.ds(row, depth)]
                    copies.append(pltpu.make_async_copy(source, target, sem.at[len(copies)]))
                    row += 2 * depth
    for one in copies:
        one.start()
    return copies


def stack_kernel(s, *refs):
    join(refs[:-1], refs[-1])


def of_head(value, number, head_size):
    lanes = lax.broadcasted_iota(jnp.int32, (1, value.shape[1]), 1) // head_size
    return jnp.where(lanes == number, value, jnp.zeros((), value.dtype))


def attend_kernel(counts, depth, head_size, s, p0, p1, p2, p3, biases, *refs):
    even, odd = refs[: counts[0]], refs[counts[0] : counts[1]]
    q_raw, q_low, k_low, h, weight, turned, sem = refs[counts[1] :]
    copies = fetch(even, odd, weight, depth, sem)
    join((p0, p1, p2, p3), h)
    for copy in copies:
        copy.wait()
    first, second = unpack(dot(h[...], weight[...]))
    first = first + biases[4:5]
    q_raw[...] = first
    q_low[...] = (first * biases[7:8]).astype(BF16)
    k_low[...] = second.astype(BF16)
    place, length = s[1], s[2]
    rows, local = q_low.shape[0], p0.shape[0]
    key_place = positions((rows, 1), 0, place, local)
    last = jnp.minimum(positions((1, rows), 1, place, local), length - 1)

    def head(number, carry):
        score = dot(k_low[...], of_head(q_low[...], number, head_size), NT)
        score = jnp.where(key_place <= last, score, -1e30)
        raised = jnp.exp(score - jnp.max(score, axis=0, keepdims=True))
        share = 1.0 / jnp.sum(raised, axis=0, keepdims=True)
        turned[number] = (raised * share).astype(BF16)
        return carry

    for number in range(turned.shape[0]):
        head(number, 0)


def mixed_heads(turned, value, head_size, dims):
    total = None
    for number in range(turned.shape[0]):
        term = dot(turned[number], of_head(value, number, head_size), dims)
        total = term if total is None else total + term
    return total


def split_weight(weight, one, two):
    one[...], two[...] = unpack(weight[...])


def context_kernel(counts, depth, head_size, s, h, turned, biases, *refs):
    even, odd = refs[: counts[0]], refs[counts[0] : counts[1]]
    v_low, context, far, near, w_value, w_output, weight, sem = refs[counts[1] :]
    for copy in fetch(even, odd, weight, depth, sem):
        copy.wait()
    split_weight(weight, w_value, w_output)
    v_low[...] = (dot(h[...], w_value[...]) + biases[5:6]).astype(BF16)
    context[...] = mixed_heads(turned, v_low[...], head_size, TN).astype(BF16)
    split_product(context, w_output, far, near)


def split_product(left, right, far, near, extra=None, along=None):
    half, total = near.shape[0], None
    for start, out in ((half, far), (0, near)):
        at = pl.ds(start, half)
        value = dot(left[at], right[...], NT)
        if extra is not None:
            value = value + dot(extra[0][at], extra[1][...], NT)
        out[...] = value.astype(out.dtype)
        if along is not None:
            summed = jnp.sum(value * along[at].astype(F32), axis=0, keepdims=True)
            total = summed if total is None else total + summed
    return total


def middle_kernel(s, near, got, send, keep):
    rows = send.shape[0]
    send[...] = (near[rows:] + got[rows:].astype(F32)).astype(BF16)
    keep[...] = near[:rows] + got[:rows].astype(F32)


def second_norm_kernel(s, keep, got, x_own, vectors, x_one, h):
    value = x_own[...].astype(F32) + keep[...] + got[...].astype(F32) + vectors[2:3]
    x_one[...] = value
    normed, _ = normalize(value)
    h[...] = (normed * vectors[1:2]).astype(BF16)


def grad_act_kernel(counts, depth, s, p0, p1, p2, p3, *refs):
    even, odd = refs[: counts[0]], refs[counts[0] : counts[1]]
    grad_act, g, w_hidden, w_down, weight, sem = refs[counts[1] :]
    copies = fetch(even, odd, weight, depth, sem)
    join((p0, p1, p2, p3), g)
    for copy in copies:
        copy.wait()
    split_weight(weight, w_hidden, w_down)
    grad_act[...] = dot(g[...], w_down[...])


def hidden_kernel(s, p0, p1, p2, p3, w_hidden, biases, grad_act, out_far, out_near, act, grad_pre, h):
    join((p0, p1, p2, p3), h)
    pre = dot(h[...], w_hidden[...]) + biases[6:7]
    sigma = jax.nn.sigmoid(pre)
    act[...] = (pre * sigma).astype(BF16)
    grad_pre[...] = (grad_act[...] * (sigma * (1.0 + pre * (1.0 - sigma)))).astype(BF16)
    split_product(grad_pre, w_hidden, out_far, out_near)


PAIR_FIRST = (3, 1, 2, 0)
RING_SENT, RING_KEPT = ((3, 1), (1, 1), (3, 0), (1, 0)), ((2, 1), (0, 1), (2, 0), (0, 0))


def spread_terms(term, outs, depth):
    if len(outs) == 1:
        outs[0][...] = term
        return
    pair_sent, pair_kept, ring_sent, ring_kept = outs
    cut = pair_kept.shape[1]

    def copy(out, at, block, columns):
        out[pl.ds(at * depth, depth)] = term[block * depth : (block + 1) * depth, columns]

    for at, j in enumerate(PAIR_FIRST):
        copy(pair_sent, at, 2 * j + 1, slice(0, cut))
        copy(pair_kept, at, 2 * j, slice(0, cut))
    for at in range(4):
        (j, i), (k, m) = RING_SENT[at], RING_KEPT[at]
        copy(ring_sent, at, 2 * j + i, slice(cut, None))
        copy(ring_kept, at, 2 * k + m, slice(cut, None))


def two_terms(left_one, right_one, left_two, right_two):
    first = dot(left_one[...], right_one[...], TN)
    second = dot(left_two[...], right_two[...], TN)
    return pack(first, second).astype(BF16)


def down_kernel(depth, s, h, g, act, grad_pre, b_hidden, *outs):
    spread_terms(two_terms(h, grad_pre, g, act), outs, depth)
    b_hidden[...] = jnp.sum(grad_pre[...].astype(F32), axis=0, keepdims=True)


def mixer_kernel(s, act, w_down, far, near):
    split_product(act, w_down, far, near)


def owned_kernel(n_got, s, keep, *refs):
    total = keep[...]
    for got in refs[:n_got]:
        total = total + got[pl.ds(0, total.shape[0])].astype(F32)
    refs[n_got][...], refs[n_got + 1][...] = unpack(total)


def grad_middle_kernel(s, keep, got, x_one, grad, vectors, grad_low, grad_full, sums):
    normed, inverse = normalize(x_one[...])
    grad_h = keep[...] + got[...].astype(F32)
    full = grad[...].astype(F32) + norm_back(grad_h, normed, inverse, vectors[1:2])
    grad_full[...] = full
    grad_low[...] = full.astype(BF16)
    sums[...] = vectors[...]
    sums[5:6] = jnp.sum(full, axis=0, keepdims=True)
    sums[6:7] = jnp.sum(grad_h * normed, axis=0, keepdims=True)


def grad_context_kernel(depth, head_size, s, p0, p1, p2, p3, w_output, turned, context, h, *refs):
    grad_context, grad_value, gm, *outs = refs
    join((p0, p1, p2, p3), gm)
    grad_context[...] = dot(gm[...], w_output[...]).astype(BF16)
    grad_value[...] = mixed_heads(turned, grad_context[...], head_size, NN).astype(BF16)
    spread_terms(two_terms(h, grad_value, gm, context), outs, depth)


def grad_scores_kernel(head_size, s, turned, grad_context, v_low, q_low, k_low, q_raw, biases, *refs):
    grad_qk, sums, scores = refs
    rows = q_low.shape[0]
    grad_q = grad_k = 0.0
    for number in range(turned.shape[0]):
        grad_chance = dot(v_low[...], of_head(grad_context[...], number, head_size), NT)
        chance = turned[number].astype(F32)
        product = chance * grad_chance
        center = jnp.sum(product, axis=0, keepdims=True)
        scores[...] = (product - chance * center).astype(BF16)
        grad_q = grad_q + dot(scores[...], of_head(k_low[...], number, head_size), TN)
        grad_k = grad_k + dot(scores[...], of_head(q_low[...], number, head_size))
    low = grad_q.astype(BF16).astype(F32)
    sums[0:1] = jnp.sum(low * q_raw[...], axis=0, keepdims=True)
    low = (low * biases[7:8]).astype(BF16).astype(F32)
    grad_qk[...] = pack(low, grad_k).astype(BF16)
    sums[1:2] = jnp.sum(low, axis=0, keepdims=True)


def grad_first_kernel(
    n_dp, depth, s, grad_qk, w_qk, grad_value, w_value, h, sums_in, sums_q, b_hidden, slope, *refs
):
    far, near, sums, *outs = refs
    spread_terms(dot(h[...], grad_qk[...], TN).astype(BF16), outs, depth)
    mine, place = s[0], s[1]
    gained = split_product(grad_qk, w_qk, far, near, (grad_value, w_value), h) / sums_in[0:1]
    row = lax.broadcasted_iota(jnp.int32, sums.shape, 0)
    sums[...] = reorder(jnp.where(row == 7, gained, sums_in[...]), mine, n_dp)
    sums[0:4] = jnp.zeros((4, sums.shape[1]), F32)
    local_width, head_size = sums_q.shape[1], slope.shape[1]
    b_value = jnp.sum(grad_value[...].astype(F32), axis=0, keepdims=True)
    share = jnp.concatenate([sums_q[1:2], b_value, b_hidden[...]], axis=0)
    for number in range(sums.shape[1] // local_width):

        @pl.when(place == number)
        def _():
            sums[0:3, number * local_width : (number + 1) * local_width] = share

    scale = sums_q[0:1]
    total = scale[:, :head_size]
    for number in range(1, local_width // head_size):
        total = total + scale[:, number * head_size : (number + 1) * head_size]
    sums[3:4, :head_size] = total * slope[...]
    if len(outs) > 1:
        outs[2][pl.ds(4 * depth, 48)] = fold(sums[...], outs[2].shape[1])


def fold(vectors, width):
    count = vectors.shape[1] // width
    rows = [vectors[:, k * width : (k + 1) * width] for k in range(count)]
    return jnp.concatenate(rows + [jnp.zeros((48 - 8 * count, width), F32)], axis=0).astype(BF16)


def unfold(rows, count):
    return jnp.concatenate([rows[8 * k : 8 * k + 8] for k in range(count)], axis=1)


def first_sum_kernel(s, pair_kept, pair_got, ring_kept, ring_got, *refs):
    *given, pair_out, pair_mid, ring_out, ring_mid = refs
    half = pair_mid.shape[0]
    value = pair_kept[...].astype(F32) + pair_got[...].astype(F32)
    pair_out[...] = value[:half].astype(BF16)
    pair_mid[...] = value[half:]
    value = ring_kept[...].astype(F32) + ring_got[pl.ds(0, 2 * half)].astype(F32)
    ring_out[pl.ds(0, half)] = value[:half].astype(BF16)
    ring_mid[...] = value[half:]
    if given:
        low = fold(given[0][...], ring_out.shape[1]).astype(F32) + ring_got[pl.ds(2 * half, 48)].astype(F32)
        ring_out[pl.ds(half, 48)] = low.astype(BF16)


def second_sum_kernel(s, pair_mid, pair_got, ring_mid, ring_got, *refs):
    half, depth, cut = pair_mid.shape[0], pair_mid.shape[0] // 2, pair_mid.shape[1]
    given, out, zero = refs[: len(refs) // 3], refs[len(refs) // 3], refs[len(refs) // 3 + 1]
    pair = pair_mid[...] + pair_got[...].astype(F32)
    ring = ring_mid[...] + ring_got[pl.ds(0, half)].astype(F32)
    out[:, :cut], out[:, cut:] = pair[:depth].astype(BF16), ring[:depth].astype(BF16)
    zero[:, :cut], zero[:, cut:] = pair[depth:], ring[depth:]
    if given:
        at, vectors = pl.ds(half, 48), refs[-1]
        total = given[0][at].astype(F32) + ring_got[at].astype(F32)
        vectors[...] = unfold(total, vectors.shape[1] // ring.shape[1])


def total_kernel(s, one, two, *outs):
    total = one[...] + two[...]
    for out, row in zip(outs[:7], (0, 1, 2, 6, 4, 5, 7)):
        for k in range(out.shape[0]):
            out[k : k + 1] = total[row : row + 1, k * LANES : (k + 1) * LANES]
    outs[7][...] = total[3:4, : outs[7].shape[1]]


def last_kernel(n_dp, s, keep, got, x_own, grad_full, sums_in, grad_in):
    normed, inverse = normalize(x_own[...].astype(F32))
    grad_h = keep[...] + got[...].astype(F32)
    full = grad_full[...] + norm_back(grad_h, normed, inverse, sums_in[0:1])
    grad_in[...] = reorder(full, s[0], n_dp).astype(BF16)


def add_kernel(s, one, two, out):
    out[...] = one[...] + two[...]


def output_kernel(n_dp, s, keep, got, x_one, vectors, out):
    value = x_one[...] + keep[...] + got[...].astype(F32) + vectors[3:4]
    out[...] = reorder(value, s[0], n_dp).astype(BF16)


def tie(*values):
    return lax.optimization_barrier(values)


class Links:
    def __init__(self, n_dp, n_tensor):
        self.n_dp, self.n_tensor = n_dp, n_tensor
        self.wide = n_dp > 8

    def move(self, value, target):
        pairs = []
        for d in range(self.n_dp):
            for t in range(self.n_tensor):
                to_d, to_t = target(d, t)
                pairs.append((d * self.n_tensor + t, to_d * self.n_tensor + to_t))
        return lax.ppermute(value, AXES, pairs)

    def chip(self, value):
        return self.move(value, lambda d, t: (d, t ^ 2))

    def core(self, value):
        return self.move(value, lambda d, t: (d, t ^ 1))

    def pair(self, value):
        return self.along(value, 1)

    def along(self, value, bits):
        return self.move(value, lambda d, t: (d ^ bits, t))

    def gather_tensor(self, rows):
        near = self.chip(rows)
        return rows, near, self.core(rows), self.core(near)

    def gather_wide(self, shard):
        blocks, place = lax.all_gather(shard, "dp", axis=0), lax.axis_index("dp")
        return jnp.take(blocks, lax.iota(jnp.int32, self.n_dp) ^ place, axis=0).reshape(-1, shard.shape[1])

    def scatter_wide(self, total):
        place = lax.axis_index("dp")
        blocks = total.reshape(self.n_dp, total.shape[0] // self.n_dp, total.shape[1])
        blocks = jnp.take(blocks, lax.iota(jnp.int32, self.n_dp) ^ place, axis=0).astype(F32)
        return unpack(lax.psum_scatter(blocks.reshape(total.shape), "dp", scatter_dimension=0, tiled=True))

    def steps(self):
        found, bit = [], 1
        while bit < self.n_dp and self.wide:
            found.append(lambda d, t, bit=bit: (d ^ bit, t))
            bit *= 2
        far = [] if self.wide else [lambda d, t: (d ^ 4, t)]
        return found + [lambda d, t: (d, t ^ 1), lambda d, t: (d, t ^ 2)] + far


def body(
    inputs,
    weight_query,
    weight_key,
    weight_value,
    weight_output,
    weight_hidden,
    weight_down,
    bias_query,
    bias_value,
    bias_hidden,
    bias_output,
    bias_final,
    gain_attention,
    gain_mixer,
    query_scale,
    lengths,
    cotangent,
    n_dp,
    n_tensor,
):
    links = Links(n_dp, n_tensor)
    wide = links.wide
    local_rows, width = inputs.shape
    all_rows = local_rows * n_tensor
    depth = width // n_dp
    local_width = weight_query.shape[1]
    both = 2 * local_width
    head_size = query_scale.shape[0]
    heads = local_width // head_size
    dp_index = lax.axis_index("dp")
    tensor_index = lax.axis_index("tensor")
    s = jnp.stack([dp_index, tensor_index, lengths[0]])
    product = 2 * all_rows * width * local_width
    mixed = 2 * all_rows * all_rows * local_width

    def run(name, kernel, outs, *arguments, **rest):
        return call(name, kernel, [shaped(*o) for o in outs], s, *arguments, **rest)

    def bind(kernel, *fixed):
        def bound(*refs):
            return kernel(*fixed, *refs)

        return bound

    packed = [((depth, both), BF16)]
    rows_low, rows_full = ((local_rows, width), BF16), ((local_rows, width), F32)
    split = [((all_rows // 2, width), BF16), ((all_rows // 2, width), F32)]
    part = ((all_rows, local_width), BF16)
    part_full = ((all_rows, local_width), F32)
    whole_rows = ((all_rows, width), BF16)
    weight = ((width, local_width), BF16)
    vector = ((8, width), F32)
    halves = [((width // 2, both), BF16)] * 2
    term = [pltpu.VMEM((width, both), BF16)]
    sems = [pltpu.SemaphoreType.DMA((n_dp,))]

    unit = SOFTPLUS_UNIT / jnp.sqrt(F32(head_size))
    scale_wide = jnp.tile(jax.nn.softplus(query_scale) * unit, heads)[None]
    slope = (jax.nn.sigmoid(query_scale) * unit)[None]
    def apart(value):
        return pltpu.with_memory_space_constraint(value, pltpu.HBM)

    weights = (weight_query, weight_key, weight_value, weight_output.T, weight_hidden, weight_down.T)
    own_qk, own_vo, own_hd = run(
        "pack",
        pack_kernel,
        packed * 3,
        *(apart(w) for w in weights),
        remote=6,
        scratch=[pltpu.VMEM((depth, local_width), BF16)] * 6 + [pltpu.SemaphoreType.DMA((6,))],
    )
    given = (gain_attention, gain_mixer, bias_output, bias_final, bias_query, bias_value, bias_hidden)
    scale_wide, slope = tie(scale_wide, slope)
    tall = (width // LANES, LANES)
    h_own, x_own, grad_own, vectors, biases = run(
        "prepare",
        bind(prepare_kernel, n_dp),
        [rows_low, rows_low, rows_low, vector, ((8, local_width), F32)],
        scale_wide,
        *(apart(v) for v in (inputs, cotangent, *(v.reshape(tall) for v in given))),
        remote=9,
        scratch=[pltpu.VMEM((local_rows, width), BF16)] * 2
        + [pltpu.VMEM(tall, F32)] * 7
        + [pltpu.SemaphoreType.DMA((9,))],
    )

    def stack(*blocks):
        rows = sum(block.shape[0] for block in blocks)
        return run("stack", stack_kernel, [((rows, both), BF16)], *blocks)[0]

    if wide:
        qk, vo, hd = (([links.gather_wide(own)], []) for own in (own_qk, own_vo, own_hd))
        h_one, grad_rows = links.gather_tensor(h_own), links.gather_tensor(grad_own)
    else:
        qk_one, qk_two = links.along(own_qk, 2), links.along(own_qk, 4)
        hd_pair = links.pair(own_hd)
        h_own, own_vo, own_hd, qk_one, qk_two, hd_pair = tie(h_own, own_vo, own_hd, qk_one, qk_two, hd_pair)
        h_chip = links.chip(h_own)
        qk_three = links.along(qk_two, 2)
        near_qk_pair = links.pair(stack(own_qk, qk_one))
        vo_two, vo_pair = links.along(own_vo, 4), links.pair(own_vo)
        far_stack = stack(qk_two, qk_three)
        far_stack, near_qk_pair = tie(far_stack, near_qk_pair)
        h_chip, vo_two, vo_pair, own_vo = tie(h_chip, vo_two, vo_pair, own_vo)
        h_one = h_own, h_chip, links.core(h_own), links.core(h_chip)
        far_qk_pair = links.pair(far_stack)
        vo_one, vo_three = links.along(own_vo, 2), links.along(vo_two, 2)
        qk = [own_qk, qk_one, qk_two, qk_three], [near_qk_pair, far_qk_pair]
        h_one, qk, vo_three, own_hd = tie(h_one, qk, vo_three, own_hd)
        near_vo_pair = links.pair(vo_one)
        hd_one, hd_two = links.along(own_hd, 2), links.along(own_hd, 4)
        grad_chip = links.chip(grad_own)
    n_qk = len(qk[0]), len(qk[0]) + len(qk[1])
    q_raw, q_low, k_low, h_all, w_qk, turned = run(
        "attend",
        bind(attend_kernel, n_qk, depth, head_size),
        [
            part_full,
            part,
            part,
            whole_rows,
            ((width, both), BF16),
            ((heads, all_rows, all_rows), BF16),
        ],
        *h_one,
        biases,
        *qk[0],
        *qk[1],
        remote=n_qk[1],
        scratch=sems,
    )
    if not wide:
        turned, near_vo_pair, hd_one, hd_two, grad_chip = tie(turned, near_vo_pair, hd_one, hd_two, grad_chip)
        far_vo_pair = links.pair(stack(vo_two, vo_three))
        hd_three = links.along(hd_two, 2)
        grad_rows = grad_own, grad_chip, links.core(grad_own), links.core(grad_chip)
        vo = [own_vo, vo_one, vo_two, vo_three], [vo_pair, near_vo_pair, far_vo_pair]
        turned, vo, grad_rows = tie(turned, vo, grad_rows)
        near_hd_pair = links.pair(hd_one)
    n_vo = len(vo[0]), len(vo[0]) + len(vo[1])
    v_low, context, far, near, w_value, w_output = run(
        "context",
        bind(context_kernel, n_vo, depth, head_size),
        [part, part, *split, weight, weight],
        h_all,
        turned,
        biases,
        *vo[0],
        *vo[1],
        remote=n_vo[1],
        scratch=term + sems,
    )

    def core_half(far, near, *extra):
        got, *extra = tie(links.core(far), *extra)
        return list(run("middle", middle_kernel, [rows_low, rows_full], near, got)) + list(extra)

    if wide:
        send, keep = core_half(far, near)
        got = links.chip(send)
    else:
        far, near_hd_pair, hd_three = tie(far, near_hd_pair, hd_three)
        send, keep = core_half(far, near)
        got = links.chip(send)
        far_hd_pair = links.pair(stack(hd_two, hd_three))
        hd = [own_hd, hd_one, hd_two, hd_three], [hd_pair, near_hd_pair, far_hd_pair]
        got, hd = tie(got, hd)
    n_hd = len(hd[0]), len(hd[0]) + len(hd[1])
    x_one, h_two_own = run("second_norm", second_norm_kernel, [rows_full, rows_low], keep, got, x_own, vectors)
    h_two_chip = links.chip(h_two_own)
    grad_act, grad_all, w_hidden, w_down = run(
        "grad_act",
        bind(grad_act_kernel, n_hd, depth),
        [part_full, whole_rows, weight, weight],
        *grad_rows,
        *hd[0],
        *hd[1],
        remote=n_hd[1],
        scratch=term + sems,
    )
    h_two_chip, grad_act = tie(h_two_chip, grad_act)
    h_two = h_two_own, h_two_chip, links.core(h_two_own), links.core(h_two_chip)
    far, near, act, grad_pre, h_two_all = run(
        "hidden",
        hidden_kernel,
        [*split, part, part, whole_rows],
        *h_two,
        w_hidden,
        biases,
        grad_act,
    )
    cut = 3 * both // 5
    tall_sent = n_dp // 2 * depth
    terms = [((width, both), BF16)]
    if not wide:
        terms = [((tall_sent, c), BF16) for c in (cut, cut, both - cut, both - cut)]
    grad_b_hidden, *terms_hd = run(
        "down",
        bind(down_kernel, depth),
        [((1, local_width), F32), *terms],
        h_two_all,
        grad_all,
        act,
        grad_pre,
    )
    send, keep, terms_hd = core_half(far, near, terms_hd)
    got = links.chip(send)
    act, keep = tie(act, keep)
    mix_far, mix_near = run("mixer", mixer_kernel, split, act, w_down)
    got, mix_far = tie(got, mix_far)

    def first_send(terms):
        return [links.pair(terms[0]), links.along(terms[2], 2)]

    def first_sum(name, terms, got, given=()):
        rows = tall_sent // 2
        extra, rest = 48 if given else 0, both - cut
        outs = [((rows, cut), BF16), ((rows, cut), F32), ((rows + extra, rest), BF16), ((rows, rest), F32)]
        return run("first_" + name, first_sum_kernel, outs, terms[1], got[0], terms[3], got[1], *given)

    def second_send(sums):
        return [links.along(sums[0], 2), links.pair(sums[2])]

    def second_sum(name, sums, got, given=False):
        outs = packed + [((depth, both), F32)] + ([vector] if given else [])
        more = sums[2:3] if given else []
        return run("second_" + name, second_sum_kernel, outs, sums[1], got[0], sums[3], got[1], *more)

    def owned(name, *parts):
        outs = [((depth, local_width), F32)] * 2
        return run("owned_" + name, bind(owned_kernel, len(parts) - 1), outs, *parts)

    if not wide:
        got_hd = first_send(terms_hd)
        got, got_hd = tie(got, got_hd)
    grad_mid_low, grad_mid, sums = run(
        "grad_middle",
        grad_middle_kernel,
        [rows_low, rows_full, vector],
        keep,
        got,
        x_one,
        grad_own,
        vectors,
    )
    if wide:
        grad_mid_rows = links.gather_tensor(grad_mid_low)
    else:
        grad_mid_chip = links.chip(grad_mid_low)
        sums_hd = first_sum("hd", terms_hd, got_hd)
        got_hd = second_send(sums_hd)
        grad_mid_chip, got_hd = tie(grad_mid_chip, got_hd)
        sent_hd, zero_hd = second_sum("hd", sums_hd, got_hd)
        grad_mid_rows = grad_mid_low, grad_mid_chip, links.core(grad_mid_low), links.core(grad_mid_chip)
    if wide:
        grad_mid_rows, mix_far = tie(grad_mid_rows, mix_far)
    else:
        grad_mid_rows, mix_far, sent_hd = tie(grad_mid_rows, mix_far, sent_hd)
    mix_send, mix_keep = core_half(mix_far, mix_near)
    mix_got = links.chip(mix_send)
    grad_context, grad_value, _, *terms_vo = run(
        "grad_context",
        bind(grad_context_kernel, depth, head_size),
        [part, part, whole_rows, *terms],
        *grad_mid_rows,
        w_output,
        turned,
        context,
        h_all,
    )
    if not wide:
        got_vo = first_send(terms_vo)
        grad_context, sent_hd = tie(grad_context, sent_hd)
        part_hd = links.along(sent_hd, 4)
    grad_qk, sums_q = run(
        "grad_scores",
        bind(grad_scores_kernel, head_size),
        [((all_rows, both), BF16), ((8, local_width), F32)],
        turned,
        grad_context,
        v_low,
        q_low,
        k_low,
        q_raw,
        biases,
        scratch=[pltpu.VMEM((all_rows, all_rows), BF16)],
    )
    if wide:
        grad_qk, mix_got = tie(grad_qk, mix_got)
    else:
        grad_qk, mix_got, got_vo = tie(grad_qk, mix_got, got_vo)
    terms_first = list(terms)
    if not wide:
        terms_first[2] = ((tall_sent + 48, both - cut), BF16)
    far, near, sums, *terms_qk = run(
        "grad_first",
        bind(grad_first_kernel, n_dp, depth),
        [*split, vector, *terms_first],
        grad_qk,
        w_qk,
        grad_value,
        w_value,
        h_all,
        sums,
        sums_q,
        grad_b_hidden,
        slope,
    )
    def exchange(value, step):
        return run("add", add_kernel, [vector], value, links.move(value, step))[0]

    total = sums
    if wide:
        send, keep = core_half(far, near)
        got = links.chip(send)
    else:
        got_qk = first_send(terms_qk)
        far, part_hd, *got_vo = tie(far, part_hd, *got_vo)
        sums_vo = first_sum("vo", terms_vo, got_vo)
        send, keep, *sums_vo = core_half(far, near, *sums_vo)
        got_vo = second_send(sums_vo)
        got = links.chip(send)
        (output,) = run("output", bind(output_kernel, n_dp), [rows_low], mix_keep, mix_got, x_one, vectors)
        grad_hidden, grad_down = owned("hd", zero_hd, part_hd)
        got_qk, got, output, grad_hidden = tie(got_qk, got, output, grad_hidden)
        got_qk, got_vo = tie(got_qk, got_vo)
        sums_qk = first_sum("qk", terms_qk, got_qk, [sums])
        got_qk = second_send(sums_qk)
        (grad_in,) = run("last", bind(last_kernel, n_dp), [rows_low], keep, got, x_own, grad_mid, vectors)
        got_qk, grad_in = tie(got_qk, grad_in)
        sent_vo, zero_vo = second_sum("vo", sums_vo, got_vo)
        part_vo = links.along(sent_vo, 4)
        sent_qk, zero_qk, total = second_sum("qk", sums_qk, got_qk, True)
        far_qk = links.along(sent_qk, 4)
        zero_vo, total = tie(zero_vo, total)
    if wide:
        (grad_in,) = run("last", bind(last_kernel, n_dp), [rows_low], keep, got, x_own, grad_mid, vectors)
    if wide:
        (output,) = run("output", bind(output_kernel, n_dp), [rows_low], mix_keep, mix_got, x_one, vectors)
    steps = links.steps()
    for step in steps[:-1]:
        total = exchange(total, step)
    moved = links.move(total, steps[-1])
    if not wide:
        grad_query, grad_key = owned("qk", zero_qk, far_qk)
        moved, grad_query = tie(moved, grad_query)
    tall_vector = (tall, F32)
    *totals, total_scale = run(
        "total", total_kernel, [tall_vector] * 7 + [((1, head_size), F32)], total, moved
    )
    totals = [v.reshape(width) for v in totals]
    if wide:
        grad_hidden, grad_down = links.scatter_wide(terms_hd[0])
        grad_output_v, grad_output_o = links.scatter_wide(terms_vo[0])
        grad_query, grad_key = links.scatter_wide(terms_qk[0])
    else:
        grad_output_v, grad_output_o = owned("vo", zero_vo, part_vo)
    return (
        output,
        grad_in,
        grad_query,
        grad_key,
        grad_output_v,
        grad_output_o.T,
        grad_hidden,
        grad_down.T,
        totals[0],
        totals[1],
        totals[2],
        totals[5],
        totals[4],
        totals[6],
        totals[3],
        total_scale.reshape(head_size),
    )


def solution(mesh):
    n_dp, n_tensor = mesh.shape["dp"], mesh.shape["tensor"]

    def local(*arguments):
        return body(*arguments, n_dp, n_tensor)

    rows = P(("dp", "tensor"), None)
    into, out_of = P("dp", "tensor"), P("tensor", "dp")
    return jax.shard_map(
        local,
        mesh=mesh,
        in_specs=(rows, into, into, into, out_of, into, out_of, *[P()] * 8, P("dp"), rows),
        out_specs=(rows, rows, into, into, into, out_of, into, out_of, *[P()] * 8),
        check_vma=False,
    )
```
